256 devices in a mesh: ha: 16 (over z, core), wa: 4 (over y), col: 4 (over x).
Axes of the slice: x: 4, y: 4, z: 8, core: 2. Of those that a mesh axis runs over, the one named last changes fastest.
Arguments:
- features: bfloat16 [4, 128, 128, 512], P(None, 'ha', 'wa', 'col'), may hold values from -64 to 64
- cache_first: bfloat16 [2, 128, 128, 512], P(None, 'ha', 'wa', 'col'), may hold values from -6 to 6
- cache_second: bfloat16 [2, 128, 128, 512], P(None, 'ha', 'wa', 'col'), may hold values from -6 to 6
- weight_first: bfloat16 [27, 512, 512], P(None, 'col'), may hold values from -0.0546875 to 0.0546875
- weight_second: bfloat16 [27, 512, 512], P(None, 'col'), may hold values from -0.0546875 to 0.0546875
- weight_up: bfloat16 [9, 512, 512], P(None, 'col'), may hold values from -0.09375 to 0.09375
Outputs:
- upsampled: bfloat16 [4, 256, 256, 512], P(None, 'ha', 'wa', 'col')
The draws below stay inside these ranges and needn't reach their ends.
All inputs are finite; a program needn't handle non-finite values.
Results may differ from the reference program's by a relative error of at most 0.01.
Values may be sent and summed in bfloat16 or wider, within the bound.
No kernel may reach another device: no remote copies, remote signals or barrier semaphores. Data moves between devices by JAX's collectives and lax.ppermute only.
A program may use at most 192 MiB of HBM per device.

```python
import math
import jax
import jax.numpy as jnp
from jax import lax

C = 512
G = 32
FRAMES = 4
CACHE = 2
HEIGHT = 128
WIDTH = 128


def draw_features(key, part):
    keys = jax.random.split(key, 5)
    row_place = jnp.arange(HEIGHT, dtype=jnp.float32) / HEIGHT
    col_place = jnp.arange(WIDTH, dtype=jnp.float32) / WIDTH
    ramp_base = 3.0
    shift_scale = 1.5
    height_profile = 0.3 * 10.0 ** row_place
    noise = jax.random.truncated_normal(keys[0], -4.0, 4.0, (FRAMES, HEIGHT, WIDTH, C), jnp.float32)
    channel_scale = jnp.exp(jax.random.uniform(keys[1], (C,), jnp.float32, math.log(0.3), math.log(3.0)))
    roughness = jax.random.uniform(keys[2], (HEIGHT, WIDTH), jnp.float32, 0.5, 1.5)
    ramp = ramp_base ** (row_place[:, None] + col_place[None, :]) / ramp_base
    group_shift = jax.random.uniform(keys[3], (G,), jnp.float32, -1.0, 1.0)
    jitter = jax.random.uniform(keys[4], (C,), jnp.float32, -0.2, 0.2)
    shift = (jnp.repeat(group_shift, C // G) + jitter) * shift_scale
    scaled = noise * channel_scale * (roughness * ramp)[None, :, :, None] + shift[None, None, None, :] * height_profile[None, :, None, None]
    return scaled.astype(jnp.bfloat16)


def shard_levels(stream_key, extent, cuts, low, top_value):
    def one(position, blocks):
        draws = jax.random.uniform(jax.random.fold_in(jax.random.fold_in(stream_key, 6), position), (blocks,), jnp.float32, low / len(cuts), top_value / len(cuts))
        return jnp.repeat(jnp.exp(draws), extent[position] // blocks).reshape((-1,) + (1,) * (len(extent) - position - 1))

    gain = one(*cuts[0])
    for cut in cuts[1:]:
        gain = gain * one(*cut)
    return gain


def centred(stream_key, dims, scale, most, cuts=(), kind=jnp.bfloat16):
    result = jax.random.normal(stream_key, dims, jnp.float32) * scale
    if len(cuts) > 0:
        result = shard_levels(stream_key, dims, cuts, -0.22, 0.18) * result
    return jnp.clip(result, min=-most, max=most).astype(kind)


def setup_inputs(seed: int = 0) -> dict:
    seeds = jax.random.split(jax.random.key(seed), 7)
    features = draw_features(jax.random.fold_in(seeds[6], 71), 0)
    cache_first = centred(seeds[1], (CACHE, HEIGHT, WIDTH, C), 1.0, 6.0, ((1, 16), (2, 4), (3, 4)))
    cache_second = centred(seeds[2], (CACHE, HEIGHT, WIDTH, C), 1.0, 6.0, ((1, 16), (2, 4), (3, 4)))
    weight_first = centred(seeds[3], (27, C, C), (27 * C) ** -0.5, 0.0546875, ((1, 4),))
    weight_second = centred(seeds[4], (27, C, C), (27 * C) ** -0.5, 0.0546875, ((1, 4),))
    weight_up = centred(seeds[5], (9, C, C), (9 * C) ** -0.5, 0.09375, ((1, 4),))
    return dict(features=features, cache_first=cache_first, cache_second=cache_second, weight_first=weight_first, weight_second=weight_second, weight_up=weight_up)


def norm_act(values):
    group_size = C // G
    shaped = values.astype(jnp.float32).reshape(values.shape[:3] + (G, group_size))
    center = lax.optimization_barrier(jnp.mean(shaped, axis=(0, 1, 2, 4), keepdims=True))
    deviation = shaped - center
    spread = lax.optimization_barrier(jnp.mean(deviation * deviation, axis=(0, 1, 2, 4), keepdims=True))
    normed = deviation * jax.lax.rsqrt(spread + 1e-06)
    return jax.nn.silu(normed).reshape(values.shape).astype(jnp.bfloat16)

def conv_frames(stack, weight, frame_taps, upsample):
    if upsample:
        stack = jnp.repeat(jnp.repeat(stack, 2, axis=1), 2, axis=2)
    rows_all = stack.shape[1]
    cols_all = stack.shape[2]
    padded = jnp.pad(stack, ((0, 0), (1, 1), (1, 1), (0, 0)))
    flat = weight.reshape(-1, weight.shape[2])
    outputs = []
    for frame in range(stack.shape[0] - frame_taps + 1):
        pieces = []
        for step_t in range(frame_taps):
            for row_off in range(3):
                for col_off in range(3):
                    pieces.append(padded[frame + step_t, row_off:row_off + rows_all, col_off:col_off + cols_all, :])
        patches = jnp.concatenate(pieces, axis=-1).reshape(rows_all * cols_all, -1)
        outputs.append(jnp.dot(patches, flat, preferred_element_type=jnp.float32).reshape(rows_all, cols_all, -1))
    return jnp.stack(outputs)

def reference(features, cache_first, cache_second, weight_first, weight_second, weight_up):
    act_first = norm_act(features)
    hidden = conv_frames(jnp.concatenate([cache_first, act_first], axis=0), weight_first, 3, False).astype(jnp.bfloat16)
    act_second = norm_act(hidden)
    branch = conv_frames(jnp.concatenate([cache_second, act_second], axis=0), weight_second, 3, False)
    resid = (features.astype(jnp.float32) + branch).astype(jnp.bfloat16)
    return conv_frames(resid, weight_up, 1, True).astype(jnp.bfloat16)
```

```python
import functools

import jax
import jax.numpy as jnp
from jax import lax
from jax.experimental import pallas as pl
from jax.experimental.pallas import tpu as pltpu
from jax.sharding import PartitionSpec as P

F32 = jnp.float32
BF16 = jnp.bfloat16
CH = 128
GROUP = 16
ROWS = 8
COLS = 32
MIB = 1 << 20

VMEM = pl.BlockSpec(memory_space=pltpu.VMEM)
SMEM = pl.BlockSpec(memory_space=pltpu.SMEM)


def call(body, outs, scratch=(), flops=0, limit=24, name=None):
    def run(*args):
        nbytes = sum(a.size * a.dtype.itemsize for a in list(args) + list(outs))
        return pl.pallas_call(
            body,
            out_shape=list(outs),
            in_specs=[SMEM if a.dtype == jnp.int32 else VMEM for a in args],
            out_specs=[VMEM] * len(outs),
            scratch_shapes=list(scratch),
            compiler_params=pltpu.CompilerParams(vmem_limit_bytes=limit * MIB),
            cost_estimate=pl.CostEstimate(flops=flops, bytes_accessed=nbytes, transcendentals=0),
            name=name,
        )(*args)

    return run


def sds(shape, dtype=BF16):
    return jax.ShapeDtypeStruct(shape, dtype)


def group_sum(row):
    lane = lax.broadcasted_iota(jnp.int32, row.shape, 1)
    shift = 1
    while shift < GROUP:
        other = jnp.where((lane & shift) != 0, pltpu.roll(row, shift, 1), pltpu.roll(row, CH - shift, 1))
        row = row + other
        shift *= 2
    return row


def local_stats(flat):
    count = flat.shape[0] * GROUP
    mean = group_sum(jnp.sum(flat, axis=0, keepdims=True)) * (1.0 / count)
    dev = flat - mean
    m2 = group_sum(jnp.sum(dev * dev, axis=0, keepdims=True))
    return mean, m2


def combine(st_ref, count):
    devices = st_ref.shape[0]
    means = st_ref[:, 0, :]
    mean = jnp.sum(means, axis=0, keepdims=True) * (1.0 / devices)
    apart = means - mean
    m2 = jnp.sum(st_ref[:, 1, :] + count * (apart * apart), axis=0, keepdims=True)
    return mean, lax.rsqrt(m2 * (1.0 / (count * devices)) + 1e-6)


def spread_stats(stats):
    devices = lax.axis_size("ha") * lax.axis_size("wa")
    slots = jnp.broadcast_to(stats[None], (devices,) + stats.shape)
    return lax.all_to_all(slots, ("ha", "wa"), 0, 0, tiled=True)


def store_edges(ref_slices, top_ref, bot_ref, lef_ref, rig_ref):
    at = 0
    for ref in ref_slices:
        n = ref.shape[0]
        top_ref[at : at + n] = ref[:, 0]
        bot_ref[at : at + n] = ref[:, ROWS - 1]
        v = ref[...].astype(F32)
        pad = jnp.zeros((n, 8, CH), F32)
        lef_ref[at : at + n] = jnp.concatenate([v[:, :, 0, :], pad], axis=1).astype(BF16)
        rig_ref[at : at + n] = jnp.concatenate([v[:, :, COLS - 1, :], pad], axis=1).astype(BF16)
        at += n


def first_body(x_ref, c1_ref, c2_ref, st_ref, top_ref, bot_ref, lef_ref, rig_ref):
    mean, m2 = local_stats(x_ref[...].astype(F32).reshape(-1, CH))
    st_ref[0:1, :] = mean
    st_ref[1:2, :] = m2
    store_edges([c1_ref, x_ref, c2_ref], top_ref, bot_ref, lef_ref, rig_ref)


def corner_body(top_ref, bot_ref, lef_ref, rig_ref, lo_ref, ro_ref):
    row = lax.broadcasted_iota(jnp.int32, lef_ref.shape, 1)
    top = top_ref[...].astype(F32)
    bot = bot_ref[...].astype(F32)
    for src, dst, at in ((lef_ref, lo_ref, 0), (rig_ref, ro_ref, COLS - 1)):
        v = src[...].astype(F32)
        v = jnp.where(row == 8, top[:, at : at + 1, :], v)
        v = jnp.where(row == 9, bot[:, at : at + 1, :], v)
        dst[...] = v.astype(BF16)


def swap_borders(top, bot, lef, rig):
    nh, nw = lax.axis_size("ha"), lax.axis_size("wa")
    above = lax.ppermute(bot, "ha", [(i, i + 1) for i in range(nh - 1)])
    below = lax.ppermute(top, "ha", [(i + 1, i) for i in range(nh - 1)])
    n = top.shape[0]
    lo, ro = call(corner_body, [sds((n, 16, CH))] * 2, name="corners")(above, below, lef, rig)
    left = lax.ppermute(ro, "wa", [(i, i + 1) for i in range(nw - 1)])
    right = lax.ppermute(lo, "wa", [(i + 1, i) for i in range(nw - 1)])
    return above, below, left, right


def shifted(rows, left, right):
    n = rows.shape[0]
    flat = rows.reshape(n * COLS, CH)
    col = lax.broadcasted_iota(jnp.int32, rows.shape, 1)
    before = pltpu.roll(flat, 1, 0).reshape(rows.shape)
    after = pltpu.roll(flat, n * COLS - 1, 0).reshape(rows.shape)
    before = jnp.where(col == 0, left[:, None, :], before)
    after = jnp.where(col == COLS - 1, right[:, None, :], after)
    return before, after


def place(patch_ref, frame, rows, at, left, right, lanes):
    n = rows.shape[0]
    before, after = shifted(rows, left, right)
    for e, v in enumerate((before, rows, after)):
        patch_ref[frame, at * COLS : (at + n) * COLS, lanes[e] : lanes[e] + CH] = v.reshape(n * COLS, CH).astype(BF16)


def place_frame(patch_ref, frame, inner, top, bot, lef, rig, lanes):
    place(patch_ref, frame, inner, 1, lef[0:8], rig[0:8], lanes)
    place(patch_ref, frame, top[None], 0, lef[8:9], rig[8:9], lanes)
    place(patch_ref, frame, bot[None], ROWS + 1, lef[9:10], rig[9:10], lanes)


def conv_body(cache_at, act_at, flag_ref, st_ref, x_ref, c_ref, tc, bc, lc, rc, ta, ba, la, ra, w_ref, *rest):
    outs, patch_ref = rest[:4], rest[4]
    has = [flag_ref[i] > 0 for i in range(4)]
    col = flag_ref[4]
    mean, scale = combine(st_ref, x_ref.shape[0] * ROWS * COLS * GROUP)

    def act(v):
        u = (v - mean) * scale
        return u / (1.0 + jnp.exp(-u))

    lanes = (0, CH, 2 * CH)
    for s in range(2):
        place_frame(
            patch_ref,
            s,
            c_ref[s].astype(F32),
            tc[cache_at + s].astype(F32),
            bc[cache_at + s].astype(F32),
            lc[cache_at + s].astype(F32),
            rc[cache_at + s].astype(F32),
            lanes,
        )
    row = lax.broadcasted_iota(jnp.int32, (16, CH), 0)
    edge = jnp.where(row == 8, flag_ref[0], jnp.where(row == 9, flag_ref[1], 1))
    for s in range(4):
        side = []
        for ref, flag in ((la, flag_ref[2]), (ra, flag_ref[3])):
            side.append(jnp.where(edge * flag > 0, act(ref[act_at + s].astype(F32)), 0.0))
        place_frame(
            patch_ref,
            2 + s,
            act(x_ref[s].astype(F32)),
            jnp.where(has[0], act(ta[act_at + s].astype(F32)), 0.0),
            jnp.where(has[1], act(ba[act_at + s].astype(F32)), 0.0),
            side[0],
            side[1],
            lanes,
        )
    depth = 9 * CH
    size = ROWS * COLS
    for t in range(4):
        acc = None
        for a in range(3):
            lhs = jnp.concatenate([patch_ref[t + a, b * COLS : b * COLS + size, :] for b in range(3)], axis=1)
            part = jnp.dot(lhs, w_ref[a * depth : (a + 1) * depth, :], preferred_element_type=F32)
            acc = part if acc is None else acc + part
        for j in range(4):
            piece = acc[:, j * CH : (j + 1) * CH].astype(BF16)
            slot = (j - col) & 3
            for k in range(4):

                @pl.when(slot == k)
                def _():
                    outs[k][t * size : (t + 1) * size, :] = piece


def conv(flags, stats, x, cache, cache_halo, cache_at, act_halo, act_at, weight, name):
    n = x.shape[0] * ROWS * COLS
    body = functools.partial(conv_body, cache_at, act_at)
    run = call(
        body,
        [sds((n, CH))] * 4,
        scratch=[pltpu.VMEM((6, (ROWS + 2) * COLS, 3 * CH), BF16)],
        flops=2 * n * weight.shape[0] * weight.shape[1],
        limit=32,
        name=name,
    )
    return run(flags, stats, x, cache, *cache_halo, *act_halo, weight)


def to_peers(pieces):
    n = lax.axis_size("col")
    return [lax.ppermute(pieces[k - 1], "col", [(i, (i + k) % n) for i in range(n)]) for k in range(1, n)]


def hidden_body(p0, p1, p2, p3, h_ref, st_ref, top_ref, bot_ref, lef_ref, rig_ref):
    total = p0[...].astype(F32) + p1[...].astype(F32) + p2[...].astype(F32) + p3[...].astype(F32)
    h = total.astype(BF16)
    h_ref[...] = h.reshape(h_ref.shape)
    mean, m2 = local_stats(h.astype(F32))
    st_ref[0:1, :] = mean
    st_ref[1:2, :] = m2
    store_edges([h_ref], top_ref, bot_ref, lef_ref, rig_ref)


def resid_body(x_ref, p0, p1, p2, p3, h_ref, top_ref, bot_ref, lef_ref, rig_ref):
    total = p0[...].astype(F32) + p1[...].astype(F32) + p2[...].astype(F32) + p3[...].astype(F32)
    h_ref[...] = (x_ref[...].astype(F32) + total.reshape(x_ref.shape)).astype(BF16)
    store_edges([h_ref], top_ref, bot_ref, lef_ref, rig_ref)


ROW_TAPS = {(0, 0): (-1, 0), (0, 1): (1,), (1, 0): (-1,), (1, 1): (0, 1)}
COL_TAPS = {(0, 0): (-1,), (0, 1): (0, 1), (1, 0): (-1, 0), (1, 1): (1,)}


def split_body(col_ref, *refs):
    for src, dst in zip(refs[:4], refs[4:]):
        dst[...] = src[...]


def split_weight(weight, col):
    taps = weight.shape[0]
    specs = [
        pl.BlockSpec((taps, CH, CH), lambda i, s, k=k: (0, 0, lax.rem(s[0] + k, 4))) for k in range(4)
    ]
    whole = pl.BlockSpec((taps, CH, CH), lambda i, s: (0, 0, 0))
    return pl.pallas_call(
        split_body,
        out_shape=[sds((taps, CH, CH))] * 4,
        grid_spec=pltpu.PrefetchScalarGridSpec(
            num_scalar_prefetch=1, grid=(1,), in_specs=specs, out_specs=[whole] * 4
        ),
        name="split_weight",
    )(col.reshape(1), *([weight] * 4))


def fold_body(w0, w1, w2, w3, o_ref):
    for k, ref in enumerate((w0, w1, w2, w3)):
        taps = [ref[i].astype(F32) for i in range(9)]
        for q in range(2):
            for r in range(2):
                for s in range(2):
                    for p in range(2):
                        total = None
                        for b in ROW_TAPS[p, r]:
                            for e in COL_TAPS[q, s]:
                                tap = taps[(b + 1) * 3 + (e + 1)]
                                total = tap if total is None else total + tap
                        at = (s * 4 + k) * CH
                        o_ref[q, r, at : at + CH, p * CH : (p + 1) * CH] = total.astype(BF16)


def up_body(*refs):
    parts = [refs[5 * k : 5 * k + 5] for k in range(4)]
    w_ref, o_ref, patch_ref, mix_ref = refs[20:24]
    size = (ROWS + 1) * COLS
    half = 2 * 4 * CH
    for k, (x, top, bot, lef, rig) in enumerate(parts):
        place_frame(
            patch_ref,
            0,
            x[0].astype(F32),
            top[0].astype(F32),
            bot[0].astype(F32),
            lef[0].astype(F32),
            rig[0].astype(F32),
            [(e * 4 + k) * CH for e in range(3)],
        )
    for q in range(2):
        acc = None
        for r in range(2):
            lhs = patch_ref[0, r * COLS : r * COLS + size, q * 4 * CH : q * 4 * CH + half]
            part = jnp.dot(lhs, w_ref[q, r], preferred_element_type=F32)
            acc = part if acc is None else acc + part
        for n in range(ROWS + 1):
            for p in range(2):
                i = 2 * n - 1 + p
                if 0 <= i < 2 * ROWS:
                    mix_ref[i, pl.ds(q, COLS, stride=2), :] = acc[n * COLS : (n + 1) * COLS, p * CH : (p + 1) * CH]
    o_ref[0] = mix_ref[...].astype(BF16)


def up_conv(parts, weight):
    specs = []
    args = []
    for part in parts:
        for a in part:
            rest = a.shape[1:]
            specs.append(pl.BlockSpec((1,) + rest, lambda t, n=len(rest): (t,) + (0,) * n))
            args.append(a)
    specs.append(pl.BlockSpec(weight.shape, lambda t: (0, 0, 0, 0)))
    frames = parts[0][0].shape[0]
    out = (frames, 2 * ROWS, 2 * COLS, CH)
    return pl.pallas_call(
        up_body,
        out_shape=sds(out),
        grid=(frames,),
        in_specs=specs,
        out_specs=pl.BlockSpec((1,) + out[1:], lambda t: (t, 0, 0, 0)),
        scratch_shapes=[
            pltpu.VMEM((1, (ROWS + 2) * COLS, 12 * CH), BF16),
            pltpu.VMEM((2 * ROWS, 2 * COLS, CH), F32),
        ],
        compiler_params=pltpu.CompilerParams(vmem_limit_bytes=24 * MIB),
        name="up_conv",
    )(*args, weight)


def on_device(features, cache_first, cache_second, weight_first, weight_second, weight_up):
    frames = features.shape[0]
    n = frames * ROWS * COLS
    ha, wa, col = lax.axis_index("ha"), lax.axis_index("wa"), lax.axis_index("col")
    nh, nw = lax.axis_size("ha"), lax.axis_size("wa")
    flags = jnp.stack([ha > 0, ha < nh - 1, wa > 0, wa < nw - 1, col]).astype(jnp.int32)

    stats, *edges = call(
        first_body, [sds((2, CH), F32)] + [sds((8, COLS, CH))] * 2 + [sds((8, 16, CH))] * 2, name="first"
    )(features, cache_first, cache_second)
    w_pieces = split_weight(weight_up, col)
    w_got = to_peers(w_pieces[1:])
    halo = swap_borders(*edges)
    stats = spread_stats(stats)
    pieces = conv(
        flags, stats, features, cache_first, halo, 0, halo, 2, weight_first.reshape(-1, 4 * CH), "conv_first"
    )
    got = to_peers(pieces[1:])
    hidden, stats, *edges = call(
        hidden_body,
        [sds(features.shape), sds((2, CH), F32)] + [sds((frames, COLS, CH))] * 2 + [sds((frames, 16, CH))] * 2,
        name="hidden",
    )(pieces[0], *got)
    halo2 = swap_borders(*edges)
    stats = spread_stats(stats)
    (folded,) = call(fold_body, [sds((2, 2, 8 * CH, 2 * CH))], name="fold")(w_pieces[0], *w_got)
    pieces = conv(
        flags, stats, hidden, cache_second, halo, 6, halo2, 0, weight_second.reshape(-1, 4 * CH), "conv_second"
    )
    got = to_peers(pieces[1:])
    resid, *edges = call(
        resid_body,
        [sds(features.shape)] + [sds((frames, COLS, CH))] * 2 + [sds((frames, 16, CH))] * 2,
        name="resid",
    )(features, pieces[0], *got)
    others = to_peers([resid] * 3)
    above, below, left, right = swap_borders(*edges)
    border = jnp.concatenate([above, below, left, right], axis=1)
    borders = to_peers([border] * 3)
    parts = [(resid, above, below, left, right)]
    for x, b in zip(others, borders):
        parts.append(
            (x, b[:, :COLS], b[:, COLS : 2 * COLS], b[:, 2 * COLS : 2 * COLS + 16], b[:, 2 * COLS + 16 :])
        )
    parts = [(x, t.reshape(frames, COLS, CH), b, le, ri) for x, t, b, le, ri in parts]
    return up_conv(parts, folded)


def solution(mesh):
    placed = (
        P(None, "ha", "wa", "col"),
        P(None, "ha", "wa", "col"),
        P(None, "ha", "wa", "col"),
        P(None, "col", None),
        P(None, "col", None),
        P(None, "col", None),
    )
    return jax.shard_map(
        on_device, mesh=mesh, in_specs=placed, out_specs=P(None, "ha", "wa", "col"), check_vma=False
    )
```

```python
import functools

import jax
import jax.numpy as jnp
from jax import lax
from jax.experimental import pallas as pl
from jax.experimental.pallas import tpu as pltpu
from jax.sharding import PartitionSpec as P

F32 = jnp.float32
BF16 = jnp.bfloat16
CH = 128
GROUP = 16
ROWS = 8
COLS = 32
MIB = 1 << 20

VMEM = pl.BlockSpec(memory_space=pltpu.VMEM)
SMEM = pl.BlockSpec(memory_space=pltpu.SMEM)
ANY = pl.BlockSpec(memory_space=pl.ANY)
HBM = pl.BlockSpec(memory_space=pltpu.HBM)
HA = ("z", "core")


class Left:
    def __init__(self, array, spec=ANY):
        self.array, self.spec = array, spec
        if spec is HBM:
            self.array = pltpu.with_memory_space_constraint(array, pltpu.HBM)


def call(body, outs, scratch=(), flops=0, limit=8, name=None):
    def run(*args):
        specs = [a.spec if isinstance(a, Left) else SMEM if a.dtype == jnp.int32 else VMEM for a in args]
        args = [a.array if isinstance(a, Left) else a for a in args]
        nbytes = sum(a.size * a.dtype.itemsize for a in args + list(outs))
        return pl.pallas_call(
            body,
            out_shape=list(outs),
            in_specs=specs,
            out_specs=[VMEM] * len(outs),
            scratch_shapes=list(scratch),
            compiler_params=pltpu.CompilerParams(vmem_limit_bytes=limit * MIB),
            cost_estimate=pl.CostEstimate(flops=flops, bytes_accessed=nbytes, transcendentals=0),
            name=name,
        )(*args)

    return run


def sds(shape, dtype=BF16):
    return jax.ShapeDtypeStruct(shape, dtype)


def group_sum(row):
    lane = lax.broadcasted_iota(jnp.int32, row.shape, 1)
    shift = 1
    while shift < GROUP:
        other = jnp.where((lane & shift) != 0, pltpu.roll(row, shift, 1), pltpu.roll(row, CH - shift, 1))
        row = row + other
        shift *= 2
    return row


def local_stats(flat):
    count = flat.shape[0] * GROUP
    mean = group_sum(jnp.sum(flat, axis=0, keepdims=True)) * (1.0 / count)
    dev = flat - mean
    m2 = group_sum(jnp.sum(dev * dev, axis=0, keepdims=True))
    return mean, m2


def combine(st_ref, count):
    devices = st_ref.shape[0]
    means = st_ref[:, 0, :]
    mean = jnp.sum(means, axis=0, keepdims=True) * (1.0 / devices)
    apart = means - mean
    m2 = jnp.sum(st_ref[:, 1, :] + count * (apart * apart), axis=0, keepdims=True)
    return mean, lax.rsqrt(m2 * (1.0 / (count * devices)) + 1e-6)


def slot_body(st_ref, *rest):
    o_ref = rest[-1]
    o_ref[...] = jnp.broadcast_to(st_ref[...][None], o_ref.shape)


def spread_stats(stats, after):
    pair = lax.all_gather(stats, "core")
    chips = lax.axis_size("z") * lax.axis_size("wa")
    pair = pair.reshape(2 * pair.shape[0], CH)
    (slots,) = call(slot_body, [sds((chips,) + pair.shape, F32)], name="slots")(pair, *[Left(a) for a in after])
    return lax.all_to_all(slots, ("z", "wa"), 0, 0, tiled=True).reshape(-1, 2, CH)


def store_edges(ref_slices, top_ref, bot_ref, lef_ref, rig_ref):
    at = 0
    for ref in ref_slices:
        n = ref.shape[0]
        top_ref[at : at + n] = ref[:, 0]
        bot_ref[at : at + n] = ref[:, ROWS - 1]
        v = ref[...].astype(F32)
        pad = jnp.zeros((n, 8, CH), F32)
        lef_ref[at : at + n] = jnp.concatenate([v[:, :, 0, :], pad], axis=1).astype(BF16)
        rig_ref[at : at + n] = jnp.concatenate([v[:, :, COLS - 1, :], pad], axis=1).astype(BF16)
        at += n


def first_body(x_hbm, c1_hbm, c2_hbm, x_ref, c1_ref, c2_ref, st_ref, top_ref, bot_ref, lef_ref, rig_ref, sem):
    copies = [
        pltpu.make_async_copy(src, dst, sem.at[i])
        for i, (src, dst) in enumerate(((x_hbm, x_ref), (c1_hbm, c1_ref), (c2_hbm, c2_ref)))
    ]
    for c in copies:
        c.start()
    for c in copies:
        c.wait()
    mean, m2 = local_stats(x_ref[...].astype(F32).reshape(-1, CH))
    st_ref[0:1, :] = mean
    st_ref[1:2, :] = m2
    store_edges([c1_ref, x_ref, c2_ref], top_ref, bot_ref, lef_ref, rig_ref)


def corner_body(top_ref, bot_ref, lef_ref, rig_ref, *rest):
    lo_ref, ro_ref = rest[-2:]
    row = lax.broadcasted_iota(jnp.int32, lef_ref.shape, 1)
    top = top_ref[...].astype(F32)
    bot = bot_ref[...].astype(F32)
    for src, dst, at in ((lef_ref, lo_ref, 0), (rig_ref, ro_ref, COLS - 1)):
        v = src[...].astype(F32)
        v = jnp.where(row == 8, top[:, at : at + 1, :], v)
        v = jnp.where(row == 9, bot[:, at : at + 1, :], v)
        dst[...] = v.astype(BF16)


def swap_rows(top, bot):
    n = lax.axis_size(HA)
    above = lax.ppermute(bot, HA, [(i, i + 1) for i in range(n - 1)])
    below = lax.ppermute(top, HA, [(i + 1, i) for i in range(n - 1)])
    return above, below


def swap_columns(above, below, lef, rig, after=()):
    n = lax.axis_size("wa")
    lo, ro = call(corner_body, [sds(lef.shape)] * 2, name="corners")(
        above, below, lef, rig, *[Left(a) for a in after]
    )
    left = lax.ppermute(ro, "wa", [(i, i + 1) for i in range(n - 1)])
    right = lax.ppermute(lo, "wa", [(i + 1, i) for i in range(n - 1)])
    return (left, right), lo


def shifted(rows, left, right):
    n = rows.shape[0]
    flat = rows.reshape(n * COLS, CH)
    col = lax.broadcasted_iota(jnp.int32, rows.shape, 1)
    before = pltpu.roll(flat, 1, 0).reshape(rows.shape)
    after = pltpu.roll(flat, n * COLS - 1, 0).reshape(rows.shape)
    before = jnp.where(col == 0, left[:, None, :], before)
    after = jnp.where(col == COLS - 1, right[:, None, :], after)
    return before, after


def place(patch_ref, frame, rows, at, left, right, lanes):
    n = rows.shape[0]
    before, after = shifted(rows, left, right)
    for e, v in enumerate((before, rows, after)):
        patch_ref[frame, at * COLS : (at + n) * COLS, lanes[e] : lanes[e] + CH] = v.reshape(n * COLS, CH).astype(BF16)


def place_frame(patch_ref, frame, inner, top, bot, lef, rig, lanes):
    place(patch_ref, frame, inner, 1, lef[0:8], rig[0:8], lanes)
    place(patch_ref, frame, top[None], 0, lef[8:9], rig[8:9], lanes)
    place(patch_ref, frame, bot[None], ROWS + 1, lef[9:10], rig[9:10], lanes)


def multiply(patch_ref, w_ref, outs):
    depth = 9 * CH
    size = ROWS * COLS
    for t in range(4):
        acc = None
        for a in range(3):
            lhs = jnp.concatenate([patch_ref[t + a, b * COLS : b * COLS + size, :] for b in range(3)], axis=1)
            part = jnp.dot(lhs, w_ref[a * depth : (a + 1) * depth, :], preferred_element_type=F32)
            acc = part if acc is None else acc + part
        for i, out in enumerate(outs):
            out[t * size : (t + 1) * size, :] = acc[:, i * CH : (i + 1) * CH].astype(BF16)


def far_body(cache_at, act_at, extra, flag_ref, st_ref, x_ref, c_ref, tc, bc, lc, rc, ta, ba, la, ra, w_hbm, *rest):
    out2, out1, patch_ref, near_ref, w_ref, sem = rest[extra:]
    col = flag_ref[4]
    copies = []
    for i, (k, dst, at) in enumerate(((2, w_ref, 0), (1, w_ref, CH), (3, near_ref, 0), (0, near_ref, CH))):
        block = pl.multiple_of(lax.rem(col + k, 4) * CH, CH)
        copies.append(
            pltpu.make_async_copy(w_hbm.at[:, pl.ds(block, CH)], dst.at[:, at : at + CH], sem.at[i])
        )
        copies[-1].start()
    has = [flag_ref[i] > 0 for i in range(4)]
    mean, scale = combine(st_ref, x_ref.shape[0] * ROWS * COLS * GROUP)

    def act(v):
        u = (v - mean) * scale
        return u / (1.0 + jnp.exp(-u))

    lanes = (0, CH, 2 * CH)
    for s in range(2):
        place_frame(
            patch_ref,
            s,
            c_ref[s].astype(F32),
            tc[cache_at + s].astype(F32),
            bc[cache_at + s].astype(F32),
            lc[cache_at + s].astype(F32),
            rc[cache_at + s].astype(F32),
            lanes,
        )
    row = lax.broadcasted_iota(jnp.int32, (16, CH), 0)
    edge = jnp.where(row == 8, flag_ref[0], jnp.where(row == 9, flag_ref[1], 1))
    for s in range(4):
        side = []
        for ref, flag in ((la, flag_ref[2]), (ra, flag_ref[3])):
            side.append(jnp.where(edge * flag > 0, act(ref[act_at + s].astype(F32)), 0.0))
        place_frame(
            patch_ref,
            2 + s,
            act(x_ref[s].astype(F32)),
            jnp.where(has[0], act(ta[act_at + s].astype(F32)), 0.0),
            jnp.where(has[1], act(ba[act_at + s].astype(F32)), 0.0),
            side[0],
            side[1],
            lanes,
        )
    copies[0].wait()
    copies[1].wait()
    multiply(patch_ref, w_ref, (out2, out1))
    copies[2].wait()
    copies[3].wait()


def near_body(patch_ref, w_ref, out3, out0):
    multiply(patch_ref, w_ref, (out3, out0))


def conv(flags, stats, x, cache, cache_halo, cache_at, act_halo, act_at, weight, name, after=()):
    n = x.shape[0] * ROWS * COLS
    depth, width = weight.shape
    flops = n * depth * width
    piece = sds((n, CH))
    body = functools.partial(far_body, cache_at, act_at, len(after))
    out2, out1, patch, near = call(
        body,
        [piece] * 2 + [sds((6, (ROWS + 2) * COLS, 3 * CH)), sds((depth, 2 * CH))],
        scratch=[pltpu.VMEM((depth, 2 * CH), BF16), pltpu.SemaphoreType.DMA((4,))],
        flops=flops,
        limit=20,
        name=name + "_far",
    )(flags, stats, x, cache, *cache_halo, *act_halo, Left(weight, HBM), *[Left(a) for a in after])
    got2 = to_peer(out2, 2)
    got1 = to_peer(out1, 1)
    out3, own = call(near_body, [piece] * 2, flops=flops, limit=16, name=name + "_near")(patch, near)
    (far,) = call(add_body, [sds((n, CH), F32)], name=name + "_add")(got1, got2)
    return own, far, to_peer(out3, 3)


def add_body(a_ref, b_ref, o_ref):
    o_ref[...] = a_ref[...].astype(F32) + b_ref[...].astype(F32)


def to_peer(piece, k):
    n = lax.axis_size("col")
    return lax.ppermute(piece, "col", [(i, (i + k) % n) for i in range(n)])


def to_peers(pieces):
    got = {k: to_peer(pieces[k - 1], k) for k in (2, 1, 3)}
    return [got[k] for k in (1, 2, 3)]


def hidden_body(p0, far, p3, h_ref, st_ref, top_ref, bot_ref, lef_ref, rig_ref):
    total = p0[...].astype(F32) + p3[...].astype(F32) + far[...]
    h = total.astype(BF16)
    h_ref[...] = h.reshape(h_ref.shape)
    mean, m2 = local_stats(h.astype(F32))
    st_ref[0:1, :] = mean
    st_ref[1:2, :] = m2
    store_edges([h_ref], top_ref, bot_ref, lef_ref, rig_ref)


def resid_body(x_ref, p0, far, p3, h_ref, top_ref, bot_ref, lef_ref, rig_ref):
    total = p0[...].astype(F32) + p3[...].astype(F32) + far[...]
    h_ref[...] = (x_ref[...].astype(F32) + total.reshape(x_ref.shape)).astype(BF16)
    store_edges([h_ref], top_ref, bot_ref, lef_ref, rig_ref)


ROW_TAPS = {(0, 0): (-1, 0), (0, 1): (1,), (1, 0): (-1,), (1, 1): (0, 1)}
COL_TAPS = {(0, 0): (-1,), (0, 1): (0, 1), (1, 0): (-1, 0), (1, 1): (1,)}


def split_body(flag_ref, w_hbm, after_ref, *rest):
    outs, sem = rest[:4], rest[4]
    copies = []
    for k, out in enumerate(outs):
        block = pl.multiple_of(lax.rem(flag_ref[4] + k, 4) * CH, CH)
        copies.append(pltpu.make_async_copy(w_hbm.at[:, :, pl.ds(block, CH)], out, sem.at[k]))
        copies[-1].start()
    for c in copies:
        c.wait()


def split_weight(flags, weight, after):
    return call(
        split_body,
        [sds(weight.shape[:2] + (CH,))] * 4,
        scratch=[pltpu.SemaphoreType.DMA((4,))],
        name="split_weight",
    )(flags, Left(weight, HBM), Left(after))


def fold_body(w0, w1, w2, w3, o_ref):
    for k, ref in enumerate((w0, w1, w2, w3)):
        taps = [ref[i].astype(F32) for i in range(9)]
        for q in range(2):
            for r in range(2):
                for s in range(2):
                    for p in range(2):
                        total = None
                        for b in ROW_TAPS[p, r]:
                            for e in COL_TAPS[q, s]:
                                tap = taps[(b + 1) * 3 + (e + 1)]
                                total = tap if total is None else total + tap
                        at = (s * 4 + k) * CH
                        o_ref[q, r, at : at + CH, p * CH : (p + 1) * CH] = total.astype(BF16)


def up_body(*refs):
    parts = [refs[2 * k : 2 * k + 2] for k in range(4)]
    w_ref, o_ref, patch_ref, mix_ref = refs[8:12]
    size = (ROWS + 1) * COLS
    half = 2 * 4 * CH
    for k, (x, border) in enumerate(parts):
        edge = border[0].astype(F32)
        place_frame(
            patch_ref,
            0,
            x[0].astype(F32),
            edge[:COLS],
            edge[COLS : 2 * COLS],
            edge[2 * COLS : 2 * COLS + 16],
            edge[2 * COLS + 16 :],
            [(e * 4 + k) * CH for e in range(3)],
        )
    for q in range(2):
        acc = None
        for r in range(2):
            lhs = patch_ref[0, r * COLS : r * COLS + size, q * 4 * CH : q * 4 * CH + half]
            part = jnp.dot(lhs, w_ref[q, r], preferred_element_type=F32)
            acc = part if acc is None else acc + part
        for n in range(ROWS + 1):
            for p in range(2):
                i = 2 * n - 1 + p
                if 0 <= i < 2 * ROWS:
                    mix_ref[i, pl.ds(q, COLS, stride=2), :] = acc[n * COLS : (n + 1) * COLS, p * CH : (p + 1) * CH]
    o_ref[0] = mix_ref[...].astype(BF16)


def up_conv(parts, weight):
    specs = []
    args = []
    for part in parts:
        for a in part:
            rest = a.shape[1:]
            specs.append(pl.BlockSpec((1,) + rest, lambda t, n=len(rest): (t,) + (0,) * n))
            args.append(a)
    specs.append(pl.BlockSpec(weight.shape, lambda t: (0, 0, 0, 0)))
    frames = parts[0][0].shape[0]
    out = (frames, 2 * ROWS, 2 * COLS, CH)
    return pl.pallas_call(
        up_body,
        out_shape=sds(out),
        grid=(frames,),
        in_specs=specs,
        out_specs=pl.BlockSpec((1,) + out[1:], lambda t: (t, 0, 0, 0)),
        scratch_shapes=[
            pltpu.VMEM((1, (ROWS + 2) * COLS, 12 * CH), BF16),
            pltpu.VMEM((2 * ROWS, 2 * COLS, CH), F32),
        ],
        compiler_params=pltpu.CompilerParams(vmem_limit_bytes=24 * MIB),
        name="up_conv",
    )(*args, weight)


def on_device(features, cache_first, cache_second, weight_first, weight_second, weight_up):
    frames = features.shape[0]
    ha, wa, col = lax.axis_index(HA), lax.axis_index("wa"), lax.axis_index("col")
    nh, nw = lax.axis_size(HA), lax.axis_size("wa")
    flags = jnp.stack([ha > 0, ha < nh - 1, wa > 0, wa < nw - 1, col]).astype(jnp.int32)

    x, c1, c2, stats, *edges = call(
        first_body,
        [sds(features.shape), sds(cache_first.shape), sds(cache_second.shape), sds((2, CH), F32)]
        + [sds((8, COLS, CH))] * 2
        + [sds((8, 16, CH))] * 2,
        scratch=[pltpu.SemaphoreType.DMA((3,))],
        limit=20,
        name="first",
    )(Left(features, HBM), Left(cache_first, HBM), Left(cache_second, HBM))
    halo = swap_rows(*edges[:2])
    stats = spread_stats(stats, halo)
    columns, carrying = swap_columns(*halo, *edges[2:])
    w_pieces = split_weight(flags, weight_up, carrying)
    w_got = to_peers(w_pieces[1:])
    halo += columns
    pieces = conv(
        flags, stats, x, c1, halo, 0, halo, 2, weight_first.reshape(-1, 4 * CH), "conv_first", after=w_got
    )
    hidden, stats, *edges = call(
        hidden_body,
        [sds(features.shape), sds((2, CH), F32)] + [sds((frames, COLS, CH))] * 2 + [sds((frames, 16, CH))] * 2,
        name="hidden",
    )(*pieces)
    halo2 = swap_rows(*edges[:2])
    stats = spread_stats(stats, halo2)
    halo2 += swap_columns(*halo2, *edges[2:])[0]
    (folded,) = call(fold_body, [sds((2, 2, 8 * CH, 2 * CH))], limit=12, name="fold")(w_pieces[0], *w_got)
    pieces = conv(
        flags, stats, hidden, c2, halo, 6, halo2, 0, weight_second.reshape(-1, 4 * CH), "conv_second"
    )
    resid, *edges = call(
        resid_body,
        [sds(features.shape)] + [sds((frames, COLS, CH))] * 2 + [sds((frames, 16, CH))] * 2,
        name="resid",
    )(features, *pieces)
    others = to_peers([resid] * 3)
    rows = swap_rows(*edges[:2])
    columns, _ = swap_columns(*rows, *edges[2:], after=others[:1])
    (border,) = call(pack_body, [sds((frames, 2 * COLS + 32, CH))], name="pack")(
        *rows, *columns, *[Left(a) for a in others[1:]]
    )
    borders = [border] + to_peers([border] * 3)
    return up_conv(list(zip([resid] + others, borders)), folded)


def pack_body(top_ref, bot_ref, lef_ref, rig_ref, *rest):
    o_ref = rest[-1]
    at = 0
    for ref in (top_ref, bot_ref, lef_ref, rig_ref):
        n = ref.shape[1]
        o_ref[:, at : at + n, :] = ref[...]
        at += n


def solution(mesh):
    shape = mesh.devices.shape
    mesh = jax.sharding.Mesh(
        mesh.devices.reshape((shape[0] // 2, 2) + shape[1:]), HA + tuple(mesh.axis_names[1:])
    )
    block = P(None, HA, "wa", "col")
    weight = P(None, "col", None)
    return jax.shard_map(
        on_device,
        mesh=mesh,
        in_specs=(block, block, block, weight, weight, weight),
        out_specs=block,
        check_vma=False,
    )
```

```python
import functools

import jax
import jax.numpy as jnp
from jax import lax
from jax.experimental import pallas as pl
from jax.experimental.pallas import tpu as pltpu
from jax.sharding import PartitionSpec as P

F32 = jnp.float32
BF16 = jnp.bfloat16
CH = 128
GROUP = 16
ROWS = 8
COLS = 32
MIB = 1 << 20
CORNERS = ((0, 0), (0, 1), (1, 0), (1, 1))

VMEM = pl.BlockSpec(memory_space=pltpu.VMEM)
SMEM = pl.BlockSpec(memory_space=pltpu.SMEM)
ANY = pl.BlockSpec(memory_space=pl.ANY)
HBM = pl.BlockSpec(memory_space=pltpu.HBM)
HA = ("z", "core")


class Left:
    def __init__(self, array, spec=ANY):
        self.array, self.spec = array, spec
        if spec is HBM:
            self.array = pltpu.with_memory_space_constraint(array, pltpu.HBM)


def call(body, outs, scratch=(), flops=0, limit=8, name=None):
    def run(*args):
        specs = [a.spec if isinstance(a, Left) else SMEM if a.dtype == jnp.int32 else VMEM for a in args]
        args = [a.array if isinstance(a, Left) else a for a in args]
        nbytes = sum(a.size * a.dtype.itemsize for a in args + list(outs))
        return pl.pallas_call(
            body,
            out_shape=list(outs),
            in_specs=specs,
            out_specs=[VMEM] * len(outs),
            scratch_shapes=list(scratch),
            compiler_params=pltpu.CompilerParams(vmem_limit_bytes=limit * MIB),
            cost_estimate=pl.CostEstimate(flops=flops, bytes_accessed=nbytes, transcendentals=0),
            name=name,
        )(*args)

    return run


def sds(shape, dtype=BF16):
    return jax.ShapeDtypeStruct(shape, dtype)


def group_sum(row):
    lane = lax.broadcasted_iota(jnp.int32, row.shape, 1)
    shift = 1
    while shift < GROUP:
        other = jnp.where((lane & shift) != 0, pltpu.roll(row, shift, 1), pltpu.roll(row, CH - shift, 1))
        row = row + other
        shift *= 2
    return row


def local_stats(flat):
    count = flat.shape[0] * GROUP
    mean = group_sum(jnp.sum(flat, axis=0, keepdims=True)) * (1.0 / count)
    dev = flat - mean
    m2 = group_sum(jnp.sum(dev * dev, axis=0, keepdims=True))
    return mean, m2


def combine(st_ref, count):
    devices = st_ref.shape[0]
    means = st_ref[:, 0, :]
    mean = jnp.sum(means, axis=0, keepdims=True) * (1.0 / devices)
    apart = means - mean
    m2 = jnp.sum(st_ref[:, 1, :] + count * (apart * apart), axis=0, keepdims=True)
    return mean, lax.rsqrt(m2 * (1.0 / (count * devices)) + 1e-6)


def spread(slots):
    return lax.all_to_all(slots, HA + ("wa",), 0, 0, tiled=True)


def diagonals(flag_ref):
    wa_size = lax.axis_size("wa")
    found = []
    for r, c in CORNERS:
        valid = flag_ref[r] * flag_ref[2 + c]
        found.append((valid, flag_ref[5] + valid * ((2 * r - 1) * wa_size + 2 * c - 1)))
    return found


def fill_slots(slot_ref, flag_ref, mean, m2, frames):
    row = lax.broadcasted_iota(jnp.int32, (8, CH), 0)
    base = jnp.where(row == 0, mean, jnp.where(row == 1, m2, 0.0))
    slot_ref[...] = jnp.broadcast_to(base[None], slot_ref.shape)
    for (r, c), (valid, at) in zip(CORNERS, diagonals(flag_ref)):

        @pl.when(valid > 0)
        def _():
            f = 0
            for v in frames:
                for i in range(v.shape[0]):
                    pixel = v[i, r * (ROWS - 1), c * (COLS - 1) : c * (COLS - 1) + 1, :]
                    slot_ref[pl.ds(at, 1), 2 + f, :] = pixel
                    f += 1


def store_edges(frames, refs, pad=0):
    top_ref, bot_ref, lef_ref, rig_ref = refs
    at = 0
    for v in frames:
        n = v.shape[0]
        top_ref[at : at + n] = v[:, 0].astype(BF16)
        bot_ref[at : at + n] = v[:, ROWS - 1].astype(BF16)
        for ref, column in ((lef_ref, v[:, :, 0, :]), (rig_ref, v[:, :, COLS - 1, :])):
            if pad:
                column = jnp.concatenate([column, jnp.zeros((n, pad, CH), F32)], axis=1)
            ref[at : at + n] = column.astype(BF16)
        at += n


def first_body(flag_ref, x_hbm, c1_hbm, c2_hbm, w_hbm, x_ref, c1_ref, c2_ref, slot_ref, *rest):
    edges, pieces, sem = rest[:4], rest[4:8], rest[8]
    pairs = [(x_hbm, x_ref), (c1_hbm, c1_ref), (c2_hbm, c2_ref)]
    for k, piece in enumerate(pieces):
        block = pl.multiple_of(lax.rem(flag_ref[4] + k, 4) * CH, CH)
        pairs.append((w_hbm.at[:, :, pl.ds(block, CH)], piece))
    copies = [pltpu.make_async_copy(src, dst, sem.at[i]) for i, (src, dst) in enumerate(pairs)]
    for c in copies:
        c.start()
    for c in copies[:3]:
        c.wait()
    x, c1, c2 = x_ref[...].astype(F32), c1_ref[...].astype(F32), c2_ref[...].astype(F32)
    mean, m2 = local_stats(x.reshape(-1, CH))
    fill_slots(slot_ref, flag_ref, mean, m2, (c1, x))
    store_edges((c1, x, c2), edges)
    for c in copies[3:]:
        c.wait()


def corner_body(top_ref, bot_ref, lef_ref, rig_ref, *rest):
    lo_ref, ro_ref = rest[-2:]
    row = lax.broadcasted_iota(jnp.int32, lef_ref.shape, 1)
    top = top_ref[...].astype(F32)
    bot = bot_ref[...].astype(F32)
    for src, dst, at in ((lef_ref, lo_ref, 0), (rig_ref, ro_ref, COLS - 1)):
        v = src[...].astype(F32)
        v = jnp.where(row == 8, top[:, at : at + 1, :], v)
        v = jnp.where(row == 9, bot[:, at : at + 1, :], v)
        dst[...] = v.astype(BF16)


def swap_rows(top, bot):
    n = lax.axis_size(HA)
    above = lax.ppermute(bot, HA, [(i, i + 1) for i in range(n - 1)])
    below = lax.ppermute(top, HA, [(i + 1, i) for i in range(n - 1)])
    return above, below


def swap_columns(lef, rig):
    n = lax.axis_size("wa")
    left = lax.ppermute(rig, "wa", [(i, i + 1) for i in range(n - 1)])
    right = lax.ppermute(lef, "wa", [(i + 1, i) for i in range(n - 1)])
    return left, right


def shifted(rows, left, right):
    n = rows.shape[0]
    flat = rows.reshape(n * COLS, CH)
    col = lax.broadcasted_iota(jnp.int32, rows.shape, 1)
    before = pltpu.roll(flat, 1, 0).reshape(rows.shape)
    after = pltpu.roll(flat, n * COLS - 1, 0).reshape(rows.shape)
    before = jnp.where(col == 0, left[:, None, :], before)
    after = jnp.where(col == COLS - 1, right[:, None, :], after)
    return before, after


def place(patch_ref, frame, rows, at, left, right, lanes):
    n = rows.shape[0]
    before, after = shifted(rows, left, right)
    for e, v in enumerate((before, rows, after)):
        patch_ref[frame, at * COLS : (at + n) * COLS, lanes[e] : lanes[e] + CH] = v.reshape(n * COLS, CH).astype(BF16)


def place_frame(patch_ref, frame, inner, top, bot, lef, rig, corners, lanes):
    place(patch_ref, frame, inner, 1, lef, rig, lanes)
    place(patch_ref, frame, top[None], 0, corners[0], corners[1], lanes)
    place(patch_ref, frame, bot[None], ROWS + 1, corners[2], corners[3], lanes)


def multiply(patch_ref, w_ref, outs):
    depth = 9 * CH
    size = ROWS * COLS
    for t in range(4):
        acc = None
        for a in range(3):
            lhs = jnp.concatenate([patch_ref[t + a, b * COLS : b * COLS + size, :] for b in range(3)], axis=1)
            part = jnp.dot(lhs, w_ref[a * depth : (a + 1) * depth, :], preferred_element_type=F32)
            acc = part if acc is None else acc + part
        for i, out in enumerate(outs):
            out[t * size : (t + 1) * size, :] = acc[:, i * CH : (i + 1) * CH].astype(BF16)


def far_body(cache_at, act_at, extra, flag_ref, st_ref, x_ref, c_ref, tc, bc, lc, rc, ta, ba, la, ra, w_hbm, *rest):
    out2, out1, patch_ref, near_ref, w_ref, sem = rest[extra:]
    col = flag_ref[4]
    copies = []
    for i, (k, dst, at) in enumerate(((2, w_ref, 0), (1, w_ref, CH), (3, near_ref, 0), (0, near_ref, CH))):
        block = pl.multiple_of(lax.rem(col + k, 4) * CH, CH)
        copies.append(
            pltpu.make_async_copy(w_hbm.at[:, pl.ds(block, CH)], dst.at[:, at : at + CH], sem.at[i])
        )
        copies[-1].start()
    has = [flag_ref[i] > 0 for i in range(4)]
    mean, scale = combine(st_ref, x_ref.shape[0] * ROWS * COLS * GROUP)

    def act(v):
        u = (v - mean) * scale
        return u / (1.0 + jnp.exp(-u))

    lanes = (0, CH, 2 * CH)
    across = diagonals(flag_ref)
    for s in range(6):
        if s < 2:
            own, at, halo, change = c_ref[s], cache_at + s, (tc, bc, lc, rc), lambda v: v
        else:
            own, at, halo, change = x_ref[s - 2], act_at + s - 2, (ta, ba, la, ra), act
        sides = [jnp.where(has[i], change(ref[at].astype(F32)), 0.0) for i, ref in enumerate(halo)]
        corners = [
            jnp.where(valid > 0, change(st_ref[pl.ds(slot, 1), 2 + s, :]), 0.0) for valid, slot in across
        ]
        place_frame(patch_ref, s, change(own.astype(F32)), *sides, corners, lanes)
    copies[0].wait()
    copies[1].wait()
    multiply(patch_ref, w_ref, (out2, out1))
    copies[2].wait()
    copies[3].wait()


def near_body(patch_ref, w_ref, out3, out0):
    multiply(patch_ref, w_ref, (out3, out0))


def conv(flags, stats, x, cache, cache_halo, cache_at, act_halo, act_at, weight, name, after=()):
    n = x.shape[0] * ROWS * COLS
    depth, width = weight.shape
    flops = n * depth * width
    piece = sds((n, CH))
    body = functools.partial(far_body, cache_at, act_at, len(after))
    out2, out1, patch, near = call(
        body,
        [piece] * 2 + [sds((6, (ROWS + 2) * COLS, 3 * CH)), sds((depth, 2 * CH))],
        scratch=[pltpu.VMEM((depth, 2 * CH), BF16), pltpu.SemaphoreType.DMA((4,))],
        flops=flops,
        limit=20,
        name=name + "_far",
    )(flags, stats, x, cache, *cache_halo, *act_halo, Left(weight, HBM), *[Left(a) for a in after])
    got2 = to_peer(out2, 2)
    got1 = to_peer(out1, 1)
    out3, own = call(near_body, [piece] * 2, flops=flops, limit=16, name=name + "_near")(patch, near)
    (far,) = call(add_body, [sds((n, CH), F32)], name=name + "_add")(got1, got2)
    return own, far, to_peer(out3, 3)


def add_body(a_ref, b_ref, o_ref):
    o_ref[...] = a_ref[...].astype(F32) + b_ref[...].astype(F32)


def to_peer(piece, k):
    n = lax.axis_size("col")
    return lax.ppermute(piece, "col", [(i, (i + k) % n) for i in range(n)])


def to_peers(pieces):
    got = {k: to_peer(pieces[k - 1], k) for k in (2, 1, 3)}
    return [got[k] for k in (1, 2, 3)]


def hidden_body(flag_ref, p0, far, p3, c2_ref, h_ref, slot_ref, *edges):
    h = (p0[...].astype(F32) + p3[...].astype(F32) + far[...]).astype(BF16)
    h_ref[...] = h.reshape(h_ref.shape)
    h = h.astype(F32)
    mean, m2 = local_stats(h)
    h = h.reshape(h_ref.shape)
    fill_slots(slot_ref, flag_ref, mean, m2, (c2_ref[...].astype(F32), h))
    store_edges((h,), edges)


def resid_body(x_ref, p0, far, p3, h_ref, *edges):
    total = p0[...].astype(F32) + p3[...].astype(F32) + far[...]
    h = (x_ref[...].astype(F32) + total.reshape(x_ref.shape)).astype(BF16)
    h_ref[...] = h
    store_edges((h.astype(F32),), edges, pad=8)


ROW_TAPS = {(0, 0): (-1, 0), (0, 1): (1,), (1, 0): (-1,), (1, 1): (0, 1)}
COL_TAPS = {(0, 0): (-1,), (0, 1): (0, 1), (1, 0): (-1, 0), (1, 1): (1,)}


def fold_body(w0, w1, w2, w3, o_ref):
    for k, ref in enumerate((w0, w1, w2, w3)):
        taps = [ref[i].astype(F32) for i in range(9)]
        for q in range(2):
            for r in range(2):
                for s in range(2):
                    for p in range(2):
                        total = None
                        for b in ROW_TAPS[p, r]:
                            for e in COL_TAPS[q, s]:
                                tap = taps[(b + 1) * 3 + (e + 1)]
                                total = tap if total is None else total + tap
                        at = (s * 4 + k) * CH
                        o_ref[q, r, at : at + CH, p * CH : (p + 1) * CH] = total.astype(BF16)


def up_body(*refs):
    parts = [refs[2 * k : 2 * k + 2] for k in range(4)]
    w_ref, o_ref, patch_ref, mix_ref = refs[8:12]
    size = (ROWS + 1) * COLS
    half = 2 * 4 * CH
    for k, (x, border) in enumerate(parts):
        edge = border[0].astype(F32)
        place_frame(
            patch_ref,
            0,
            x[0].astype(F32),
            edge[:COLS],
            edge[COLS : 2 * COLS],
            edge[2 * COLS : 2 * COLS + 8],
            edge[2 * COLS + 16 : 2 * COLS + 24],
            [edge[2 * COLS + i : 2 * COLS + i + 1] for i in (8, 24, 9, 25)],
            [(e * 4 + k) * CH for e in range(3)],
        )
    for q in range(2):
        acc = None
        for r in range(2):
            lhs = patch_ref[0, r * COLS : r * COLS + size, q * 4 * CH : q * 4 * CH + half]
            part = jnp.dot(lhs, w_ref[q, r], preferred_element_type=F32)
            acc = part if acc is None else acc + part
        for n in range(ROWS + 1):
            for p in range(2):
                i = 2 * n - 1 + p
                if 0 <= i < 2 * ROWS:
                    mix_ref[i, pl.ds(q, COLS, stride=2), :] = acc[n * COLS : (n + 1) * COLS, p * CH : (p + 1) * CH]
    o_ref[0] = mix_ref[...].astype(BF16)


def up_conv(parts, weight):
    specs = []
    args = []
    for part in parts:
        for a in part:
            rest = a.shape[1:]
            specs.append(pl.BlockSpec((1,) + rest, lambda t, n=len(rest): (t,) + (0,) * n))
            args.append(a)
    specs.append(pl.BlockSpec(weight.shape, lambda t: (0, 0, 0, 0)))
    frames = parts[0][0].shape[0]
    out = (frames, 2 * ROWS, 2 * COLS, CH)
    return pl.pallas_call(
        up_body,
        out_shape=sds(out),
        grid=(frames,),
        in_specs=specs,
        out_specs=pl.BlockSpec((1,) + out[1:], lambda t: (t, 0, 0, 0)),
        scratch_shapes=[
            pltpu.VMEM((1, (ROWS + 2) * COLS, 12 * CH), BF16),
            pltpu.VMEM((2 * ROWS, 2 * COLS, CH), F32),
        ],
        compiler_params=pltpu.CompilerParams(vmem_limit_bytes=24 * MIB),
        name="up_conv",
    )(*args, weight)


def on_device(features, cache_first, cache_second, weight_first, weight_second, weight_up):
    frames = features.shape[0]
    ha, wa, col = lax.axis_index(HA), lax.axis_index("wa"), lax.axis_index("col")
    nh, nw = lax.axis_size(HA), lax.axis_size("wa")
    flags = jnp.stack([ha > 0, ha < nh - 1, wa > 0, wa < nw - 1, col, ha * nw + wa]).astype(jnp.int32)
    slots = sds((nh * nw, 8, CH), F32)

    x, c1, c2, stats, *edges = call(
        first_body,
        [sds(features.shape), sds(cache_first.shape), sds(cache_second.shape), slots]
        + [sds((8, COLS, CH))] * 2
        + [sds((8, ROWS, CH))] * 2
        + [sds(weight_up.shape[:2] + (CH,))] * 4,
        scratch=[pltpu.SemaphoreType.DMA((7,))],
        limit=20,
        name="first",
    )(flags, *[Left(a, HBM) for a in (features, cache_first, cache_second, weight_up)])
    edges, w_pieces = edges[:4], edges[4:]
    w_got = to_peers(w_pieces[1:])
    halo = swap_rows(*edges[:2]) + swap_columns(*edges[2:])
    stats = spread(stats)
    pieces = conv(
        flags, stats, x, c1, halo, 0, halo, 2, weight_first.reshape(-1, 4 * CH), "conv_first", after=w_got
    )
    hidden, stats, *edges = call(
        hidden_body,
        [sds(features.shape), slots] + [sds((frames, COLS, CH))] * 2 + [sds((frames, ROWS, CH))] * 2,
        limit=12,
        name="hidden",
    )(flags, *pieces, c2)
    halo2 = swap_rows(*edges[:2]) + swap_columns(*edges[2:])
    stats = spread(stats)
    (folded,) = call(fold_body, [sds((2, 2, 8 * CH, 2 * CH))], limit=12, name="fold")(w_pieces[0], *w_got)
    pieces = conv(
        flags, stats, hidden, c2, halo, 6, halo2, 0, weight_second.reshape(-1, 4 * CH), "conv_second"
    )
    resid, *edges = call(
        resid_body,
        [sds(features.shape)] + [sds((frames, COLS, CH))] * 2 + [sds((frames, 16, CH))] * 2,
        name="resid",
    )(features, *pieces)
    others = to_peers([resid] * 3)
    rows = swap_rows(*edges[:2])
    cornered = call(corner_body, [sds((frames, 16, CH))] * 2, name="corners")(*rows, *edges[2:], Left(others[0]))
    columns = swap_columns(*cornered)
    (border,) = call(pack_body, [sds((frames, 2 * COLS + 32, CH))], name="pack")(
        *rows, *columns, *[Left(a) for a in others[1:]]
    )
    borders = [border] + to_peers([border] * 3)
    return up_conv(list(zip([resid] + others, borders)), folded)


def pack_body(top_ref, bot_ref, lef_ref, rig_ref, *rest):
    o_ref = rest[-1]
    at = 0
    for ref in (top_ref, bot_ref, lef_ref, rig_ref):
        n = ref.shape[1]
        o_ref[:, at : at + n, :] = ref[...]
        at += n


def solution(mesh):
    shape = mesh.devices.shape
    mesh = jax.sharding.Mesh(
        mesh.devices.reshape((shape[0] // 2, 2) + shape[1:]), HA + tuple(mesh.axis_names[1:])
    )
    block = P(None, HA, "wa", "col")
    weight = P(None, "col", None)
    return jax.shard_map(
        on_device,
        mesh=mesh,
        in_specs=(block, block, block, weight, weight, weight),
        out_specs=block,
        check_vma=False,
    )
```

```python
import functools

import jax
import jax.numpy as jnp
from jax import lax
from jax.experimental import pallas as pl
from jax.experimental.pallas import tpu as pltpu
from jax.sharding import PartitionSpec as P

F32 = jnp.float32
BF16 = jnp.bfloat16
CH = 128
GROUP = 16
ROWS = 8
COLS = 32
BLOCK = 4 * ROWS * COLS * GROUP
MIB = 1 << 20
CORNERS = ((0, 0), (0, 1), (1, 0), (1, 1))

VMEM = pl.BlockSpec(memory_space=pltpu.VMEM)
SMEM = pl.BlockSpec(memory_space=pltpu.SMEM)
ANY = pl.BlockSpec(memory_space=pl.ANY)
HBM = pl.BlockSpec(memory_space=pltpu.HBM)
HA = ("z", "core")


class Left:
    def __init__(self, array, spec=ANY):
        self.array, self.spec = array, spec
        if spec is HBM:
            self.array = pltpu.with_memory_space_constraint(array, pltpu.HBM)


def call(body, outs, scratch=(), flops=0, limit=8, name=None):
    def run(*args):
        specs = [a.spec if isinstance(a, Left) else SMEM if a.dtype == jnp.int32 else VMEM for a in args]
        args = [a.array if isinstance(a, Left) else a for a in args]
        nbytes = sum(a.size * a.dtype.itemsize for a in args + list(outs))
        return pl.pallas_call(
            body,
            out_shape=list(outs),
            in_specs=specs,
            out_specs=[VMEM] * len(outs),
            scratch_shapes=list(scratch),
            compiler_params=pltpu.CompilerParams(vmem_limit_bytes=limit * MIB),
            cost_estimate=pl.CostEstimate(flops=flops, bytes_accessed=nbytes, transcendentals=0),
            name=name,
        )(*args)

    return run


def sds(shape, dtype=BF16):
    return jax.ShapeDtypeStruct(shape, dtype)


def group_sum(row):
    lane = lax.broadcasted_iota(jnp.int32, row.shape, 1)
    shift = 1
    while shift < GROUP:
        other = jnp.where((lane & shift) != 0, pltpu.roll(row, shift, 1), pltpu.roll(row, CH - shift, 1))
        row = row + other
        shift *= 2
    return row


def local_stats(flat):
    count = flat.shape[0] * GROUP
    mean = group_sum(jnp.sum(flat, axis=0, keepdims=True)) * (1.0 / count)
    dev = flat - mean
    m2 = group_sum(jnp.sum(dev * dev, axis=0, keepdims=True))
    return mean, m2


def merge(st_ref, count):
    means = st_ref[:, 0, :]
    mean = jnp.sum(means, axis=0, keepdims=True) * (1.0 / st_ref.shape[0])
    apart = means - mean
    return mean, jnp.sum(st_ref[:, 1, :] + count * (apart * apart), axis=0, keepdims=True)


def store_stats(ref, mean, m2):
    row = lax.broadcasted_iota(jnp.int32, ref.shape[1:], 0)
    ref[...] = jnp.broadcast_to(jnp.where(row == 0, mean, jnp.where(row == 1, m2, 0.0))[None], ref.shape)


def mix_body(count, flag_ref, st_ref, top_ref, bot_ref, *rest):
    o_ref = rest[-1]
    store_stats(o_ref, *merge(st_ref, count))
    n = top_ref.shape[0]
    for c in range(2):

        @pl.when(flag_ref[2 + c] > 0)
        def _():
            peer = flag_ref[5] + 2 * c - 1
            for i, ref in enumerate((top_ref, bot_ref)):
                pixels = ref[...].astype(F32)[:, c * (COLS - 1), :]
                o_ref[pl.ds(peer, 1), 2 + i * n : 2 + (i + 1) * n, :] = pixels[None]


def spread(flags, stats, rows, after):
    stats = lax.all_to_all(stats, HA, 0, 0, tiled=True)
    n = rows[0].shape[0]
    slots = sds((lax.axis_size("wa"), (2 + 2 * n + 7) // 8 * 8, CH), F32)
    (slots,) = call(functools.partial(mix_body, BLOCK), [slots], name="mix")(
        flags, stats, *rows, *[Left(a) for a in after]
    )
    return lax.all_to_all(slots, "wa", 0, 0, tiled=True)


def corner_pixels(flag_ref, ref, frames, frame):
    found = []
    for r, c in CORNERS:
        inside = flag_ref[2 + c]
        source = flag_ref[5] + inside * (2 * c - 1)
        found.append((inside * flag_ref[r], ref[pl.ds(source, 1), 2 + r * frames + frame, :]))
    return found


def store_edges(frames, refs, pad=0):
    top_ref, bot_ref, lef_ref, rig_ref = refs
    at = 0
    for v in frames:
        n = v.shape[0]
        top_ref[at : at + n] = v[:, 0].astype(BF16)
        bot_ref[at : at + n] = v[:, ROWS - 1].astype(BF16)
        for ref, column in ((lef_ref, v[:, :, 0, :]), (rig_ref, v[:, :, COLS - 1, :])):
            if pad:
                column = jnp.concatenate([column, jnp.zeros((n, pad, CH), F32)], axis=1)
            ref[at : at + n] = column.astype(BF16)
        at += n


def first_body(flag_ref, x_hbm, c1_hbm, c2_hbm, w_hbm, x_ref, c1_ref, c2_ref, slot_ref, *rest):
    edges, pieces, sem = rest[:4], rest[4:8], rest[8]
    pairs = [(x_hbm, x_ref), (c1_hbm, c1_ref), (c2_hbm, c2_ref)]
    for k, piece in enumerate(pieces):
        block = pl.multiple_of(lax.rem(flag_ref[4] + k, 4) * CH, CH)
        pairs.append((w_hbm.at[:, :, pl.ds(block, CH)], piece))
    copies = [pltpu.make_async_copy(src, dst, sem.at[i]) for i, (src, dst) in enumerate(pairs)]
    for c in copies:
        c.start()
    for c in copies[:3]:
        c.wait()
    x, c1, c2 = x_ref[...].astype(F32), c1_ref[...].astype(F32), c2_ref[...].astype(F32)
    mean, m2 = local_stats(x.reshape(-1, CH))
    store_stats(slot_ref, mean, m2)
    store_edges((c1, x, c2), edges)
    for c in copies[3:]:
        c.wait()


def corner_body(top_ref, bot_ref, lef_ref, rig_ref, *rest):
    lo_ref, ro_ref = rest[-2:]
    row = lax.broadcasted_iota(jnp.int32, lef_ref.shape, 1)
    top = top_ref[...].astype(F32)
    bot = bot_ref[...].astype(F32)
    for src, dst, at in ((lef_ref, lo_ref, 0), (rig_ref, ro_ref, COLS - 1)):
        v = src[...].astype(F32)
        v = jnp.where(row == 8, top[:, at : at + 1, :], v)
        v = jnp.where(row == 9, bot[:, at : at + 1, :], v)
        dst[...] = v.astype(BF16)


def swap_rows(top, bot):
    n = lax.axis_size(HA)
    above = lax.ppermute(bot, HA, [(i, i + 1) for i in range(n - 1)])
    below = lax.ppermute(top, HA, [(i + 1, i) for i in range(n - 1)])
    return above, below


def swap_columns(lef, rig):
    n = lax.axis_size("wa")
    left = lax.ppermute(rig, "wa", [(i, i + 1) for i in range(n - 1)])
    right = lax.ppermute(lef, "wa", [(i + 1, i) for i in range(n - 1)])
    return left, right


def shifted(rows, left, right):
    n = rows.shape[0]
    flat = rows.reshape(n * COLS, CH)
    col = lax.broadcasted_iota(jnp.int32, rows.shape, 1)
    before = pltpu.roll(flat, 1, 0).reshape(rows.shape)
    after = pltpu.roll(flat, n * COLS - 1, 0).reshape(rows.shape)
    before = jnp.where(col == 0, left[:, None, :], before)
    after = jnp.where(col == COLS - 1, right[:, None, :], after)
    return before, after


def place(patch_ref, frame, rows, at, left, right, lanes):
    n = rows.shape[0]
    before, after = shifted(rows, left, right)
    for e, v in enumerate((before, rows, after)):
        patch_ref[frame, at * COLS : (at + n) * COLS, lanes[e] : lanes[e] + CH] = v.reshape(n * COLS, CH).astype(BF16)


def place_frame(patch_ref, frame, inner, top, bot, lef, rig, corners, lanes):
    place(patch_ref, frame, inner, 1, lef, rig, lanes)
    place(patch_ref, frame, top[None], 0, corners[0], corners[1], lanes)
    place(patch_ref, frame, bot[None], ROWS + 1, corners[2], corners[3], lanes)


def multiply(patch_ref, w_ref, outs):
    depth = 9 * CH
    size = ROWS * COLS
    for t in range(4):
        acc = None
        for a in range(3):
            lhs = jnp.concatenate([patch_ref[t + a, b * COLS : b * COLS + size, :] for b in range(3)], axis=1)
            part = jnp.dot(lhs, w_ref[a * depth : (a + 1) * depth, :], preferred_element_type=F32)
            acc = part if acc is None else acc + part
        for i, out in enumerate(outs):
            out[t * size : (t + 1) * size, :] = acc[:, i * CH : (i + 1) * CH].astype(BF16)


def far_body(
    cache_at, act_at, extra, flag_ref, x_ref, c_ref, tc, bc, lc, rc, pc, ta, ba, la, ra, st_ref, w_hbm, *rest
):
    out2, out1, patch_ref, near_ref, w_ref, sem = rest[extra:]
    col = flag_ref[4]
    copies = []
    for i, (k, dst, at) in enumerate(((2, w_ref, 0), (1, w_ref, CH), (3, near_ref, 0), (0, near_ref, CH))):
        block = pl.multiple_of(lax.rem(col + k, 4) * CH, CH)
        copies.append(
            pltpu.make_async_copy(w_hbm.at[:, pl.ds(block, CH)], dst.at[:, at : at + CH], sem.at[i])
        )
        copies[-1].start()
    has = [flag_ref[i] > 0 for i in range(4)]
    count = BLOCK * lax.axis_size(HA)
    mean, m2 = merge(st_ref, count)
    scale = lax.rsqrt(m2 * (1.0 / (count * st_ref.shape[0])) + 1e-6)

    def act(v):
        u = (v - mean) * scale
        return u / (1.0 + jnp.exp(-u))

    lanes = (0, CH, 2 * CH)
    for s in range(6):
        if s < 2:
            own, at, halo, pixels, change = c_ref[s], cache_at + s, (tc, bc, lc, rc), pc, lambda v: v
        else:
            own, at, halo, pixels, change = x_ref[s - 2], act_at + s - 2, (ta, ba, la, ra), st_ref, act
        sides = [jnp.where(has[i], change(ref[at].astype(F32)), 0.0) for i, ref in enumerate(halo)]
        corners = [
            jnp.where(inside > 0, change(v), 0.0)
            for inside, v in corner_pixels(flag_ref, pixels, halo[0].shape[0], at)
        ]
        place_frame(patch_ref, s, change(own.astype(F32)), *sides, corners, lanes)
    copies[0].wait()
    copies[1].wait()
    multiply(patch_ref, w_ref, (out2, out1))
    copies[2].wait()
    copies[3].wait()


def near_body(patch_ref, w_ref, out3, out0):
    multiply(patch_ref, w_ref, (out3, out0))


def conv(flags, x, cache, cache_halo, cache_at, act_halo, act_at, weight, name, after=()):
    n = x.shape[0] * ROWS * COLS
    depth, width = weight.shape
    flops = n * depth * width
    piece = sds((n, CH))
    body = functools.partial(far_body, cache_at, act_at, len(after))
    out2, out1, patch, near = call(
        body,
        [piece] * 2 + [sds((6, (ROWS + 2) * COLS, 3 * CH)), sds((depth, 2 * CH))],
        scratch=[pltpu.VMEM((depth, 2 * CH), BF16), pltpu.SemaphoreType.DMA((4,))],
        flops=flops,
        limit=20,
        name=name + "_far",
    )(flags, x, cache, *cache_halo, *act_halo, Left(weight, HBM), *[Left(a) for a in after])
    got2 = to_peer(out2, 2)
    got1 = to_peer(out1, 1)
    out3, own = call(near_body, [piece] * 2, flops=flops, limit=16, name=name + "_near")(patch, near)
    (far,) = call(add_body, [sds((n, CH), F32)], name=name + "_add")(got1, got2)
    return own, far, to_peer(out3, 3)


def add_body(a_ref, b_ref, o_ref):
    o_ref[...] = a_ref[...].astype(F32) + b_ref[...].astype(F32)


def to_peer(piece, k):
    n = lax.axis_size("col")
    return lax.ppermute(piece, "col", [(i, (i + k) % n) for i in range(n)])


def to_peers(pieces):
    got = {k: to_peer(pieces[k - 1], k) for k in (2, 1, 3)}
    return [got[k] for k in (1, 2, 3)]


def hidden_body(p0, far, p3, h_ref, slot_ref, *edges):
    h = (p0[...].astype(F32) + p3[...].astype(F32) + far[...]).astype(BF16)
    h_ref[...] = h.reshape(h_ref.shape)
    h = h.astype(F32)
    mean, m2 = local_stats(h)
    store_stats(slot_ref, mean, m2)
    store_edges((h.reshape(h_ref.shape),), edges)


def resid_body(x_ref, p0, far, p3, h_ref, *edges):
    total = p0[...].astype(F32) + p3[...].astype(F32) + far[...]
    h = (x_ref[...].astype(F32) + total.reshape(x_ref.shape)).astype(BF16)
    h_ref[...] = h
    store_edges((h.astype(F32),), edges, pad=8)


ROW_TAPS = {(0, 0): (-1, 0), (0, 1): (1,), (1, 0): (-1,), (1, 1): (0, 1)}
COL_TAPS = {(0, 0): (-1,), (0, 1): (0, 1), (1, 0): (-1, 0), (1, 1): (1,)}


def fold_body(w0, w1, w2, w3, o_ref):
    for k, ref in enumerate((w0, w1, w2, w3)):
        taps = [ref[i].astype(F32) for i in range(9)]
        for q in range(2):
            for r in range(2):
                for s in range(2):
                    for p in range(2):
                        total = None
                        for b in ROW_TAPS[p, r]:
                            for e in COL_TAPS[q, s]:
                                tap = taps[(b + 1) * 3 + (e + 1)]
                                total = tap if total is None else total + tap
                        at = (s * 4 + k) * CH
                        o_ref[q, r, at : at + CH, p * CH : (p + 1) * CH] = total.astype(BF16)


def up_body(*refs):
    parts = [refs[2 * k : 2 * k + 2] for k in range(4)]
    w_ref, o_ref, patch_ref, mix_ref = refs[8:12]
    size = (ROWS + 1) * COLS
    half = 2 * 4 * CH
    for k, (x, border) in enumerate(parts):
        edge = border[0].astype(F32)
        place_frame(
            patch_ref,
            0,
            x[0].astype(F32),
            edge[:COLS],
            edge[COLS : 2 * COLS],
            edge[2 * COLS : 2 * COLS + 8],
            edge[2 * COLS + 16 : 2 * COLS + 24],
            [edge[2 * COLS + i : 2 * COLS + i + 1] for i in (8, 24, 9, 25)],
            [(e * 4 + k) * CH for e in range(3)],
        )
    for q in range(2):
        acc = None
        for r in range(2):
            lhs = patch_ref[0, r * COLS : r * COLS + size, q * 4 * CH : q * 4 * CH + half]
            part = jnp.dot(lhs, w_ref[q, r], preferred_element_type=F32)
            acc = part if acc is None else acc + part
        for n in range(ROWS + 1):
            for p in range(2):
                i = 2 * n - 1 + p
                if 0 <= i < 2 * ROWS:
                    mix_ref[i, pl.ds(q, COLS, stride=2), :] = acc[n * COLS : (n + 1) * COLS, p * CH : (p + 1) * CH]
    o_ref[0] = mix_ref[...].astype(BF16)


def up_conv(parts, weight):
    specs = []
    args = []
    for part in parts:
        for a in part:
            rest = a.shape[1:]
            specs.append(pl.BlockSpec((1,) + rest, lambda t, n=len(rest): (t,) + (0,) * n))
            args.append(a)
    specs.append(pl.BlockSpec(weight.shape, lambda t: (0, 0, 0, 0)))
    frames = parts[0][0].shape[0]
    out = (frames, 2 * ROWS, 2 * COLS, CH)
    return pl.pallas_call(
        up_body,
        out_shape=sds(out),
        grid=(frames,),
        in_specs=specs,
        out_specs=pl.BlockSpec((1,) + out[1:], lambda t: (t, 0, 0, 0)),
        scratch_shapes=[
            pltpu.VMEM((1, (ROWS + 2) * COLS, 12 * CH), BF16),
            pltpu.VMEM((2 * ROWS, 2 * COLS, CH), F32),
        ],
        compiler_params=pltpu.CompilerParams(vmem_limit_bytes=24 * MIB),
        name="up_conv",
    )(*args, weight)


def on_device(features, cache_first, cache_second, weight_first, weight_second, weight_up):
    frames = features.shape[0]
    ha, wa, col = lax.axis_index(HA), lax.axis_index("wa"), lax.axis_index("col")
    nh, nw = lax.axis_size(HA), lax.axis_size("wa")
    flags = jnp.stack([ha > 0, ha < nh - 1, wa > 0, wa < nw - 1, col, wa]).astype(jnp.int32)
    slots = sds((nh, 2, CH), F32)

    x, c1, c2, stats, *edges = call(
        first_body,
        [sds(features.shape), sds(cache_first.shape), sds(cache_second.shape), slots]
        + [sds((8, COLS, CH))] * 2
        + [sds((8, ROWS, CH))] * 2
        + [sds(weight_up.shape[:2] + (CH,))] * 4,
        scratch=[pltpu.SemaphoreType.DMA((7,))],
        limit=20,
        name="first",
    )(flags, *[Left(a, HBM) for a in (features, cache_first, cache_second, weight_up)])
    edges, w_pieces = edges[:4], edges[4:]
    w_got = to_peers(w_pieces[1:])
    rows = swap_rows(*edges[:2])
    columns = swap_columns(*edges[2:])
    halo = rows + columns + (spread(flags, stats, rows, ()),)
    pieces = conv(flags, x, c1, halo, 0, halo, 2, weight_first.reshape(-1, 4 * CH), "conv_first", after=w_got)
    hidden, stats, *edges = call(
        hidden_body,
        [sds(features.shape), slots] + [sds((frames, COLS, CH))] * 2 + [sds((frames, ROWS, CH))] * 2,
        limit=12,
        name="hidden",
    )(*pieces)
    rows = swap_rows(*edges[:2])
    columns = swap_columns(*edges[2:])
    halo2 = rows + columns + (spread(flags, stats, rows, columns),)
    (folded,) = call(fold_body, [sds((2, 2, 8 * CH, 2 * CH))], limit=12, name="fold")(w_pieces[0], *w_got)
    pieces = conv(flags, hidden, c2, halo, 6, halo2, 0, weight_second.reshape(-1, 4 * CH), "conv_second")
    resid, *edges = call(
        resid_body,
        [sds(features.shape)] + [sds((frames, COLS, CH))] * 2 + [sds((frames, 16, CH))] * 2,
        name="resid",
    )(features, *pieces)
    others = to_peers([resid] * 3)
    rows = swap_rows(*edges[:2])
    cornered = call(corner_body, [sds((frames, 16, CH))] * 2, name="corners")(*rows, *edges[2:], Left(others[0]))
    columns = swap_columns(*cornered)
    (border,) = call(pack_body, [sds((frames, 2 * COLS + 32, CH))], name="pack")(
        *rows, *columns, *[Left(a) for a in others[1:]]
    )
    borders = [border] + to_peers([border] * 3)
    return up_conv(list(zip([resid] + others, borders)), folded)


def pack_body(top_ref, bot_ref, lef_ref, rig_ref, *rest):
    o_ref = rest[-1]
    at = 0
    for ref in (top_ref, bot_ref, lef_ref, rig_ref):
        n = ref.shape[1]
        o_ref[:, at : at + n, :] = ref[...]
        at += n


def solution(mesh):
    shape = mesh.devices.shape
    mesh = jax.sharding.Mesh(
        mesh.devices.reshape((shape[0] // 2, 2) + shape[1:]), HA + tuple(mesh.axis_names[1:])
    )
    block = P(None, HA, "wa", "col")
    weight = P(None, "col", None)
    return jax.shard_map(
        on_device,
        mesh=mesh,
        in_specs=(block, block, block, weight, weight, weight),
        out_specs=block,
        check_vma=False,
    )
```

```python
import functools

import jax
import jax.numpy as jnp
from jax import lax
from jax.experimental import pallas as pl
from jax.experimental.pallas import tpu as pltpu
from jax.sharding import PartitionSpec as P

F32 = jnp.float32
BF16 = jnp.bfloat16
CH = 128
GROUP = 16
ROWS = 8
COLS = 32
WIDE = 3
BLOCK = 4 * ROWS * COLS * GROUP
MIB = 1 << 20

VMEM = pl.BlockSpec(memory_space=pltpu.VMEM)
SMEM = pl.BlockSpec(memory_space=pltpu.SMEM)
ANY = pl.BlockSpec(memory_space=pl.ANY)
HBM = pl.BlockSpec(memory_space=pltpu.HBM)
HA = ("z", "core")


class Left:
    def __init__(self, array, spec=ANY):
        self.array, self.spec = array, spec
        if spec is HBM:
            self.array = pltpu.with_memory_space_constraint(array, pltpu.HBM)


def call(body, outs, scratch=(), flops=0, limit=8, name=None):
    def run(*args):
        specs = [a.spec if isinstance(a, Left) else SMEM if a.dtype == jnp.int32 else VMEM for a in args]
        args = [a.array if isinstance(a, Left) else a for a in args]
        nbytes = sum(a.size * a.dtype.itemsize for a in args + list(outs))
        return pl.pallas_call(
            body,
            out_shape=list(outs),
            in_specs=specs,
            out_specs=[VMEM] * len(outs),
            scratch_shapes=list(scratch),
            compiler_params=pltpu.CompilerParams(vmem_limit_bytes=limit * MIB),
            cost_estimate=pl.CostEstimate(flops=flops, bytes_accessed=nbytes, transcendentals=0),
            name=name,
        )(*args)

    return run


def sds(shape, dtype=BF16):
    return jax.ShapeDtypeStruct(shape, dtype)


def group_sum(row):
    lane = lax.broadcasted_iota(jnp.int32, row.shape, 1)
    shift = 1
    while shift < GROUP:
        other = jnp.where((lane & shift) != 0, pltpu.roll(row, shift, 1), pltpu.roll(row, CH - shift, 1))
        row = row + other
        shift *= 2
    return row


def local_stats(flat):
    count = flat.shape[0] * GROUP
    mean = group_sum(jnp.sum(flat, axis=0, keepdims=True)) * (1.0 / count)
    dev = flat - mean
    m2 = group_sum(jnp.sum(dev * dev, axis=0, keepdims=True))
    return mean, m2


def merge(st_ref, count):
    means = st_ref[:, 0, :]
    mean = jnp.sum(means, axis=0, keepdims=True) * (1.0 / st_ref.shape[0])
    apart = means - mean
    m2 = jnp.sum(st_ref[:, 1, :] + count * (apart * apart), axis=0, keepdims=True)
    return mean, lax.rsqrt(m2 * (1.0 / (count * st_ref.shape[0])) + 1e-6)


def store_stats(ref, mean, m2):
    row = lax.broadcasted_iota(jnp.int32, (2, CH), 0)
    ref[...] = jnp.broadcast_to(jnp.where(row == 0, mean, m2)[None], ref.shape)


def spread(slots):
    return lax.all_to_all(slots, HA + ("wa",), 0, 0, tiled=True)


def store_edges(frames, refs):
    top_ref, bot_ref, lef_ref, rig_ref = refs
    at = 0
    for v in frames:
        n = v.shape[0]
        top_ref[at : at + n] = v[:, 0].astype(BF16)
        bot_ref[at : at + n] = v[:, ROWS - 1].astype(BF16)
        for i in range(WIDE):
            for ref, j in ((lef_ref, i), (rig_ref, COLS - WIDE + i)):
                column = jnp.concatenate([v[:, :, j, :], jnp.zeros((n, 8, CH), F32)], axis=1)
                ref[at : at + n, i] = column.astype(BF16)
        at += n


def first_body(flag_ref, x_hbm, c1_hbm, c2_hbm, w_hbm, x_ref, c1_ref, c2_ref, slot_ref, *rest):
    edges, pieces, sem = rest[:4], rest[4:8], rest[8]
    pairs = [(x_hbm, x_ref), (c1_hbm, c1_ref), (c2_hbm, c2_ref)]
    for k, piece in enumerate(pieces):
        block = pl.multiple_of(lax.rem(flag_ref[4] + k, 4) * CH, CH)
        pairs.append((w_hbm.at[:, :, pl.ds(block, CH)], piece))
    copies = [pltpu.make_async_copy(src, dst, sem.at[i]) for i, (src, dst) in enumerate(pairs)]
    for c in copies:
        c.start()
    for c in copies[:3]:
        c.wait()
    x, c1, c2 = x_ref[...].astype(F32), c1_ref[...].astype(F32), c2_ref[...].astype(F32)
    mean, m2 = local_stats(x.reshape(-1, CH))
    store_stats(slot_ref, mean, m2)
    store_edges((c1, x, c2), edges)
    for c in copies[3:]:
        c.wait()


def corner_body(top_ref, bot_ref, lef_ref, rig_ref, lo_ref, ro_ref):
    top = top_ref[...].astype(F32)
    bot = bot_ref[...].astype(F32)
    shape = (lef_ref.shape[0],) + lef_ref.shape[2:]
    row = lax.broadcasted_iota(jnp.int32, shape, 1)
    for i in range(WIDE):
        for src, dst, at in ((lef_ref, lo_ref, i), (rig_ref, ro_ref, COLS - WIDE + i)):
            v = src[:, i].astype(F32)
            v = jnp.where(row == 8, top[:, at : at + 1, :], v)
            v = jnp.where(row == 9, bot[:, at : at + 1, :], v)
            dst[:, i] = v.astype(BF16)


def swap_rows(top, bot):
    n = lax.axis_size(HA)
    above = lax.ppermute(bot, HA, [(i, i + 1) for i in range(n - 1)])
    below = lax.ppermute(top, HA, [(i + 1, i) for i in range(n - 1)])
    return above, below


def swap_columns(lef, rig):
    n = lax.axis_size("wa")
    left = lax.ppermute(rig, "wa", [(i, i + 1) for i in range(n - 1)])
    right = lax.ppermute(lef, "wa", [(i + 1, i) for i in range(n - 1)])
    return left, right


def shifted(rows, left, right):
    n = rows.shape[0]
    flat = rows.reshape(n * COLS, CH)
    col = lax.broadcasted_iota(jnp.int32, rows.shape, 1)
    before = pltpu.roll(flat, 1, 0).reshape(rows.shape)
    after = pltpu.roll(flat, n * COLS - 1, 0).reshape(rows.shape)
    before = jnp.where(col == 0, left[:, None, :], before)
    after = jnp.where(col == COLS - 1, right[:, None, :], after)
    return before, after


def place(patch_ref, frame, rows, at, left, right, lanes):
    n = rows.shape[0]
    before, after = shifted(rows, left, right)
    for e, v in enumerate((before, rows, after)):
        patch_ref[frame, at * COLS : (at + n) * COLS, lanes[e] : lanes[e] + CH] = v.reshape(n * COLS, CH).astype(BF16)


def place_frame(patch_ref, frame, inner, top, bot, lef, rig, corners, lanes):
    place(patch_ref, frame, inner, 1, lef, rig, lanes)
    place(patch_ref, frame, top[None], 0, corners[0], corners[1], lanes)
    place(patch_ref, frame, bot[None], ROWS + 1, corners[2], corners[3], lanes)


def multiply(patch_ref, side_ref, w_ref, outs):
    depth = 9 * CH
    size = ROWS * COLS
    slot = side_ref.shape[1] // (ROWS + 2)
    jobs = [(t * size, size, [(patch_ref, t + a, COLS) for a in range(3)]) for t in range(4)]
    jobs.append((4 * size, ROWS * slot, [(side_ref, a, slot) for a in range(3)]))
    for at, rows, sources in jobs:
        acc = None
        for a, (ref, i, step) in enumerate(sources):
            lhs = jnp.concatenate([ref[i, b * step : b * step + rows, :] for b in range(3)], axis=1)
            part = jnp.dot(lhs, w_ref[a * depth : (a + 1) * depth, :], preferred_element_type=F32)
            acc = part if acc is None else acc + part
        for i, out in enumerate(outs):
            out[at : at + rows, :] = acc[:, i * CH : (i + 1) * CH].astype(BF16)


def halo_frame(refs, at, change, has, reach):
    top, bot, lef, rig = refs
    above = jnp.where(has[0], change(top[at].astype(F32)), 0.0)
    below = jnp.where(has[1], change(bot[at].astype(F32)), 0.0)
    columns = {}
    for i in range(reach):
        for ref, flag, j, x in ((lef, has[2], WIDE - 1 - i, -1 - i), (rig, has[3], i, COLS + i)):
            v = jnp.where(flag, change(ref[at, j].astype(F32)), 0.0)
            columns[x] = (v[0:8], jnp.where(has[0], v[8:9], 0.0), jnp.where(has[1], v[9:10], 0.0))
    return above, below, columns


def place_sides(mix_ref, frame, ext, inner, above, below, columns):
    columns = dict(columns)
    for x in (0, COLS - 1):
        columns[x] = (inner[:, x, :], above[x : x + 1], below[x : x + 1])
    step = 8 * ext
    for a in range(3):
        t = frame - a
        if not 0 <= t < 4:
            continue
        for c, x in enumerate(list(range(-ext, 0)) + list(range(COLS, COLS + ext))):
            w = t * 2 * ext + c
            for e in range(3):
                rows, up, down = columns[x + e - 1]
                mix_ref[a, e, pl.ds(w, 1), :] = up
                mix_ref[a, e, pl.ds(step + w, ROWS, stride=step), :] = rows
                mix_ref[a, e, pl.ds((ROWS + 1) * step + w, 1), :] = down


def far_body(ext, cache_at, act_at, extra, flag_ref, x_ref, c_ref, st_ref, *rest):
    halo, rest = rest[:4], rest[4:]
    if act_at is None:
        beside_ref, above_ref, below_ref = rest[:3]
        rest = rest[3:]
    w_hbm, rest = rest[0], rest[1 + extra :]
    out2, out1, patch_ref, side_ref, near_ref, w_ref, mix_ref, wide_ref, sem = rest
    col = flag_ref[4]
    copies = []
    for i, (k, dst, at) in enumerate(((2, w_ref, 0), (1, w_ref, CH), (3, near_ref, 0), (0, near_ref, CH))):
        block = pl.multiple_of(lax.rem(col + k, 4) * CH, CH)
        copies.append(
            pltpu.make_async_copy(w_hbm.at[:, pl.ds(block, CH)], dst.at[:, at : at + CH], sem.at[i])
        )
        copies[-1].start()
    has = [flag_ref[i] > 0 for i in range(4)]
    mean, scale = merge(st_ref, BLOCK)

    def act(v):
        u = (v - mean) * scale
        return u / (1.0 + jnp.exp(-u))

    if act_at is None:
        wide_ref[...] = act(beside_ref[...])
        outer = [
            jnp.where(flag, act(ref[...].astype(F32)), 0.0) for ref, flag in ((above_ref, has[0]), (below_ref, has[1]))
        ]
    for s in range(6):
        if s < 2:
            inner = c_ref[s].astype(F32)
            above, below, columns = halo_frame(halo, cache_at + s, lambda v: v, has, ext + 1)
        else:
            t = s - 2
            inner = act(x_ref[t].astype(F32))
            if act_at is not None:
                above, below, columns = halo_frame(halo, act_at + t, act, has, ext + 1)
            else:
                above, below = [v[t * COLS : (t + 1) * COLS] for v in outer]
                columns = {}
                for c, x in enumerate((-2, -1, COLS, COLS + 1)):
                    flag = has[2 + c // 2]
                    px = 4 * COLS + 4 * t + c
                    rows = wide_ref[pl.ds(4 * t + c, ROWS, stride=16), :]
                    columns[x] = tuple(
                        jnp.where(flag, v, 0.0) for v in (rows, outer[0][px : px + 1], outer[1][px : px + 1])
                    )
        corners = [columns[-1][1], columns[COLS][1], columns[-1][2], columns[COLS][2]]
        place_frame(
            patch_ref, s, inner, above, below, columns[-1][0], columns[COLS][0], corners, (0, CH, 2 * CH)
        )
        place_sides(mix_ref, s, ext, inner, above, below, columns)
    for a in range(3):
        for e in range(3):
            side_ref[a, :, e * CH : (e + 1) * CH] = mix_ref[a, e].astype(BF16)
    copies[0].wait()
    copies[1].wait()
    multiply(patch_ref, side_ref, w_ref, (out2, out1))
    copies[2].wait()
    copies[3].wait()


def near_body(patch_ref, side_ref, w_ref, out3, out0):
    multiply(patch_ref, side_ref, w_ref, (out3, out0))


def conv(flags, x, cache, stats, halo, cache_at, act_at, around, weight, ext, name, after=()):
    n = x.shape[0] * ROWS * COLS + ROWS * 8 * ext
    depth, width = weight.shape
    flops = n * depth * width
    piece = sds((n, CH))
    body = functools.partial(far_body, ext, cache_at, act_at, len(after))
    out2, out1, patch, side, near = call(
        body,
        [piece] * 2
        + [
            sds((6, (ROWS + 2) * COLS, 3 * CH)),
            sds((3, (ROWS + 2) * 8 * ext, 3 * CH)),
            sds((depth, 2 * CH)),
        ],
        scratch=[
            pltpu.VMEM((depth, 2 * CH), BF16),
            pltpu.VMEM((3, 3, (ROWS + 2) * 8 * ext, CH), F32),
            pltpu.VMEM((16 * ROWS, CH), F32),
            pltpu.SemaphoreType.DMA((4,)),
        ],
        flops=flops,
        limit=20,
        name=name + "_far",
    )(flags, x, cache, stats, *halo, *around, Left(weight, HBM), *[Left(a) for a in after])
    got2 = to_peer(out2, 2)
    got1 = to_peer(out1, 1)
    out3, own = call(near_body, [piece] * 2, flops=flops, limit=16, name=name + "_near")(patch, side, near)
    (far,) = call(add_body, [sds((n, CH), F32)], name=name + "_add")(got1, got2)
    return own, far, to_peer(out3, 3)


def add_body(a_ref, b_ref, o_ref):
    o_ref[...] = a_ref[...].astype(F32) + b_ref[...].astype(F32)


def to_peer(piece, k):
    n = lax.axis_size("col")
    return lax.ppermute(piece, "col", [(i, (i + k) % n) for i in range(n)])


def to_peers(pieces):
    got = {k: to_peer(pieces[k - 1], k) for k in (2, 1, 3)}
    return [got[k] for k in (1, 2, 3)]


def hidden_body(p0, far, p3, h_ref, side_ref, slot_ref, top_ref, bot_ref):
    h = (p0[...].astype(F32) + p3[...].astype(F32) + far[...]).astype(BF16).astype(F32)
    size = 4 * ROWS * COLS
    mean, m2 = local_stats(h[:size])
    store_stats(slot_ref, mean, m2)
    main = h[:size].reshape(h_ref.shape)
    h_ref[...] = main.astype(BF16)
    side_ref[...] = h[size:]
    for ref, r in ((top_ref, 0), (bot_ref, ROWS - 1)):
        ref[0 : 4 * COLS, :] = main[:, r].reshape(4 * COLS, CH).astype(BF16)
        ref[4 * COLS :, :] = h[size + 16 * r : size + 16 * (r + 1)].astype(BF16)


def resid_body(flag_ref, x_ref, lef_ref, rig_ref, p0, far, p3, o_ref, top_ref, bot_ref, side_ref):
    total = p0[...].astype(F32) + p3[...].astype(F32) + far[...]
    size = ROWS * COLS
    side_ref[...] = total[4 * size :]
    row = lax.broadcasted_iota(jnp.int32, (8, CH), 0)
    for t in range(4):
        main = x_ref[t].astype(F32).reshape(size, CH) + total[t * size : (t + 1) * size]
        o_ref[t, 0:size, :] = main.astype(BF16)
        beside = []
        for c, (ref, i) in enumerate(((lef_ref, WIDE - 1), (rig_ref, 0))):
            v = ref[2 + t, i].astype(F32)[0:ROWS] + side_ref[pl.ds(2 * t + c, ROWS, stride=8), :]
            beside.append(jnp.where(flag_ref[2 + c] > 0, v, 0.0))
            o_ref[t, size + 8 * c : size + 8 * (c + 1), :] = beside[c].astype(BF16)
        for ref, r in ((top_ref, 0), (bot_ref, ROWS - 1)):
            ref[t, 0:COLS, :] = main[r * COLS : (r + 1) * COLS].astype(BF16)
            px = [v[r : r + 1] for v in beside]
            ref[t, COLS:, :] = jnp.where(row == 0, px[0], jnp.where(row == 1, px[1], 0.0)).astype(BF16)


ROW_TAPS = {(0, 0): (-1, 0), (0, 1): (1,), (1, 0): (-1,), (1, 1): (0, 1)}
COL_TAPS = {(0, 0): (-1,), (0, 1): (0, 1), (1, 0): (-1, 0), (1, 1): (1,)}


def fold_body(w0, w1, w2, w3, *rest):
    o_ref = rest[-1]
    for k, ref in enumerate((w0, w1, w2, w3)):
        taps = [ref[i].astype(F32) for i in range(9)]
        for q in range(2):
            for r in range(2):
                for s in range(2):
                    for p in range(2):
                        total = None
                        for b in ROW_TAPS[p, r]:
                            for e in COL_TAPS[q, s]:
                                tap = taps[(b + 1) * 3 + (e + 1)]
                                total = tap if total is None else total + tap
                        at = (s * 4 + k) * CH
                        o_ref[q, r, at : at + CH, p * CH : (p + 1) * CH] = total.astype(BF16)


def up_body(*refs):
    parts = [refs[2 * k : 2 * k + 2] for k in range(4)]
    w_ref, o_ref, patch_ref, mix_ref = refs[8:12]
    size = (ROWS + 1) * COLS
    half = 2 * 4 * CH
    for k, (x, border) in enumerate(parts):
        edge = border[0].astype(F32)
        own = x[0].astype(F32)
        inside = ROWS * COLS
        place_frame(
            patch_ref,
            0,
            own[:inside].reshape(ROWS, COLS, CH),
            edge[:COLS],
            edge[COLS + 8 : 2 * COLS + 8],
            own[inside : inside + 8],
            own[inside + 8 :],
            [edge[i : i + 1] for i in (COLS, COLS + 1, 2 * COLS + 8, 2 * COLS + 9)],
            [(e * 4 + k) * CH for e in range(3)],
        )
    for q in range(2):
        acc = None
        for r in range(2):
            lhs = patch_ref[0, r * COLS : r * COLS + size, q * 4 * CH : q * 4 * CH + half]
            part = jnp.dot(lhs, w_ref[q, r], preferred_element_type=F32)
            acc = part if acc is None else acc + part
        for n in range(ROWS + 1):
            for p in range(2):
                i = 2 * n - 1 + p
                if 0 <= i < 2 * ROWS:
                    mix_ref[i, pl.ds(q, COLS, stride=2), :] = acc[n * COLS : (n + 1) * COLS, p * CH : (p + 1) * CH]
    o_ref[0] = mix_ref[...].astype(BF16)


def up_conv(parts, weight):
    specs = []
    args = []
    for part in parts:
        for a in part:
            rest = a.shape[1:]
            specs.append(pl.BlockSpec((1,) + rest, lambda t, n=len(rest): (t,) + (0,) * n))
            args.append(a)
    specs.append(pl.BlockSpec(weight.shape, lambda t: (0, 0, 0, 0)))
    frames = parts[0][0].shape[0]
    out = (frames, 2 * ROWS, 2 * COLS, CH)
    return pl.pallas_call(
        up_body,
        out_shape=sds(out),
        grid=(frames,),
        in_specs=specs,
        out_specs=pl.BlockSpec((1,) + out[1:], lambda t: (t, 0, 0, 0)),
        scratch_shapes=[
            pltpu.VMEM((1, (ROWS + 2) * COLS, 12 * CH), BF16),
            pltpu.VMEM((2 * ROWS, 2 * COLS, CH), F32),
        ],
        compiler_params=pltpu.CompilerParams(vmem_limit_bytes=24 * MIB),
        name="up_conv",
    )(*args, weight)


def on_device(features, cache_first, cache_second, weight_first, weight_second, weight_up):
    frames = features.shape[0]
    ha, wa, col = lax.axis_index(HA), lax.axis_index("wa"), lax.axis_index("col")
    nh, nw = lax.axis_size(HA), lax.axis_size("wa")
    flags = jnp.stack([ha > 0, ha < nh - 1, wa > 0, wa < nw - 1, col]).astype(jnp.int32)
    slots = sds((nh * nw, 2, CH), F32)

    x, c1, c2, stats, *edges = call(
        first_body,
        [sds(features.shape), sds(cache_first.shape), sds(cache_second.shape), slots]
        + [sds((8, COLS, CH))] * 2
        + [sds((8, WIDE, 16, CH))] * 2
        + [sds(weight_up.shape[:2] + (CH,))] * 4,
        scratch=[pltpu.SemaphoreType.DMA((7,))],
        limit=20,
        name="first",
    )(flags, *[Left(a, HBM) for a in (features, cache_first, cache_second, weight_up)])
    edges, w_pieces = edges[:4], edges[4:]
    w_got = to_peers(w_pieces[1:])
    stats = spread(stats)
    rows = swap_rows(*edges[:2])
    cornered = call(corner_body, [sds((8, WIDE, 16, CH))] * 2, name="corners")(*rows, *edges[2:])
    halo = rows + swap_columns(*cornered)
    pieces = conv(
        flags, x, c1, stats, halo, 0, 2, (), weight_first.reshape(-1, 4 * CH), 2, "conv_first", after=w_got
    )
    hidden, side, stats, top, bot = call(
        hidden_body,
        [sds(features.shape), sds((16 * ROWS, CH), F32), slots] + [sds((4 * COLS + 16, CH))] * 2,
        limit=12,
        name="hidden",
    )(*pieces)
    stats = spread(stats)
    around = (side,) + swap_rows(top, bot)
    pieces = conv(
        flags, hidden, c2, stats, halo, 6, None, around, weight_second.reshape(-1, 4 * CH), 1, "conv_second"
    )
    resid, top, bot = call(
        resid_body,
        [sds((frames, ROWS * COLS + 16, CH))] + [sds((frames, COLS + 8, CH))] * 2,
        scratch=[pltpu.VMEM((8 * ROWS, CH), F32)],
        name="resid",
    )(flags, features, *halo[2:], *pieces)
    others = to_peers([resid] * 3)
    (border,) = call(pack_body, [sds((frames, 2 * COLS + 16, CH))], name="pack")(
        *swap_rows(top, bot), Left(others[0])
    )
    borders = [border] + to_peers([border] * 3)
    (folded,) = call(fold_body, [sds((2, 2, 8 * CH, 2 * CH))], limit=12, name="fold")(
        w_pieces[0], *w_got, *[Left(a) for a in others[1:]]
    )
    return up_conv(list(zip([resid] + others, borders)), folded)


def pack_body(top_ref, bot_ref, after_ref, o_ref):
    o_ref[:, : COLS + 8, :] = top_ref[...]
    o_ref[:, COLS + 8 :, :] = bot_ref[...]


def solution(mesh):
    shape = mesh.devices.shape
    mesh = jax.sharding.Mesh(
        mesh.devices.reshape((shape[0] // 2, 2) + shape[1:]), HA + tuple(mesh.axis_names[1:])
    )
    block = P(None, HA, "wa", "col")
    weight = P(None, "col", None)
    return jax.shard_map(
        on_device,
        mesh=mesh,
        in_specs=(block, block, block, weight, weight, weight),
        out_specs=block,
        check_vma=False,
    )
```

```python
import functools

import jax
import jax.numpy as jnp
from jax import lax
from jax.experimental import pallas as pl
from jax.experimental.pallas import tpu as pltpu
from jax.sharding import PartitionSpec as P

F32 = jnp.float32
BF16 = jnp.bfloat16
CH = 128
GROUP = 16
ROWS = 8
COLS = 32
WIDE = 3
BLOCK = 4 * ROWS * COLS * GROUP
MIB = 1 << 20

VMEM = pl.BlockSpec(memory_space=pltpu.VMEM)
SMEM = pl.BlockSpec(memory_space=pltpu.SMEM)
ANY = pl.BlockSpec(memory_space=pl.ANY)
HBM = pl.BlockSpec(memory_space=pltpu.HBM)
HA = ("z", "core")


class Left:
    def __init__(self, array, spec=ANY):
        self.array, self.spec = array, spec
        if spec is HBM:
            self.array = pltpu.with_memory_space_constraint(array, pltpu.HBM)


def call(body, outs, scratch=(), flops=0, limit=8, name=None):
    def run(*args):
        specs = [a.spec if isinstance(a, Left) else SMEM if a.dtype == jnp.int32 else VMEM for a in args]
        args = [a.array if isinstance(a, Left) else a for a in args]
        nbytes = sum(a.size * a.dtype.itemsize for a in args + list(outs))
        return pl.pallas_call(
            body,
            out_shape=list(outs),
            in_specs=specs,
            out_specs=[VMEM] * len(outs),
            scratch_shapes=list(scratch),
            compiler_params=pltpu.CompilerParams(vmem_limit_bytes=limit * MIB),
            cost_estimate=pl.CostEstimate(flops=flops, bytes_accessed=nbytes, transcendentals=0),
            name=name,
        )(*args)

    return run


def sds(shape, dtype=BF16):
    return jax.ShapeDtypeStruct(shape, dtype)


def group_sum(row):
    lane = lax.broadcasted_iota(jnp.int32, row.shape, 1)
    shift = 1
    while shift < GROUP:
        other = jnp.where((lane & shift) != 0, pltpu.roll(row, shift, 1), pltpu.roll(row, CH - shift, 1))
        row = row + other
        shift *= 2
    return row


def local_stats(flat):
    count = flat.shape[0] * GROUP
    mean = group_sum(jnp.sum(flat, axis=0, keepdims=True)) * (1.0 / count)
    dev = flat - mean
    m2 = group_sum(jnp.sum(dev * dev, axis=0, keepdims=True))
    return mean, m2


def merge(st_ref, count):
    means = st_ref[:, 0, :]
    mean = jnp.sum(means, axis=0, keepdims=True) * (1.0 / st_ref.shape[0])
    apart = means - mean
    m2 = jnp.sum(st_ref[:, 1, :] + count * (apart * apart), axis=0, keepdims=True)
    return mean, lax.rsqrt(m2 * (1.0 / (count * st_ref.shape[0])) + 1e-6)


def store_stats(ref, mean, m2):
    row = lax.broadcasted_iota(jnp.int32, (2, CH), 0)
    ref[...] = jnp.broadcast_to(jnp.where(row == 0, mean, m2)[None], ref.shape)


def spread(slots):
    return lax.all_to_all(slots, HA + ("wa",), 0, 0, tiled=True)


def store_edges(frames, refs):
    top_ref, bot_ref, lef_ref, rig_ref = refs
    at = 0
    for v in frames:
        n = v.shape[0]
        top_ref[at : at + n] = v[:, 0].astype(BF16)
        bot_ref[at : at + n] = v[:, ROWS - 1].astype(BF16)
        for i in range(WIDE):
            for ref, j in ((lef_ref, i), (rig_ref, COLS - WIDE + i)):
                column = jnp.concatenate([v[:, :, j, :], jnp.zeros((n, 8, CH), F32)], axis=1)
                ref[at : at + n, i] = column.astype(BF16)
        at += n


def first_body(x_hbm, c1_hbm, c2_hbm, x_ref, c1_ref, c2_ref, slot_ref, *rest):
    edges, sem = rest[:4], rest[4]
    copies = [
        pltpu.make_async_copy(src, dst, sem.at[i])
        for i, (src, dst) in enumerate(((x_hbm, x_ref), (c1_hbm, c1_ref), (c2_hbm, c2_ref)))
    ]
    for c in copies:
        c.start()
    for c in copies:
        c.wait()
    x, c1, c2 = x_ref[...].astype(F32), c1_ref[...].astype(F32), c2_ref[...].astype(F32)
    store_stats(slot_ref, *local_stats(x.reshape(-1, CH)))
    store_edges((c1, x, c2), edges)


def corner_body(top_ref, bot_ref, lef_ref, rig_ref, lo_ref, ro_ref):
    top = top_ref[...].astype(F32)
    bot = bot_ref[...].astype(F32)
    shape = (lef_ref.shape[0],) + lef_ref.shape[2:]
    row = lax.broadcasted_iota(jnp.int32, shape, 1)
    for i in range(WIDE):
        for src, dst, at in ((lef_ref, lo_ref, i), (rig_ref, ro_ref, COLS - WIDE + i)):
            v = src[:, i].astype(F32)
            v = jnp.where(row == 8, top[:, at : at + 1, :], v)
            v = jnp.where(row == 9, bot[:, at : at + 1, :], v)
            dst[:, i] = v.astype(BF16)


def swap_rows(top, bot):
    n = lax.axis_size(HA)
    above = lax.ppermute(bot, HA, [(i, i + 1) for i in range(n - 1)])
    below = lax.ppermute(top, HA, [(i + 1, i) for i in range(n - 1)])
    return above, below


def swap_columns(lef, rig):
    n = lax.axis_size("wa")
    left = lax.ppermute(rig, "wa", [(i, i + 1) for i in range(n - 1)])
    right = lax.ppermute(lef, "wa", [(i + 1, i) for i in range(n - 1)])
    return left, right


def shifted(rows, left, right):
    n = rows.shape[0]
    flat = rows.reshape(n * COLS, CH)
    col = lax.broadcasted_iota(jnp.int32, rows.shape, 1)
    before = pltpu.roll(flat, 1, 0).reshape(rows.shape)
    after = pltpu.roll(flat, n * COLS - 1, 0).reshape(rows.shape)
    before = jnp.where(col == 0, left[:, None, :], before)
    after = jnp.where(col == COLS - 1, right[:, None, :], after)
    return before, after


def place(patch_ref, frame, rows, at, left, right, lanes):
    n = rows.shape[0]
    before, after = shifted(rows, left, right)
    for e, v in enumerate((before, rows, after)):
        patch_ref[frame, at * COLS : (at + n) * COLS, lanes[e] : lanes[e] + CH] = v.reshape(n * COLS, CH).astype(BF16)


def place_frame(patch_ref, frame, inner, top, bot, lef, rig, corners, lanes):
    place(patch_ref, frame, inner, 1, lef, rig, lanes)
    place(patch_ref, frame, top[None], 0, corners[0], corners[1], lanes)
    place(patch_ref, frame, bot[None], ROWS + 1, corners[2], corners[3], lanes)


def multiply(patch_ref, side_ref, w_ref, outs):
    depth = 9 * CH
    size = ROWS * COLS
    slot = side_ref.shape[1] // (ROWS + 2)
    jobs = [(t * size, size, [(patch_ref, t + a, COLS) for a in range(3)]) for t in range(4)]
    jobs.append((4 * size, ROWS * slot, [(side_ref, a, slot) for a in range(3)]))
    for at, rows, sources in jobs:
        acc = None
        for a, (ref, i, step) in enumerate(sources):
            lhs = jnp.concatenate([ref[i, b * step : b * step + rows, :] for b in range(3)], axis=1)
            part = jnp.dot(lhs, w_ref[a * depth : (a + 1) * depth, :], preferred_element_type=F32)
            acc = part if acc is None else acc + part
        for i, out in enumerate(outs):
            out[at : at + rows, :] = acc[:, i * CH : (i + 1) * CH].astype(BF16)


def halo_frame(refs, at, change, has, reach):
    top, bot, lef, rig = refs
    above = jnp.where(has[0], change(top[at].astype(F32)), 0.0)
    below = jnp.where(has[1], change(bot[at].astype(F32)), 0.0)
    columns = {}
    for i in range(reach):
        for ref, flag, j, x in ((lef, has[2], WIDE - 1 - i, -1 - i), (rig, has[3], i, COLS + i)):
            v = jnp.where(flag, change(ref[at, j].astype(F32)), 0.0)
            columns[x] = (v[0:8], jnp.where(has[0], v[8:9], 0.0), jnp.where(has[1], v[9:10], 0.0))
    return above, below, columns


def place_sides(mix_ref, frame, ext, inner, above, below, columns):
    columns = dict(columns)
    for x in (0, COLS - 1):
        columns[x] = (inner[:, x, :], above[x : x + 1], below[x : x + 1])
    step = 8 * ext
    for a in range(3):
        t = frame - a
        if not 0 <= t < 4:
            continue
        for c, x in enumerate(list(range(-ext, 0)) + list(range(COLS, COLS + ext))):
            w = t * 2 * ext + c
            for e in range(3):
                rows, up, down = columns[x + e - 1]
                mix_ref[a, e, pl.ds(w, 1), :] = up
                mix_ref[a, e, pl.ds(step + w, ROWS, stride=step), :] = rows
                mix_ref[a, e, pl.ds((ROWS + 1) * step + w, 1), :] = down


def far_body(ext, cache_at, act_at, extra, flag_ref, x_ref, c_ref, st_ref, *rest):
    halo, rest = rest[:4], rest[4:]
    if act_at is None:
        beside_ref, above_ref, below_ref = rest[:3]
        rest = rest[3:]
    w_hbm, rest = rest[0], rest[1 + extra :]
    out2, out1, patch_ref, side_ref, near_ref, w_ref, mix_ref, wide_ref, sem = rest
    col = flag_ref[4]
    copies = []
    for i, (k, dst, at) in enumerate(((2, w_ref, 0), (1, w_ref, CH), (3, near_ref, 0), (0, near_ref, CH))):
        block = pl.multiple_of(lax.rem(col + k, 4) * CH, CH)
        copies.append(
            pltpu.make_async_copy(w_hbm.at[:, pl.ds(block, CH)], dst.at[:, at : at + CH], sem.at[i])
        )
        copies[-1].start()
    has = [flag_ref[i] > 0 for i in range(4)]
    mean, scale = merge(st_ref, BLOCK)

    def act(v):
        u = (v - mean) * scale
        return u / (1.0 + jnp.exp(-u))

    if act_at is None:
        wide_ref[...] = act(beside_ref[...])
        outer = [
            jnp.where(flag, act(ref[...].astype(F32)), 0.0) for ref, flag in ((above_ref, has[0]), (below_ref, has[1]))
        ]
    for s in range(6):
        if s < 2:
            inner = c_ref[s].astype(F32)
            above, below, columns = halo_frame(halo, cache_at + s, lambda v: v, has, ext + 1)
        else:
            t = s - 2
            inner = act(x_ref[t].astype(F32))
            if act_at is not None:
                above, below, columns = halo_frame(halo, act_at + t, act, has, ext + 1)
            else:
                above, below = [v[t * COLS : (t + 1) * COLS] for v in outer]
                columns = {}
                for c, x in enumerate((-2, -1, COLS, COLS + 1)):
                    flag = has[2 + c // 2]
                    px = 4 * COLS + 4 * t + c
                    rows = wide_ref[pl.ds(4 * t + c, ROWS, stride=16), :]
                    columns[x] = tuple(
                        jnp.where(flag, v, 0.0) for v in (rows, outer[0][px : px + 1], outer[1][px : px + 1])
                    )
        corners = [columns[-1][1], columns[COLS][1], columns[-1][2], columns[COLS][2]]
        place_frame(
            patch_ref, s, inner, above, below, columns[-1][0], columns[COLS][0], corners, (0, CH, 2 * CH)
        )
        place_sides(mix_ref, s, ext, inner, above, below, columns)
    for a in range(3):
        for e in range(3):
            side_ref[a, :, e * CH : (e + 1) * CH] = mix_ref[a, e].astype(BF16)
    copies[0].wait()
    copies[1].wait()
    multiply(patch_ref, side_ref, w_ref, (out2, out1))
    copies[2].wait()
    copies[3].wait()


def near_body(patch_ref, side_ref, w_ref, *rest):
    multiply(patch_ref, side_ref, w_ref, rest[-2:])


def conv(flags, x, cache, stats, halo, cache_at, act_at, around, weight, ext, name, after=(), cut=None):
    n = x.shape[0] * ROWS * COLS + ROWS * 8 * ext
    depth, width = weight.shape
    flops = n * depth * width
    piece = sds((n, CH))
    body = functools.partial(far_body, ext, cache_at, act_at, 0)
    out2, out1, patch, side, near = call(
        body,
        [piece] * 2
        + [
            sds((6, (ROWS + 2) * COLS, 3 * CH)),
            sds((3, (ROWS + 2) * 8 * ext, 3 * CH)),
            sds((depth, 2 * CH)),
        ],
        scratch=[
            pltpu.VMEM((depth, 2 * CH), BF16),
            pltpu.VMEM((3, 3, (ROWS + 2) * 8 * ext, CH), F32),
            pltpu.VMEM((16 * ROWS, CH), F32),
            pltpu.SemaphoreType.DMA((4,)),
        ],
        flops=flops,
        limit=20,
        name=name + "_far",
    )(flags, x, cache, stats, *halo, *around, Left(weight, HBM))
    got2 = to_peer(out2, 2)
    got1 = to_peer(out1, 1)
    out3, own = call(near_body, [piece] * 2, flops=flops, limit=16, name=name + "_near")(
        patch, side, near, *[Left(a) for a in after]
    )
    total = sds((n, CH), F32)
    if cut is None:
        return [own, *call(add_body, [total], name=name + "_add")(got1, got2), to_peer(out3, 3)]
    far, *cut = call(
        add_cut_body,
        [total] + [sds(cut.shape[:2] + (CH,))] * 4,
        scratch=[pltpu.SemaphoreType.DMA((4,))],
        name=name + "_add",
    )(flags, got1, got2, Left(cut, HBM))
    return [own, far, to_peer(out3, 3)], cut


def add_body(a_ref, b_ref, o_ref):
    o_ref[...] = a_ref[...].astype(F32) + b_ref[...].astype(F32)


def add_cut_body(flag_ref, a_ref, b_ref, w_hbm, o_ref, *rest):
    pieces, sem = rest[:4], rest[4]
    copies = []
    for k, piece in enumerate(pieces):
        block = pl.multiple_of(lax.rem(flag_ref[4] + k, 4) * CH, CH)
        copies.append(pltpu.make_async_copy(w_hbm.at[:, :, pl.ds(block, CH)], piece, sem.at[k]))
        copies[-1].start()
    add_body(a_ref, b_ref, o_ref)
    for c in copies:
        c.wait()


def gate_body(*refs):
    del refs


def gate(arrays, after):
    n = len(arrays)
    return pl.pallas_call(
        gate_body,
        out_shape=[sds(a.shape) for a in arrays],
        in_specs=[ANY] * (n + 1),
        out_specs=[ANY] * n,
        input_output_aliases={i: i for i in range(n)},
        compiler_params=pltpu.CompilerParams(vmem_limit_bytes=8 * MIB),
        name="gate",
    )(*arrays, after)


def to_peer(piece, k):
    n = lax.axis_size("col")
    return lax.ppermute(piece, "col", [(i, (i + k) % n) for i in range(n)])


def to_peers(pieces):
    got = {k: to_peer(pieces[k - 1], k) for k in (2, 1, 3)}
    return [got[k] for k in (1, 2, 3)]


def hidden_body(p0, far, p3, h_ref, side_ref, slot_ref, top_ref, bot_ref):
    h = (p0[...].astype(F32) + p3[...].astype(F32) + far[...]).astype(BF16).astype(F32)
    size = 4 * ROWS * COLS
    mean, m2 = local_stats(h[:size])
    store_stats(slot_ref, mean, m2)
    main = h[:size].reshape(h_ref.shape)
    h_ref[...] = main.astype(BF16)
    side_ref[...] = h[size:]
    for ref, r in ((top_ref, 0), (bot_ref, ROWS - 1)):
        ref[0 : 4 * COLS, :] = main[:, r].reshape(4 * COLS, CH).astype(BF16)
        ref[4 * COLS :, :] = h[size + 16 * r : size + 16 * (r + 1)].astype(BF16)


def resid_body(flag_ref, x_ref, lef_ref, rig_ref, p0, far, p3, o_ref, top_ref, bot_ref, side_ref):
    total = p0[...].astype(F32) + p3[...].astype(F32) + far[...]
    size = ROWS * COLS
    side_ref[...] = total[4 * size :]
    row = lax.broadcasted_iota(jnp.int32, (8, CH), 0)
    for t in range(4):
        main = x_ref[t].astype(F32).reshape(size, CH) + total[t * size : (t + 1) * size]
        o_ref[t, 0:size, :] = main.astype(BF16)
        beside = []
        for c, (ref, i) in enumerate(((lef_ref, WIDE - 1), (rig_ref, 0))):
            v = ref[2 + t, i].astype(F32)[0:ROWS] + side_ref[pl.ds(2 * t + c, ROWS, stride=8), :]
            beside.append(jnp.where(flag_ref[2 + c] > 0, v, 0.0))
            o_ref[t, size + 8 * c : size + 8 * (c + 1), :] = beside[c].astype(BF16)
        for ref, r in ((top_ref, 0), (bot_ref, ROWS - 1)):
            ref[t, 0:COLS, :] = main[r * COLS : (r + 1) * COLS].astype(BF16)
            px = [v[r : r + 1] for v in beside]
            ref[t, COLS:, :] = jnp.where(row == 0, px[0], jnp.where(row == 1, px[1], 0.0)).astype(BF16)


ROW_TAPS = {(0, 0): (-1, 0), (0, 1): (1,), (1, 0): (-1,), (1, 1): (0, 1)}
COL_TAPS = {(0, 0): (-1,), (0, 1): (0, 1), (1, 0): (-1, 0), (1, 1): (1,)}


def fold_body(w0, w1, w2, w3, *rest):
    o_ref = rest[-1]
    for k, ref in enumerate((w0, w1, w2, w3)):
        taps = [ref[i].astype(F32) for i in range(9)]
        for q in range(2):
            for r in range(2):
                for s in range(2):
                    for p in range(2):
                        total = None
                        for b in ROW_TAPS[p, r]:
                            for e in COL_TAPS[q, s]:
                                tap = taps[(b + 1) * 3 + (e + 1)]
                                total = tap if total is None else total + tap
                        at = (s * 4 + k) * CH
                        o_ref[q, r, at : at + CH, p * CH : (p + 1) * CH] = total.astype(BF16)


def up_body(*refs):
    parts = [refs[2 * k : 2 * k + 2] for k in range(4)]
    w_ref, o_ref, patch_ref, mix_ref = refs[8:12]
    size = (ROWS + 1) * COLS
    half = 2 * 4 * CH
    for k, (x, border) in enumerate(parts):
        edge = border[0].astype(F32)
        own = x[0].astype(F32)
        inside = ROWS * COLS
        place_frame(
            patch_ref,
            0,
            own[:inside].reshape(ROWS, COLS, CH),
            edge[:COLS],
            edge[COLS + 8 : 2 * COLS + 8],
            own[inside : inside + 8],
            own[inside + 8 :],
            [edge[i : i + 1] for i in (COLS, COLS + 1, 2 * COLS + 8, 2 * COLS + 9)],
            [(e * 4 + k) * CH for e in range(3)],
        )
    for q in range(2):
        acc = None
        for r in range(2):
            lhs = patch_ref[0, r * COLS : r * COLS + size, q * 4 * CH : q * 4 * CH + half]
            part = jnp.dot(lhs, w_ref[q, r], preferred_element_type=F32)
            acc = part if acc is None else acc + part
        for n in range(ROWS + 1):
            for p in range(2):
                i = 2 * n - 1 + p
                if 0 <= i < 2 * ROWS:
                    mix_ref[i, pl.ds(q, COLS, stride=2), :] = acc[n * COLS : (n + 1) * COLS, p * CH : (p + 1) * CH]
    o_ref[0] = mix_ref[...].astype(BF16)


def up_conv(parts, weight):
    specs = []
    args = []
    for part in parts:
        for a in part:
            rest = a.shape[1:]
            specs.append(pl.BlockSpec((1,) + rest, lambda t, n=len(rest): (t,) + (0,) * n))
            args.append(a)
    specs.append(pl.BlockSpec(weight.shape, lambda t: (0, 0, 0, 0)))
    frames = parts[0][0].shape[0]
    out = (frames, 2 * ROWS, 2 * COLS, CH)
    return pl.pallas_call(
        up_body,
        out_shape=sds(out),
        grid=(frames,),
        in_specs=specs,
        out_specs=pl.BlockSpec((1,) + out[1:], lambda t: (t, 0, 0, 0)),
        scratch_shapes=[
            pltpu.VMEM((1, (ROWS + 2) * COLS, 12 * CH), BF16),
            pltpu.VMEM((2 * ROWS, 2 * COLS, CH), F32),
        ],
        compiler_params=pltpu.CompilerParams(vmem_limit_bytes=24 * MIB),
        name="up_conv",
    )(*args, weight)


def on_device(features, cache_first, cache_second, weight_first, weight_second, weight_up):
    frames = features.shape[0]
    ha, wa, col = lax.axis_index(HA), lax.axis_index("wa"), lax.axis_index("col")
    nh, nw = lax.axis_size(HA), lax.axis_size("wa")
    flags = jnp.stack([ha > 0, ha < nh - 1, wa > 0, wa < nw - 1, col]).astype(jnp.int32)
    slots = sds((nh * nw, 2, CH), F32)

    x, c1, c2, stats, *edges = call(
        first_body,
        [sds(features.shape), sds(cache_first.shape), sds(cache_second.shape), slots]
        + [sds((8, COLS, CH))] * 2
        + [sds((8, WIDE, 16, CH))] * 2,
        scratch=[pltpu.SemaphoreType.DMA((3,))],
        limit=20,
        name="first",
    )(*[Left(a, HBM) for a in (features, cache_first, cache_second)])
    stats = spread(stats)
    rows = swap_rows(*edges[:2])
    cornered = call(corner_body, [sds((8, WIDE, 16, CH))] * 2, name="corners")(*rows, *edges[2:])
    halo = rows + swap_columns(*cornered)
    pieces, w_pieces = conv(
        flags, x, c1, stats, halo, 0, 2, (), weight_first.reshape(-1, 4 * CH), 2, "conv_first", cut=weight_up
    )
    hidden, side, stats, top, bot = call(
        hidden_body,
        [sds(features.shape), sds((16 * ROWS, CH), F32), slots] + [sds((4 * COLS + 16, CH))] * 2,
        limit=12,
        name="hidden",
    )(*pieces)
    w_got = to_peers(gate(w_pieces[1:], stats))
    stats = spread(stats)
    around = (side,) + swap_rows(top, bot)
    pieces = conv(
        flags, hidden, c2, stats, halo, 6, None, around, weight_second.reshape(-1, 4 * CH), 1, "conv_second", w_got
    )
    resid, top, bot = call(
        resid_body,
        [sds((frames, ROWS * COLS + 16, CH))] + [sds((frames, COLS + 8, CH))] * 2,
        scratch=[pltpu.VMEM((8 * ROWS, CH), F32)],
        name="resid",
    )(flags, features, *halo[2:], *pieces)
    others = to_peers([resid] * 3)
    (border,) = call(pack_body, [sds((frames, 2 * COLS + 16, CH))], name="pack")(
        *swap_rows(top, bot), Left(others[0])
    )
    borders = [border] + to_peers([border] * 3)
    (folded,) = call(fold_body, [sds((2, 2, 8 * CH, 2 * CH))], limit=12, name="fold")(
        w_pieces[0], *w_got, *[Left(a) for a in others[1:]]
    )
    return up_conv(list(zip([resid] + others, borders)), folded)


def pack_body(top_ref, bot_ref, after_ref, o_ref):
    o_ref[:, : COLS + 8, :] = top_ref[...]
    o_ref[:, COLS + 8 :, :] = bot_ref[...]


def solution(mesh):
    shape = mesh.devices.shape
    mesh = jax.sharding.Mesh(
        mesh.devices.reshape((shape[0] // 2, 2) + shape[1:]), HA + tuple(mesh.axis_names[1:])
    )
    block = P(None, HA, "wa", "col")
    weight = P(None, "col", None)
    return jax.shard_map(
        on_device,
        mesh=mesh,
        in_specs=(block, block, block, weight, weight, weight),
        out_specs=block,
        check_vma=False,
    )
```

```python
import functools

import jax
import jax.numpy as jnp
from jax import lax
from jax.experimental import pallas as pl
from jax.experimental.pallas import tpu as pltpu
from jax.sharding import PartitionSpec as P

F32 = jnp.float32
BF16 = jnp.bfloat16
CH = 128
GROUP = 16
ROWS = 8
COLS = 32
WIDE = 3
BLOCK = 4 * ROWS * COLS * GROUP
MIB = 1 << 20

VMEM = pl.BlockSpec(memory_space=pltpu.VMEM)
SMEM = pl.BlockSpec(memory_space=pltpu.SMEM)
ANY = pl.BlockSpec(memory_space=pl.ANY)
HBM = pl.BlockSpec(memory_space=pltpu.HBM)
HA = ("z", "core")


class Left:
    def __init__(self, array, spec=ANY):
        self.array, self.spec = array, spec
        if spec is HBM:
            self.array = pltpu.with_memory_space_constraint(array, pltpu.HBM)


def call(body, outs, scratch=(), flops=0, limit=8, name=None):
    def run(*args):
        specs = [a.spec if isinstance(a, Left) else SMEM if a.dtype == jnp.int32 else VMEM for a in args]
        args = [a.array if isinstance(a, Left) else a for a in args]
        nbytes = sum(a.size * a.dtype.itemsize for a in args + list(outs))
        return pl.pallas_call(
            body,
            out_shape=list(outs),
            in_specs=specs,
            out_specs=[VMEM] * len(outs),
            scratch_shapes=list(scratch),
            compiler_params=pltpu.CompilerParams(vmem_limit_bytes=limit * MIB),
            cost_estimate=pl.CostEstimate(flops=flops, bytes_accessed=nbytes, transcendentals=0),
            name=name,
        )(*args)

    return run


def sds(shape, dtype=BF16):
    return jax.ShapeDtypeStruct(shape, dtype)


def group_sum(row):
    lane = lax.broadcasted_iota(jnp.int32, row.shape, 1)
    shift = 1
    while shift < GROUP:
        other = jnp.where((lane & shift) != 0, pltpu.roll(row, shift, 1), pltpu.roll(row, CH - shift, 1))
        row = row + other
        shift *= 2
    return row


def local_stats(flat):
    count = flat.shape[0] * GROUP
    mean = group_sum(jnp.sum(flat, axis=0, keepdims=True)) * (1.0 / count)
    dev = flat - mean
    m2 = group_sum(jnp.sum(dev * dev, axis=0, keepdims=True))
    return mean, m2


def merge(st_ref, count):
    means = st_ref[:, 0, :]
    mean = jnp.sum(means, axis=0, keepdims=True) * (1.0 / st_ref.shape[0])
    apart = means - mean
    m2 = jnp.sum(st_ref[:, 1, :] + count * (apart * apart), axis=0, keepdims=True)
    return mean, lax.rsqrt(m2 * (1.0 / (count * st_ref.shape[0])) + 1e-6)


def store_stats(ref, mean, m2):
    row = lax.broadcasted_iota(jnp.int32, (2, CH), 0)
    ref[...] = jnp.broadcast_to(jnp.where(row == 0, mean, m2)[None], ref.shape)


def spread(slots):
    return lax.all_to_all(slots, HA + ("wa",), 0, 0, tiled=True)


def store_edges(frames, refs):
    top_ref, bot_ref, lef_ref, rig_ref = refs
    at = 0
    for v in frames:
        n = v.shape[0]
        top_ref[at : at + n] = v[:, 0].astype(BF16)
        bot_ref[at : at + n] = v[:, ROWS - 1].astype(BF16)
        for i in range(WIDE):
            for ref, j in ((lef_ref, i), (rig_ref, COLS - WIDE + i)):
                column = jnp.concatenate([v[:, :, j, :], jnp.zeros((n, 8, CH), F32)], axis=1)
                ref[at : at + n, i] = column.astype(BF16)
        at += n


def first_body(x_hbm, c1_hbm, c2_hbm, x_ref, c1_ref, c2_ref, slot_ref, *rest):
    edges, sem = rest[:4], rest[4]
    copies = [
        pltpu.make_async_copy(src, dst, sem.at[i])
        for i, (src, dst) in enumerate(((x_hbm, x_ref), (c1_hbm, c1_ref), (c2_hbm, c2_ref)))
    ]
    for c in copies:
        c.start()
    for c in copies:
        c.wait()
    x, c1, c2 = x_ref[...].astype(F32), c1_ref[...].astype(F32), c2_ref[...].astype(F32)
    store_stats(slot_ref, *local_stats(x.reshape(-1, CH)))
    store_edges((c1, x, c2), edges)


def corner_body(top_ref, bot_ref, lef_ref, rig_ref, lo_ref, ro_ref):
    top = top_ref[...].astype(F32)
    bot = bot_ref[...].astype(F32)
    shape = (lef_ref.shape[0],) + lef_ref.shape[2:]
    row = lax.broadcasted_iota(jnp.int32, shape, 1)
    for i in range(WIDE):
        for src, dst, at in ((lef_ref, lo_ref, i), (rig_ref, ro_ref, COLS - WIDE + i)):
            v = src[:, i].astype(F32)
            v = jnp.where(row == 8, top[:, at : at + 1, :], v)
            v = jnp.where(row == 9, bot[:, at : at + 1, :], v)
            dst[:, i] = v.astype(BF16)


def swap_rows(top, bot):
    n = lax.axis_size(HA)
    above = lax.ppermute(bot, HA, [(i, i + 1) for i in range(n - 1)])
    below = lax.ppermute(top, HA, [(i + 1, i) for i in range(n - 1)])
    return above, below


def swap_columns(lef, rig):
    n = lax.axis_size("wa")
    left = lax.ppermute(rig, "wa", [(i, i + 1) for i in range(n - 1)])
    right = lax.ppermute(lef, "wa", [(i + 1, i) for i in range(n - 1)])
    return left, right


def shifted(rows, left, right):
    n = rows.shape[0]
    flat = rows.reshape(n * COLS, CH)
    col = lax.broadcasted_iota(jnp.int32, rows.shape, 1)
    before = pltpu.roll(flat, 1, 0).reshape(rows.shape)
    after = pltpu.roll(flat, n * COLS - 1, 0).reshape(rows.shape)
    before = jnp.where(col == 0, left[:, None, :], before)
    after = jnp.where(col == COLS - 1, right[:, None, :], after)
    return before, after


def place(patch_ref, frame, rows, at, left, right, lanes):
    n = rows.shape[0]
    before, after = shifted(rows, left, right)
    for e, v in enumerate((before, rows, after)):
        patch_ref[frame, at * COLS : (at + n) * COLS, lanes[e] : lanes[e] + CH] = v.reshape(n * COLS, CH).astype(BF16)


def place_frame(patch_ref, frame, inner, top, bot, lef, rig, corners, lanes):
    place(patch_ref, frame, inner, 1, lef, rig, lanes)
    place(patch_ref, frame, top[None], 0, corners[0], corners[1], lanes)
    place(patch_ref, frame, bot[None], ROWS + 1, corners[2], corners[3], lanes)


def multiply(patch_ref, side_ref, w_ref, outs):
    depth = 9 * CH
    size = ROWS * COLS
    slot = side_ref.shape[1] // (ROWS + 2)
    jobs = [(t * size, size, [(patch_ref, t + a, COLS) for a in range(3)]) for t in range(4)]
    jobs.append((4 * size, ROWS * slot, [(side_ref, a, slot) for a in range(3)]))
    for at, rows, sources in jobs:
        acc = None
        for a, (ref, i, step) in enumerate(sources):
            lhs = jnp.concatenate([ref[i, b * step : b * step + rows, :] for b in range(3)], axis=1)
            part = jnp.dot(lhs, w_ref[a * depth : (a + 1) * depth, :], preferred_element_type=F32)
            acc = part if acc is None else acc + part
        for i, out in enumerate(outs):
            out[at : at + rows, :] = acc[:, i * CH : (i + 1) * CH].astype(BF16)


def halo_frame(refs, at, change, has, reach):
    top, bot, lef, rig = refs
    above = jnp.where(has[0], change(top[at].astype(F32)), 0.0)
    below = jnp.where(has[1], change(bot[at].astype(F32)), 0.0)
    columns = {}
    for i in range(reach):
        for ref, flag, j, x in ((lef, has[2], WIDE - 1 - i, -1 - i), (rig, has[3], i, COLS + i)):
            v = jnp.where(flag, change(ref[at, j].astype(F32)), 0.0)
            columns[x] = (v[0:8], jnp.where(has[0], v[8:9], 0.0), jnp.where(has[1], v[9:10], 0.0))
    return above, below, columns


def place_sides(mix_ref, frame, ext, inner, above, below, columns):
    columns = dict(columns)
    for x in (0, COLS - 1):
        columns[x] = (inner[:, x, :], above[x : x + 1], below[x : x + 1])
    step = 8 * ext
    for a in range(3):
        t = frame - a
        if not 0 <= t < 4:
            continue
        for c, x in enumerate(list(range(-ext, 0)) + list(range(COLS, COLS + ext))):
            w = t * 2 * ext + c
            for e in range(3):
                rows, up, down = columns[x + e - 1]
                mix_ref[a, e, pl.ds(w, 1), :] = up
                mix_ref[a, e, pl.ds(step + w, ROWS, stride=step), :] = rows
                mix_ref[a, e, pl.ds((ROWS + 1) * step + w, 1), :] = down


def far_body(ext, cache_at, act_at, extra, flag_ref, x_ref, c_ref, st_ref, *rest):
    halo, rest = rest[:4], rest[4:]
    if act_at is None:
        beside_ref, above_ref, below_ref = rest[:3]
        rest = rest[3:]
    w_hbm, rest = rest[0], rest[1 + extra :]
    out2, out1, patch_ref, side_ref, near_ref, w_ref, mix_ref, wide_ref, sem = rest
    col = flag_ref[4]
    copies = []
    for i, (k, dst, at) in enumerate(((2, w_ref, 0), (1, w_ref, CH), (3, near_ref, 0), (0, near_ref, CH))):
        block = pl.multiple_of(lax.rem(col + k, 4) * CH, CH)
        copies.append(
            pltpu.make_async_copy(w_hbm.at[:, pl.ds(block, CH)], dst.at[:, at : at + CH], sem.at[i])
        )
        copies[-1].start()
    has = [flag_ref[i] > 0 for i in range(4)]
    mean, scale = merge(st_ref, BLOCK)

    def act(v):
        u = (v - mean) * scale
        return u / (1.0 + jnp.exp(-u))

    if act_at is None:
        wide_ref[...] = act(beside_ref[...])
        outer = [
            jnp.where(flag, act(ref[...].astype(F32)), 0.0) for ref, flag in ((above_ref, has[0]), (below_ref, has[1]))
        ]
    for s in range(6):
        if s < 2:
            inner = c_ref[s].astype(F32)
            above, below, columns = halo_frame(halo, cache_at + s, lambda v: v, has, ext + 1)
        else:
            t = s - 2
            inner = act(x_ref[t].astype(F32))
            if act_at is not None:
                above, below, columns = halo_frame(halo, act_at + t, act, has, ext + 1)
            else:
                above, below = [v[t * COLS : (t + 1) * COLS] for v in outer]
                columns = {}
                for c, x in enumerate((-2, -1, COLS, COLS + 1)):
                    flag = has[2 + c // 2]
                    px = 4 * COLS + 4 * t + c
                    rows = wide_ref[pl.ds(4 * t + c, ROWS, stride=16), :]
                    columns[x] = tuple(
                        jnp.where(flag, v, 0.0) for v in (rows, outer[0][px : px + 1], outer[1][px : px + 1])
                    )
        corners = [columns[-1][1], columns[COLS][1], columns[-1][2], columns[COLS][2]]
        place_frame(
            patch_ref, s, inner, above, below, columns[-1][0], columns[COLS][0], corners, (0, CH, 2 * CH)
        )
        place_sides(mix_ref, s, ext, inner, above, below, columns)
    for a in range(3):
        for e in range(3):
            side_ref[a, :, e * CH : (e + 1) * CH] = mix_ref[a, e].astype(BF16)
    copies[0].wait()
    copies[1].wait()
    multiply(patch_ref, side_ref, w_ref, (out2, out1))
    copies[2].wait()
    copies[3].wait()


def near_body(patch_ref, side_ref, w_ref, *rest):
    multiply(patch_ref, side_ref, w_ref, rest[-2:])


def near_cut_body(flag_ref, patch_ref, side_ref, w_ref, cut_hbm, out3, out0, *rest):
    pieces, sem = rest[:4], rest[4]
    copies = []
    for k, piece in enumerate(pieces):
        block = pl.multiple_of(lax.rem(flag_ref[4] + k, 4) * CH, CH)
        copies.append(pltpu.make_async_copy(cut_hbm.at[:, :, pl.ds(block, CH)], piece, sem.at[k]))
        copies[-1].start()
    multiply(patch_ref, side_ref, w_ref, (out3, out0))
    for c in copies:
        c.wait()


def conv(flags, x, cache, stats, halo, cache_at, act_at, around, weight, ext, name, after=(), cut=None):
    n = x.shape[0] * ROWS * COLS + ROWS * 8 * ext
    depth, width = weight.shape
    flops = n * depth * width
    piece = sds((n, CH))
    body = functools.partial(far_body, ext, cache_at, act_at, 0)
    out2, out1, patch, side, near = call(
        body,
        [piece] * 2
        + [
            sds((6, (ROWS + 2) * COLS, 3 * CH)),
            sds((3, (ROWS + 2) * 8 * ext, 3 * CH)),
            sds((depth, 2 * CH)),
        ],
        scratch=[
            pltpu.VMEM((depth, 2 * CH), BF16),
            pltpu.VMEM((3, 3, (ROWS + 2) * 8 * ext, CH), F32),
            pltpu.VMEM((16 * ROWS, CH), F32),
            pltpu.SemaphoreType.DMA((4,)),
        ],
        flops=flops,
        limit=20,
        name=name + "_far",
    )(flags, x, cache, stats, *halo, *around, Left(weight, HBM))
    got2 = to_peer(out2, 2)
    got1 = to_peer(out1, 1)
    pieces = []
    if cut is None:
        out3, own = call(near_body, [piece] * 2, flops=flops, limit=16, name=name + "_near")(
            patch, side, near, *[Left(a) for a in after]
        )
    else:
        out3, own, *pieces = call(
            near_cut_body,
            [piece] * 2 + [sds(cut.shape[:2] + (CH,))] * 4,
            scratch=[pltpu.SemaphoreType.DMA((4,))],
            flops=flops,
            limit=20,
            name=name + "_near",
        )(flags, patch, side, near, Left(cut, HBM))
    (far,) = call(add_body, [sds((n, CH), F32)], name=name + "_add")(got1, got2)
    return (own, far, to_peer(out3, 3)), pieces


def add_body(a_ref, b_ref, o_ref):
    o_ref[...] = a_ref[...].astype(F32) + b_ref[...].astype(F32)


def gate_body(*refs):
    del refs


def gate(arrays, after, flops=0):
    n = len(arrays)
    return pl.pallas_call(
        gate_body,
        out_shape=[sds(a.shape) for a in arrays],
        in_specs=[ANY] * (n + 1),
        out_specs=[ANY] * n,
        input_output_aliases={i: i for i in range(n)},
        compiler_params=pltpu.CompilerParams(vmem_limit_bytes=8 * MIB),
        cost_estimate=pl.CostEstimate(flops=flops, bytes_accessed=0, transcendentals=0),
        name="gate",
    )(*arrays, after)


def to_peer(piece, k):
    n = lax.axis_size("col")
    return lax.ppermute(piece, "col", [(i, (i + k) % n) for i in range(n)])


def to_peers(pieces):
    got = {k: to_peer(pieces[k - 1], k) for k in (2, 1, 3)}
    return [got[k] for k in (1, 2, 3)]


def hidden_body(p0, far, p3, h_ref, side_ref, slot_ref, top_ref, bot_ref):
    h = (p0[...].astype(F32) + p3[...].astype(F32) + far[...]).astype(BF16).astype(F32)
    size = 4 * ROWS * COLS
    mean, m2 = local_stats(h[:size])
    store_stats(slot_ref, mean, m2)
    main = h[:size].reshape(h_ref.shape)
    h_ref[...] = main.astype(BF16)
    side_ref[...] = h[size:]
    for ref, r in ((top_ref, 0), (bot_ref, ROWS - 1)):
        ref[0 : 4 * COLS, :] = main[:, r].reshape(4 * COLS, CH).astype(BF16)
        ref[4 * COLS :, :] = h[size + 16 * r : size + 16 * (r + 1)].astype(BF16)


def resid_body(flag_ref, x_ref, lef_ref, rig_ref, p0, far, p3, o_ref, top_ref, bot_ref, side_ref):
    total = p0[...].astype(F32) + p3[...].astype(F32) + far[...]
    size = ROWS * COLS
    side_ref[...] = total[4 * size :]
    row = lax.broadcasted_iota(jnp.int32, (8, CH), 0)
    for t in range(4):
        main = x_ref[t].astype(F32).reshape(size, CH) + total[t * size : (t + 1) * size]
        o_ref[t, 0:size, :] = main.astype(BF16)
        beside = []
        for c, (ref, i) in enumerate(((lef_ref, WIDE - 1), (rig_ref, 0))):
            v = ref[2 + t, i].astype(F32)[0:ROWS] + side_ref[pl.ds(2 * t + c, ROWS, stride=8), :]
            beside.append(jnp.where(flag_ref[2 + c] > 0, v, 0.0))
            o_ref[t, size + 8 * c : size + 8 * (c + 1), :] = beside[c].astype(BF16)
        for ref, r in ((top_ref, 0), (bot_ref, ROWS - 1)):
            ref[t, 0:COLS, :] = main[r * COLS : (r + 1) * COLS].astype(BF16)
            px = [v[r : r + 1] for v in beside]
            ref[t, COLS:, :] = jnp.where(row == 0, px[0], jnp.where(row == 1, px[1], 0.0)).astype(BF16)


ROW_TAPS = {(0, 0): (-1, 0), (0, 1): (1,), (1, 0): (-1,), (1, 1): (0, 1)}
COL_TAPS = {(0, 0): (-1,), (0, 1): (0, 1), (1, 0): (-1, 0), (1, 1): (1,)}


def fold_body(w0, w1, w2, w3, *rest):
    o_ref = rest[-1]
    for k, ref in enumerate((w0, w1, w2, w3)):
        taps = [ref[i].astype(F32) for i in range(9)]
        for q in range(2):
            for r in range(2):
                for s in range(2):
                    for p in range(2):
                        total = None
                        for b in ROW_TAPS[p, r]:
                            for e in COL_TAPS[q, s]:
                                tap = taps[(b + 1) * 3 + (e + 1)]
                                total = tap if total is None else total + tap
                        at = (s * 4 + k) * CH
                        o_ref[q, r, at : at + CH, p * CH : (p + 1) * CH] = total.astype(BF16)


def up_body(*refs):
    parts = [refs[2 * k : 2 * k + 2] for k in range(4)]
    w_ref, o_ref, patch_ref, mix_ref = refs[8:12]
    size = (ROWS + 1) * COLS
    half = 2 * 4 * CH
    for k, (x, border) in enumerate(parts):
        edge = border[0].astype(F32)
        own = x[0].astype(F32)
        inside = ROWS * COLS
        place_frame(
            patch_ref,
            0,
            own[:inside].reshape(ROWS, COLS, CH),
            edge[:COLS],
            edge[COLS + 8 : 2 * COLS + 8],
            own[inside : inside + 8],
            own[inside + 8 :],
            [edge[i : i + 1] for i in (COLS, COLS + 1, 2 * COLS + 8, 2 * COLS + 9)],
            [(e * 4 + k) * CH for e in range(3)],
        )
    for q in range(2):
        acc = None
        for r in range(2):
            lhs = patch_ref[0, r * COLS : r * COLS + size, q * 4 * CH : q * 4 * CH + half]
            part = jnp.dot(lhs, w_ref[q, r], preferred_element_type=F32)
            acc = part if acc is None else acc + part
        for n in range(ROWS + 1):
            for p in range(2):
                i = 2 * n - 1 + p
                if 0 <= i < 2 * ROWS:
                    mix_ref[i, pl.ds(q, COLS, stride=2), :] = acc[n * COLS : (n + 1) * COLS, p * CH : (p + 1) * CH]
    o_ref[0] = mix_ref[...].astype(BF16)


def up_conv(parts, weight):
    specs = []
    args = []
    for part in parts:
        for a in part:
            rest = a.shape[1:]
            specs.append(pl.BlockSpec((1,) + rest, lambda t, n=len(rest): (t,) + (0,) * n))
            args.append(a)
    specs.append(pl.BlockSpec(weight.shape, lambda t: (0, 0, 0, 0)))
    frames = parts[0][0].shape[0]
    out = (frames, 2 * ROWS, 2 * COLS, CH)
    return pl.pallas_call(
        up_body,
        out_shape=sds(out),
        grid=(frames,),
        in_specs=specs,
        out_specs=pl.BlockSpec((1,) + out[1:], lambda t: (t, 0, 0, 0)),
        scratch_shapes=[
            pltpu.VMEM((1, (ROWS + 2) * COLS, 12 * CH), BF16),
            pltpu.VMEM((2 * ROWS, 2 * COLS, CH), F32),
        ],
        compiler_params=pltpu.CompilerParams(vmem_limit_bytes=24 * MIB),
        name="up_conv",
    )(*args, weight)


def on_device(features, cache_first, cache_second, weight_first, weight_second, weight_up):
    frames = features.shape[0]
    ha, wa, col = lax.axis_index(HA), lax.axis_index("wa"), lax.axis_index("col")
    nh, nw = lax.axis_size(HA), lax.axis_size("wa")
    flags = jnp.stack([ha > 0, ha < nh - 1, wa > 0, wa < nw - 1, col]).astype(jnp.int32)
    slots = sds((nh * nw, 2, CH), F32)

    x, c1, c2, stats, *edges = call(
        first_body,
        [sds(features.shape), sds(cache_first.shape), sds(cache_second.shape), slots]
        + [sds((8, COLS, CH))] * 2
        + [sds((8, WIDE, 16, CH))] * 2,
        scratch=[pltpu.SemaphoreType.DMA((3,))],
        limit=20,
        name="first",
    )(*[Left(a, HBM) for a in (features, cache_first, cache_second)])
    stats = spread(stats)
    rows = swap_rows(*edges[:2])
    cornered = call(corner_body, [sds((8, WIDE, 16, CH))] * 2, name="corners")(*rows, *edges[2:])
    halo = rows + swap_columns(*cornered)
    pieces, w_pieces = conv(
        flags, x, c1, stats, halo, 0, 2, (), weight_first.reshape(-1, 4 * CH), 2, "conv_first", cut=weight_up
    )
    hidden, side, stats, top, bot = call(
        hidden_body,
        [sds(features.shape), sds((16 * ROWS, CH), F32), slots] + [sds((4 * COLS + 16, CH))] * 2,
        limit=12,
        name="hidden",
    )(*pieces)
    w_got = to_peers(gate(w_pieces[1:], stats))
    stats = spread(stats)
    top, bot = swap_rows(top, bot)
    around = (side, *gate([top, bot], side, 5000000000))
    pieces, _ = conv(
        flags, hidden, c2, stats, halo, 6, None, around, weight_second.reshape(-1, 4 * CH), 1, "conv_second", w_got
    )
    resid, top, bot = call(
        resid_body,
        [sds((frames, ROWS * COLS + 16, CH))] + [sds((frames, COLS + 8, CH))] * 2,
        scratch=[pltpu.VMEM((8 * ROWS, CH), F32)],
        name="resid",
    )(flags, features, *halo[2:], *pieces)
    others = to_peers([resid] * 3)
    (border,) = call(pack_body, [sds((frames, 2 * COLS + 16, CH))], name="pack")(
        *gate(swap_rows(top, bot), resid, 2000000000), Left(others[0])
    )
    borders = [border] + to_peers([border] * 3)
    (folded,) = call(fold_body, [sds((2, 2, 8 * CH, 2 * CH))], limit=12, name="fold")(
        w_pieces[0], *w_got, *[Left(a) for a in others[1:]]
    )
    return up_conv(list(zip([resid] + others, borders)), folded)


def pack_body(top_ref, bot_ref, after_ref, o_ref):
    o_ref[:, : COLS + 8, :] = top_ref[...]
    o_ref[:, COLS + 8 :, :] = bot_ref[...]


def solution(mesh):
    shape = mesh.devices.shape
    mesh = jax.sharding.Mesh(
        mesh.devices.reshape((shape[0] // 2, 2) + shape[1:]), HA + tuple(mesh.axis_names[1:])
    )
    block = P(None, HA, "wa", "col")
    weight = P(None, "col", None)
    return jax.shard_map(
        on_device,
        mesh=mesh,
        in_specs=(block, block, block, weight, weight, weight),
        out_specs=block,
        check_vma=False,
    )
```

```python
import functools

import jax
import jax.numpy as jnp
from jax import lax
from jax.experimental import pallas as pl
from jax.experimental.pallas import tpu as pltpu
from jax.sharding import PartitionSpec as P

F32 = jnp.float32
BF16 = jnp.bfloat16
CH = 128
GROUP = 16
ROWS = 8
COLS = 32
WIDE = 3
BLOCK = 4 * ROWS * COLS * GROUP
MIB = 1 << 20

VMEM = pl.BlockSpec(memory_space=pltpu.VMEM)
SMEM = pl.BlockSpec(memory_space=pltpu.SMEM)
ANY = pl.BlockSpec(memory_space=pl.ANY)
HBM = pl.BlockSpec(memory_space=pltpu.HBM)
HA = ("z", "core")


class Left:
    def __init__(self, array, spec=ANY):
        self.array, self.spec = array, spec
        if spec is HBM:
            self.array = pltpu.with_memory_space_constraint(array, pltpu.HBM)


def call(body, outs, scratch=(), flops=0, limit=8, name=None):
    def run(*args):
        specs = [a.spec if isinstance(a, Left) else SMEM if a.dtype == jnp.int32 else VMEM for a in args]
        args = [a.array if isinstance(a, Left) else a for a in args]
        nbytes = sum(a.size * a.dtype.itemsize for a in args + list(outs))
        return pl.pallas_call(
            body,
            out_shape=list(outs),
            in_specs=specs,
            out_specs=[VMEM] * len(outs),
            scratch_shapes=list(scratch),
            compiler_params=pltpu.CompilerParams(vmem_limit_bytes=limit * MIB),
            cost_estimate=pl.CostEstimate(flops=flops, bytes_accessed=nbytes, transcendentals=0),
            name=name,
        )(*args)

    return run


def sds(shape, dtype=BF16):
    return jax.ShapeDtypeStruct(shape, dtype)


def group_sum(row):
    lane = lax.broadcasted_iota(jnp.int32, row.shape, 1)
    shift = 1
    while shift < GROUP:
        other = jnp.where((lane & shift) != 0, pltpu.roll(row, shift, 1), pltpu.roll(row, CH - shift, 1))
        row = row + other
        shift *= 2
    return row


def local_stats(flat):
    count = flat.shape[0] * GROUP
    mean = group_sum(jnp.sum(flat, axis=0, keepdims=True)) * (1.0 / count)
    dev = flat - mean
    m2 = group_sum(jnp.sum(dev * dev, axis=0, keepdims=True))
    return mean, m2


def merge(st_ref, count):
    means = st_ref[:, 0, :]
    mean = jnp.sum(means, axis=0, keepdims=True) * (1.0 / st_ref.shape[0])
    apart = means - mean
    m2 = jnp.sum(st_ref[:, 1, :] + count * (apart * apart), axis=0, keepdims=True)
    return mean, lax.rsqrt(m2 * (1.0 / (count * st_ref.shape[0])) + 1e-6)


def store_stats(ref, mean, m2):
    row = lax.broadcasted_iota(jnp.int32, (2, CH), 0)
    ref[...] = jnp.broadcast_to(jnp.where(row == 0, mean, m2)[None], ref.shape)


def spread(slots):
    return lax.all_to_all(slots, HA + ("wa",), 0, 0, tiled=True)


def store_edges(frames, refs):
    top_ref, bot_ref, lef_ref, rig_ref = refs
    at = 0
    for v in frames:
        n = v.shape[0]
        top_ref[at : at + n] = v[:, 0].astype(BF16)
        bot_ref[at : at + n] = v[:, ROWS - 1].astype(BF16)
        for i in range(WIDE):
            for ref, j in ((lef_ref, i), (rig_ref, COLS - WIDE + i)):
                column = jnp.concatenate([v[:, :, j, :], jnp.zeros((n, 8, CH), F32)], axis=1)
                ref[at : at + n, i] = column.astype(BF16)
        at += n


def first_body(flag_ref, x_hbm, c1_hbm, c2_hbm, w_hbm, x_ref, c1_ref, c2_ref, slot_ref, *rest):
    edges, pieces, sem = rest[:4], rest[4:8], rest[8]
    pairs = [(x_hbm, x_ref), (c1_hbm, c1_ref), (c2_hbm, c2_ref)]
    for k, piece in enumerate(pieces):
        block = pl.multiple_of(lax.rem(flag_ref[4] + k, 4) * CH, CH)
        pairs.append((w_hbm.at[:, :, pl.ds(block, CH)], piece))
    copies = [pltpu.make_async_copy(src, dst, sem.at[i]) for i, (src, dst) in enumerate(pairs)]
    for c in copies:
        c.start()
    for c in copies[:3]:
        c.wait()
    x, c1, c2 = x_ref[...].astype(F32), c1_ref[...].astype(F32), c2_ref[...].astype(F32)
    store_stats(slot_ref, *local_stats(x.reshape(-1, CH)))
    store_edges((c1, x, c2), edges)
    for c in copies[3:]:
        c.wait()


def corner_body(top_ref, bot_ref, lef_ref, rig_ref, lo_ref, ro_ref):
    top = top_ref[...].astype(F32)
    bot = bot_ref[...].astype(F32)
    shape = (lef_ref.shape[0],) + lef_ref.shape[2:]
    row = lax.broadcasted_iota(jnp.int32, shape, 1)
    for i in range(WIDE):
        for src, dst, at in ((lef_ref, lo_ref, i), (rig_ref, ro_ref, COLS - WIDE + i)):
            v = src[:, i].astype(F32)
            v = jnp.where(row == 8, top[:, at : at + 1, :], v)
            v = jnp.where(row == 9, bot[:, at : at + 1, :], v)
            dst[:, i] = v.astype(BF16)


def swap_rows(top, bot):
    n = lax.axis_size(HA)
    above = lax.ppermute(bot, HA, [(i, i + 1) for i in range(n - 1)])
    below = lax.ppermute(top, HA, [(i + 1, i) for i in range(n - 1)])
    return above, below


def swap_columns(lef, rig):
    n = lax.axis_size("wa")
    left = lax.ppermute(rig, "wa", [(i, i + 1) for i in range(n - 1)])
    right = lax.ppermute(lef, "wa", [(i + 1, i) for i in range(n - 1)])
    return left, right


def shifted(rows, left, right):
    n = rows.shape[0]
    flat = rows.reshape(n * COLS, CH)
    col = lax.broadcasted_iota(jnp.int32, rows.shape, 1)
    before = pltpu.roll(flat, 1, 0).reshape(rows.shape)
    after = pltpu.roll(flat, n * COLS - 1, 0).reshape(rows.shape)
    before = jnp.where(col == 0, left[:, None, :], before)
    after = jnp.where(col == COLS - 1, right[:, None, :], after)
    return before, after


def place(patch_ref, frame, rows, at, left, right, lanes):
    n = rows.shape[0]
    before, after = shifted(rows, left, right)
    for e, v in enumerate((before, rows, after)):
        patch_ref[frame, at * COLS : (at + n) * COLS, lanes[e] : lanes[e] + CH] = v.reshape(n * COLS, CH).astype(BF16)


def place_frame(patch_ref, frame, inner, top, bot, lef, rig, corners, lanes):
    place(patch_ref, frame, inner, 1, lef, rig, lanes)
    place(patch_ref, frame, top[None], 0, corners[0], corners[1], lanes)
    place(patch_ref, frame, bot[None], ROWS + 1, corners[2], corners[3], lanes)


def multiply(patch_ref, side_ref, w_ref, outs):
    depth = 9 * CH
    size = ROWS * COLS
    slot = side_ref.shape[1] // (ROWS + 2)
    jobs = [(t * size, size, [(patch_ref, t + a, COLS) for a in range(3)]) for t in range(4)]
    jobs.append((4 * size, ROWS * slot, [(side_ref, a, slot) for a in range(3)]))
    for at, rows, sources in jobs:
        acc = None
        for a, (ref, i, step) in enumerate(sources):
            lhs = jnp.concatenate([ref[i, b * step : b * step + rows, :] for b in range(3)], axis=1)
            part = jnp.dot(lhs, w_ref[a * depth : (a + 1) * depth, :], preferred_element_type=F32)
            acc = part if acc is None else acc + part
        for i, out in enumerate(outs):
            out[at : at + rows, :] = acc[:, i * CH : (i + 1) * CH].astype(BF16)


def halo_frame(refs, at, change, has, reach):
    top, bot, lef, rig = refs
    above = jnp.where(has[0], change(top[at].astype(F32)), 0.0)
    below = jnp.where(has[1], change(bot[at].astype(F32)), 0.0)
    columns = {}
    for i in range(reach):
        for ref, flag, j, x in ((lef, has[2], WIDE - 1 - i, -1 - i), (rig, has[3], i, COLS + i)):
            v = jnp.where(flag, change(ref[at, j].astype(F32)), 0.0)
            columns[x] = (v[0:8], jnp.where(has[0], v[8:9], 0.0), jnp.where(has[1], v[9:10], 0.0))
    return above, below, columns


def place_sides(mix_ref, frame, ext, inner, above, below, columns):
    columns = dict(columns)
    for x in (0, COLS - 1):
        columns[x] = (inner[:, x, :], above[x : x + 1], below[x : x + 1])
    step = 8 * ext
    for a in range(3):
        t = frame - a
        if not 0 <= t < 4:
            continue
        for c, x in enumerate(list(range(-ext, 0)) + list(range(COLS, COLS + ext))):
            w = t * 2 * ext + c
            for e in range(3):
                rows, up, down = columns[x + e - 1]
                mix_ref[a, e, pl.ds(w, 1), :] = up
                mix_ref[a, e, pl.ds(step + w, ROWS, stride=step), :] = rows
                mix_ref[a, e, pl.ds((ROWS + 1) * step + w, 1), :] = down


def far_body(ext, cache_at, act_at, extra, flag_ref, x_ref, c_ref, st_ref, *rest):
    halo, rest = rest[:4], rest[4:]
    if act_at is None:
        beside_ref, above_ref, below_ref = rest[:3]
        rest = rest[3:]
    w_hbm, rest = rest[0], rest[1 + extra :]
    out2, out1, patch_ref, side_ref, near_ref, w_ref, mix_ref, wide_ref, sem = rest
    col = flag_ref[4]
    copies = []
    for i, (k, dst, at) in enumerate(((2, w_ref, 0), (1, w_ref, CH), (3, near_ref, 0), (0, near_ref, CH))):
        block = pl.multiple_of(lax.rem(col + k, 4) * CH, CH)
        copies.append(
            pltpu.make_async_copy(w_hbm.at[:, pl.ds(block, CH)], dst.at[:, at : at + CH], sem.at[i])
        )
        copies[-1].start()
    has = [flag_ref[i] > 0 for i in range(4)]
    mean, scale = merge(st_ref, BLOCK)

    def act(v):
        u = (v - mean) * scale
        return u / (1.0 + jnp.exp(-u))

    if act_at is None:
        wide_ref[...] = act(beside_ref[...])
        outer = [
            jnp.where(flag, act(ref[...].astype(F32)), 0.0) for ref, flag in ((above_ref, has[0]), (below_ref, has[1]))
        ]
    for s in range(6):
        if s < 2:
            inner = c_ref[s].astype(F32)
            above, below, columns = halo_frame(halo, cache_at + s, lambda v: v, has, ext + 1)
        else:
            t = s - 2
            inner = act(x_ref[t].astype(F32))
            if act_at is not None:
                above, below, columns = halo_frame(halo, act_at + t, act, has, ext + 1)
            else:
                above, below = [v[t * COLS : (t + 1) * COLS] for v in outer]
                columns = {}
                for c, x in enumerate((-2, -1, COLS, COLS + 1)):
                    flag = has[2 + c // 2]
                    px = 4 * COLS + 4 * t + c
                    rows = wide_ref[pl.ds(4 * t + c, ROWS, stride=16), :]
                    columns[x] = tuple(
                        jnp.where(flag, v, 0.0) for v in (rows, outer[0][px : px + 1], outer[1][px : px + 1])
                    )
        corners = [columns[-1][1], columns[COLS][1], columns[-1][2], columns[COLS][2]]
        place_frame(
            patch_ref, s, inner, above, below, columns[-1][0], columns[COLS][0], corners, (0, CH, 2 * CH)
        )
        place_sides(mix_ref, s, ext, inner, above, below, columns)
    for a in range(3):
        for e in range(3):
            side_ref[a, :, e * CH : (e + 1) * CH] = mix_ref[a, e].astype(BF16)
    copies[0].wait()
    copies[1].wait()
    multiply(patch_ref, side_ref, w_ref, (out2, out1))
    copies[2].wait()
    copies[3].wait()


def near_body(patch_ref, side_ref, w_ref, *rest):
    multiply(patch_ref, side_ref, w_ref, rest[-2:])


def conv(flags, x, cache, stats, halo, cache_at, act_at, around, weight, ext, name, after=()):
    n = x.shape[0] * ROWS * COLS + ROWS * 8 * ext
    depth, width = weight.shape
    flops = n * depth * width
    piece = sds((n, CH))
    body = functools.partial(far_body, ext, cache_at, act_at, 0)
    out2, out1, patch, side, near = call(
        body,
        [piece] * 2
        + [
            sds((6, (ROWS + 2) * COLS, 3 * CH)),
            sds((3, (ROWS + 2) * 8 * ext, 3 * CH)),
            sds((depth, 2 * CH)),
        ],
        scratch=[
            pltpu.VMEM((depth, 2 * CH), BF16),
            pltpu.VMEM((3, 3, (ROWS + 2) * 8 * ext, CH), F32),
            pltpu.VMEM((16 * ROWS, CH), F32),
            pltpu.SemaphoreType.DMA((4,)),
        ],
        flops=flops,
        limit=20,
        name=name + "_far",
    )(flags, x, cache, stats, *halo, *around, Left(weight, HBM))
    got2 = to_peer(out2, 2)
    got1 = to_peer(out1, 1)
    out3, own = call(near_body, [piece] * 2, flops=flops, limit=16, name=name + "_near")(
        patch, side, near, *[Left(a) for a in after]
    )
    (far,) = call(add_body, [sds((n, CH), F32)], name=name + "_add")(got1, got2)
    return own, far, to_peer(out3, 3)


def add_body(a_ref, b_ref, o_ref):
    o_ref[...] = a_ref[...].astype(F32) + b_ref[...].astype(F32)


def gate_body(*refs):
    del refs


def gate(arrays, after):
    n = len(arrays)
    return pl.pallas_call(
        gate_body,
        out_shape=[sds(a.shape) for a in arrays],
        in_specs=[ANY] * (n + 1),
        out_specs=[ANY] * n,
        input_output_aliases={i: i for i in range(n)},
        compiler_params=pltpu.CompilerParams(vmem_limit_bytes=8 * MIB),
        name="gate",
    )(*arrays, after)


def to_peer(piece, k):
    n = lax.axis_size("col")
    return lax.ppermute(piece, "col", [(i, (i + k) % n) for i in range(n)])


def to_peers(pieces):
    got = {k: to_peer(pieces[k - 1], k) for k in (2, 1, 3)}
    return [got[k] for k in (1, 2, 3)]


def hidden_body(p0, far, p3, h_ref, side_ref, slot_ref, top_ref, bot_ref):
    h = (p0[...].astype(F32) + p3[...].astype(F32) + far[...]).astype(BF16).astype(F32)
    size = 4 * ROWS * COLS
    mean, m2 = local_stats(h[:size])
    store_stats(slot_ref, mean, m2)
    main = h[:size].reshape(h_ref.shape)
    h_ref[...] = main.astype(BF16)
    side_ref[...] = h[size:]
    for ref, r in ((top_ref, 0), (bot_ref, ROWS - 1)):
        ref[0 : 4 * COLS, :] = main[:, r].reshape(4 * COLS, CH).astype(BF16)
        ref[4 * COLS :, :] = h[size + 16 * r : size + 16 * (r + 1)].astype(BF16)


def resid_body(flag_ref, x_ref, lef_ref, rig_ref, p0, far, p3, o_ref, top_ref, bot_ref, side_ref):
    total = p0[...].astype(F32) + p3[...].astype(F32) + far[...]
    size = ROWS * COLS
    side_ref[...] = total[4 * size :]
    row = lax.broadcasted_iota(jnp.int32, (8, CH), 0)
    for t in range(4):
        main = x_ref[t].astype(F32).reshape(size, CH) + total[t * size : (t + 1) * size]
        o_ref[t, 0:size, :] = main.astype(BF16)
        beside = []
        for c, (ref, i) in enumerate(((lef_ref, WIDE - 1), (rig_ref, 0))):
            v = ref[2 + t, i].astype(F32)[0:ROWS] + side_ref[pl.ds(2 * t + c, ROWS, stride=8), :]
            beside.append(jnp.where(flag_ref[2 + c] > 0, v, 0.0))
            o_ref[t, size + 8 * c : size + 8 * (c + 1), :] = beside[c].astype(BF16)
        for ref, r in ((top_ref, 0), (bot_ref, ROWS - 1)):
            ref[t, 0:COLS, :] = main[r * COLS : (r + 1) * COLS].astype(BF16)
            px = [v[r : r + 1] for v in beside]
            ref[t, COLS:, :] = jnp.where(row == 0, px[0], jnp.where(row == 1, px[1], 0.0)).astype(BF16)


ROW_TAPS = {(0, 0): (-1, 0), (0, 1): (1,), (1, 0): (-1,), (1, 1): (0, 1)}
COL_TAPS = {(0, 0): (-1,), (0, 1): (0, 1), (1, 0): (-1, 0), (1, 1): (1,)}


def fold_body(w0, w1, w2, w3, *rest):
    o_ref = rest[-1]
    for k, ref in enumerate((w0, w1, w2, w3)):
        taps = [ref[i].astype(F32) for i in range(9)]
        for q in range(2):
            for r in range(2):
                for s in range(2):
                    for p in range(2):
                        total = None
                        for b in ROW_TAPS[p, r]:
                            for e in COL_TAPS[q, s]:
                                tap = taps[(b + 1) * 3 + (e + 1)]
                                total = tap if total is None else total + tap
                        at = (s * 4 + k) * CH
                        o_ref[q, r, at : at + CH, p * CH : (p + 1) * CH] = total.astype(BF16)


def inner_body(*refs):
    o_ref = refs[-1]
    size = ROWS * COLS
    for k, ref in enumerate(refs[:4]):
        for t in range(4):
            v = ref[t].astype(F32)
            rows = v[:size].reshape(ROWS, COLS, CH)
            place(o_ref, t, rows, 0, v[size : size + 8], v[size + 8 :], [(e * 4 + k) * CH for e in range(3)])


def up_body(*refs):
    borders = refs[:4]
    patch_ref, w_ref, o_ref, edge_ref, mix_ref = refs[4:]
    half = 2 * 4 * CH
    for k, border in enumerate(borders):
        edge = border[0].astype(F32)
        for i in range(2):
            v = edge[i * (COLS + 8) : (i + 1) * (COLS + 8)]
            lanes = [(e * 4 + k) * CH for e in range(3)]
            place(edge_ref, i, v[:COLS][None], 0, v[COLS : COLS + 1], v[COLS + 1 : COLS + 2], lanes)
    for q in range(2):
        lanes = pl.ds(q * 4 * CH, half)
        inner = patch_ref[0, :, lanes]
        acc = jnp.dot(jnp.concatenate([edge_ref[0, :, lanes], inner], axis=0), w_ref[q, 0], preferred_element_type=F32)
        acc += jnp.dot(jnp.concatenate([inner, edge_ref[1, :, lanes]], axis=0), w_ref[q, 1], preferred_element_type=F32)
        for n in range(ROWS + 1):
            for p in range(2):
                i = 2 * n - 1 + p
                if 0 <= i < 2 * ROWS:
                    mix_ref[i, pl.ds(q, COLS, stride=2), :] = acc[n * COLS : (n + 1) * COLS, p * CH : (p + 1) * CH]
    o_ref[0] = mix_ref[...].astype(BF16)


def up_conv(inner, borders, weight):
    def by_frame(a):
        return pl.BlockSpec((1,) + a.shape[1:], lambda t: (t, 0, 0))

    frames = inner.shape[0]
    out = (frames, 2 * ROWS, 2 * COLS, CH)
    return pl.pallas_call(
        up_body,
        out_shape=sds(out),
        grid=(frames,),
        in_specs=[by_frame(a) for a in borders]
        + [by_frame(inner), pl.BlockSpec(weight.shape, lambda t: (0, 0, 0, 0))],
        out_specs=pl.BlockSpec((1,) + out[1:], lambda t: (t, 0, 0, 0)),
        scratch_shapes=[
            pltpu.VMEM((2, COLS, 12 * CH), BF16),
            pltpu.VMEM((2 * ROWS, 2 * COLS, CH), F32),
        ],
        compiler_params=pltpu.CompilerParams(vmem_limit_bytes=24 * MIB),
        name="up_conv",
    )(*borders, inner, weight)


def on_device(features, cache_first, cache_second, weight_first, weight_second, weight_up):
    frames = features.shape[0]
    ha, wa, col = lax.axis_index(HA), lax.axis_index("wa"), lax.axis_index("col")
    nh, nw = lax.axis_size(HA), lax.axis_size("wa")
    flags = jnp.stack([ha > 0, ha < nh - 1, wa > 0, wa < nw - 1, col]).astype(jnp.int32)
    slots = sds((nh * nw, 2, CH), F32)

    x, c1, c2, stats, *edges = call(
        first_body,
        [sds(features.shape), sds(cache_first.shape), sds(cache_second.shape), slots]
        + [sds((8, COLS, CH))] * 2
        + [sds((8, WIDE, 16, CH))] * 2
        + [sds(weight_up.shape[:2] + (CH,))] * 4,
        scratch=[pltpu.SemaphoreType.DMA((7,))],
        limit=20,
        name="first",
    )(flags, *[Left(a, HBM) for a in (features, cache_first, cache_second, weight_up)])
    edges, w_pieces = edges[:4], edges[4:]
    stats = spread(stats)
    rows = swap_rows(*edges[:2])
    cornered = call(corner_body, [sds((8, WIDE, 16, CH))] * 2, name="corners")(*rows, *edges[2:])
    halo = rows + swap_columns(*cornered)
    pieces = conv(
        flags, x, c1, stats, halo, 0, 2, (), weight_first.reshape(-1, 4 * CH), 2, "conv_first"
    )
    hidden, side, stats, top, bot = call(
        hidden_body,
        [sds(features.shape), sds((16 * ROWS, CH), F32), slots] + [sds((4 * COLS + 16, CH))] * 2,
        limit=12,
        name="hidden",
    )(*pieces)
    w_got = to_peers(gate(w_pieces[1:], stats))
    stats = spread(stats)
    around = (side,) + swap_rows(top, bot)
    pieces = conv(
        flags, hidden, c2, stats, halo, 6, None, around, weight_second.reshape(-1, 4 * CH), 1, "conv_second", w_got
    )
    resid, top, bot = call(
        resid_body,
        [sds((frames, ROWS * COLS + 16, CH))] + [sds((frames, COLS + 8, CH))] * 2,
        scratch=[pltpu.VMEM((8 * ROWS, CH), F32)],
        name="resid",
    )(flags, features, *halo[2:], *pieces)
    others = to_peers([resid] * 3)
    (border,) = call(pack_body, [sds((frames, 2 * COLS + 16, CH))], name="pack")(
        *swap_rows(top, bot), Left(others[0])
    )
    borders = [border] + to_peers([border] * 3)
    (folded,) = call(fold_body, [sds((2, 2, 8 * CH, 2 * CH))], limit=12, name="fold")(
        w_pieces[0], *w_got, *[Left(a) for a in others[1:]]
    )
    (inner,) = call(inner_body, [sds((frames, ROWS * COLS, 12 * CH))], limit=16, name="inner")(resid, *others)
    return up_conv(inner, borders, folded)


def pack_body(top_ref, bot_ref, after_ref, o_ref):
    o_ref[:, : COLS + 8, :] = top_ref[...]
    o_ref[:, COLS + 8 :, :] = bot_ref[...]


def solution(mesh):
    shape = mesh.devices.shape
    mesh = jax.sharding.Mesh(
        mesh.devices.reshape((shape[0] // 2, 2) + shape[1:]), HA + tuple(mesh.axis_names[1:])
    )
    block = P(None, HA, "wa", "col")
    weight = P(None, "col", None)
    return jax.shard_map(
        on_device,
        mesh=mesh,
        in_specs=(block, block, block, weight, weight, weight),
        out_specs=block,
        check_vma=False,
    )
```

```python
import functools

import jax
import jax.numpy as jnp
from jax import lax
from jax.experimental import pallas as pl
from jax.experimental.pallas import tpu as pltpu
from jax.sharding import PartitionSpec as P

F32 = jnp.float32
BF16 = jnp.bfloat16
CH = 128
GROUP = 16
ROWS = 8
COLS = 32
WIDE = 3
BLOCK = 4 * ROWS * COLS * GROUP
MIB = 1 << 20

VMEM = pl.BlockSpec(memory_space=pltpu.VMEM)
SMEM = pl.BlockSpec(memory_space=pltpu.SMEM)
ANY = pl.BlockSpec(memory_space=pl.ANY)
HBM = pl.BlockSpec(memory_space=pltpu.HBM)
HA = ("z", "core")


class Left:
    def __init__(self, array, spec=ANY):
        self.array, self.spec = array, spec
        if spec is HBM:
            self.array = pltpu.with_memory_space_constraint(array, pltpu.HBM)


def call(body, outs, scratch=(), flops=0, limit=8, name=None):
    def run(*args):
        specs = [a.spec if isinstance(a, Left) else SMEM if a.dtype == jnp.int32 else VMEM for a in args]
        args = [a.array if isinstance(a, Left) else a for a in args]
        nbytes = sum(a.size * a.dtype.itemsize for a in args + list(outs))
        return pl.pallas_call(
            body,
            out_shape=list(outs),
            in_specs=specs,
            out_specs=[VMEM] * len(outs),
            scratch_shapes=list(scratch),
            compiler_params=pltpu.CompilerParams(vmem_limit_bytes=limit * MIB),
            cost_estimate=pl.CostEstimate(flops=flops, bytes_accessed=nbytes, transcendentals=0),
            name=name,
        )(*args)

    return run


def sds(shape, dtype=BF16):
    return jax.ShapeDtypeStruct(shape, dtype)


def group_sum(row):
    lane = lax.broadcasted_iota(jnp.int32, row.shape, 1)
    shift = 1
    while shift < GROUP:
        other = jnp.where((lane & shift) != 0, pltpu.roll(row, shift, 1), pltpu.roll(row, CH - shift, 1))
        row = row + other
        shift *= 2
    return row


def local_stats(flat):
    count = flat.shape[0] * GROUP
    mean = group_sum(jnp.sum(flat, axis=0, keepdims=True)) * (1.0 / count)
    dev = flat - mean
    m2 = group_sum(jnp.sum(dev * dev, axis=0, keepdims=True))
    return mean, m2


def merge(st_ref, count):
    means = st_ref[:, 0, :]
    mean = jnp.sum(means, axis=0, keepdims=True) * (1.0 / st_ref.shape[0])
    apart = means - mean
    m2 = jnp.sum(st_ref[:, 1, :] + count * (apart * apart), axis=0, keepdims=True)
    return mean, lax.rsqrt(m2 * (1.0 / (count * st_ref.shape[0])) + 1e-6)


def store_stats(ref, mean, m2):
    row = lax.broadcasted_iota(jnp.int32, (2, CH), 0)
    ref[...] = jnp.broadcast_to(jnp.where(row == 0, mean, m2)[None], ref.shape)


def spread(slots):
    return lax.all_to_all(slots, HA + ("wa",), 0, 0, tiled=True)


def store_edges(frames, refs):
    top_ref, bot_ref, lef_ref, rig_ref = refs
    at = 0
    for v in frames:
        n = v.shape[0]
        top_ref[at : at + n] = v[:, 0].astype(BF16)
        bot_ref[at : at + n] = v[:, ROWS - 1].astype(BF16)
        for i in range(WIDE):
            for ref, j in ((lef_ref, i), (rig_ref, COLS - WIDE + i)):
                column = jnp.concatenate([v[:, :, j, :], jnp.zeros((n, 8, CH), F32)], axis=1)
                ref[at : at + n, i] = column.astype(BF16)
        at += n


def first_body(flag_ref, x_hbm, c1_hbm, c2_hbm, w_hbm, x_ref, c1_ref, c2_ref, slot_ref, *rest):
    edges, pieces, sem = rest[:4], rest[4:8], rest[8]
    pairs = [(x_hbm, x_ref), (c1_hbm, c1_ref), (c2_hbm, c2_ref)]
    for k, piece in enumerate(pieces):
        block = pl.multiple_of(lax.rem(flag_ref[4] + k, 4) * CH, CH)
        pairs.append((w_hbm.at[:, :, pl.ds(block, CH)], piece))
    copies = [pltpu.make_async_copy(src, dst, sem.at[i]) for i, (src, dst) in enumerate(pairs)]
    for c in copies[:3]:
        c.start()
    for c in copies[:3]:
        c.wait()
    for c in copies[3:]:
        c.start()
    x, c1, c2 = x_ref[...].astype(F32), c1_ref[...].astype(F32), c2_ref[...].astype(F32)
    store_stats(slot_ref, *local_stats(x.reshape(-1, CH)))
    store_edges((c1, x, c2), edges)
    for c in copies[3:]:
        c.wait()


def corner_body(top_ref, bot_ref, lef_ref, rig_ref, lo_ref, ro_ref):
    top = top_ref[...].astype(F32)
    bot = bot_ref[...].astype(F32)
    shape = (lef_ref.shape[0],) + lef_ref.shape[2:]
    row = lax.broadcasted_iota(jnp.int32, shape, 1)
    for i in range(WIDE):
        for src, dst, at in ((lef_ref, lo_ref, i), (rig_ref, ro_ref, COLS - WIDE + i)):
            v = src[:, i].astype(F32)
            v = jnp.where(row == 8, top[:, at : at + 1, :], v)
            v = jnp.where(row == 9, bot[:, at : at + 1, :], v)
            dst[:, i] = v.astype(BF16)


def swap_rows(top, bot):
    n = lax.axis_size(HA)
    above = lax.ppermute(bot, HA, [(i, i + 1) for i in range(n - 1)])
    below = lax.ppermute(top, HA, [(i + 1, i) for i in range(n - 1)])
    return above, below


def swap_columns(lef, rig):
    n = lax.axis_size("wa")
    left = lax.ppermute(rig, "wa", [(i, i + 1) for i in range(n - 1)])
    right = lax.ppermute(lef, "wa", [(i + 1, i) for i in range(n - 1)])
    return left, right


def shifted(rows, left, right):
    n = rows.shape[0]
    flat = rows.reshape(n * COLS, CH)
    col = lax.broadcasted_iota(jnp.int32, rows.shape, 1)
    before = pltpu.roll(flat, 1, 0).reshape(rows.shape)
    after = pltpu.roll(flat, n * COLS - 1, 0).reshape(rows.shape)
    before = jnp.where(col == 0, left[:, None, :], before)
    after = jnp.where(col == COLS - 1, right[:, None, :], after)
    return before, after


def place(patch_ref, frame, rows, at, left, right, lanes):
    n = rows.shape[0]
    before, after = shifted(rows, left, right)
    for e, v in enumerate((before, rows, after)):
        patch_ref[frame, at * COLS : (at + n) * COLS, lanes[e] : lanes[e] + CH] = v.reshape(n * COLS, CH).astype(BF16)


def place_frame(patch_ref, frame, inner, top, bot, lef, rig, corners, lanes):
    place(patch_ref, frame, inner, 1, lef, rig, lanes)
    place(patch_ref, frame, top[None], 0, corners[0], corners[1], lanes)
    place(patch_ref, frame, bot[None], ROWS + 1, corners[2], corners[3], lanes)


def multiply(patch_ref, side_ref, w_ref, outs):
    depth = 9 * CH
    size = ROWS * COLS
    slot = side_ref.shape[1] // (ROWS + 2)
    jobs = [(t * size, size, [(patch_ref, t + a, COLS) for a in range(3)]) for t in range(4)]
    jobs.append((4 * size, ROWS * slot, [(side_ref, a, slot) for a in range(3)]))
    for at, rows, sources in jobs:
        acc = None
        for a, (ref, i, step) in enumerate(sources):
            lhs = jnp.concatenate([ref[i, b * step : b * step + rows, :] for b in range(3)], axis=1)
            part = jnp.dot(lhs, w_ref[a * depth : (a + 1) * depth, :], preferred_element_type=F32)
            acc = part if acc is None else acc + part
        for i, out in enumerate(outs):
            out[at : at + rows, :] = acc[:, i * CH : (i + 1) * CH].astype(BF16)


def halo_frame(refs, at, change, has, reach):
    top, bot, lef, rig = refs
    above = jnp.where(has[0], change(top[at].astype(F32)), 0.0)
    below = jnp.where(has[1], change(bot[at].astype(F32)), 0.0)
    columns = {}
    for i in range(reach):
        for ref, flag, j, x in ((lef, has[2], WIDE - 1 - i, -1 - i), (rig, has[3], i, COLS + i)):
            v = jnp.where(flag, change(ref[at, j].astype(F32)), 0.0)
            columns[x] = (v[0:8], jnp.where(has[0], v[8:9], 0.0), jnp.where(has[1], v[9:10], 0.0))
    return above, below, columns


def place_sides(mix_ref, frame, ext, inner, above, below, columns):
    columns = dict(columns)
    for x in (0, COLS - 1):
        columns[x] = (inner[:, x, :], above[x : x + 1], below[x : x + 1])
    step = 8 * ext
    for a in range(3):
        t = frame - a
        if not 0 <= t < 4:
            continue
        for c, x in enumerate(list(range(-ext, 0)) + list(range(COLS, COLS + ext))):
            w = t * 2 * ext + c
            for e in range(3):
                rows, up, down = columns[x + e - 1]
                mix_ref[a, e, pl.ds(w, 1), :] = up
                mix_ref[a, e, pl.ds(step + w, ROWS, stride=step), :] = rows
                mix_ref[a, e, pl.ds((ROWS + 1) * step + w, 1), :] = down


def far_body(ext, cache_at, act_at, extra, flag_ref, x_ref, c_ref, st_ref, *rest):
    halo, rest = rest[:4], rest[4:]
    if act_at is None:
        beside_ref, above_ref, below_ref = rest[:3]
        rest = rest[3:]
    w_hbm, rest = rest[0], rest[1 + extra :]
    out2, out1, patch_ref, side_ref, near_ref, w_ref, mix_ref, wide_ref, sem = rest
    col = flag_ref[4]
    copies = []
    for i, (k, dst, at) in enumerate(((2, w_ref, 0), (1, w_ref, CH), (3, near_ref, 0), (0, near_ref, CH))):
        block = pl.multiple_of(lax.rem(col + k, 4) * CH, CH)
        copies.append(
            pltpu.make_async_copy(w_hbm.at[:, pl.ds(block, CH)], dst.at[:, at : at + CH], sem.at[i])
        )
    for c in copies[:2]:
        c.start()
    has = [flag_ref[i] > 0 for i in range(4)]
    mean, scale = merge(st_ref, BLOCK)

    def act(v):
        u = (v - mean) * scale
        return u / (1.0 + jnp.exp(-u))

    if act_at is None:
        wide_ref[...] = act(beside_ref[...])
        outer = [
            jnp.where(flag, act(ref[...].astype(F32)), 0.0) for ref, flag in ((above_ref, has[0]), (below_ref, has[1]))
        ]
    for s in range(6):
        if s < 2:
            inner = c_ref[s].astype(F32)
            above, below, columns = halo_frame(halo, cache_at + s, lambda v: v, has, ext + 1)
        else:
            t = s - 2
            inner = act(x_ref[t].astype(F32))
            if act_at is not None:
                above, below, columns = halo_frame(halo, act_at + t, act, has, ext + 1)
            else:
                above, below = [v[t * COLS : (t + 1) * COLS] for v in outer]
                columns = {}
                for c, x in enumerate((-2, -1, COLS, COLS + 1)):
                    flag = has[2 + c // 2]
                    px = 4 * COLS + 4 * t + c
                    rows = wide_ref[pl.ds(4 * t + c, ROWS, stride=16), :]
                    columns[x] = tuple(
                        jnp.where(flag, v, 0.0) for v in (rows, outer[0][px : px + 1], outer[1][px : px + 1])
                    )
        corners = [columns[-1][1], columns[COLS][1], columns[-1][2], columns[COLS][2]]
        place_frame(
            patch_ref, s, inner, above, below, columns[-1][0], columns[COLS][0], corners, (0, CH, 2 * CH)
        )
        place_sides(mix_ref, s, ext, inner, above, below, columns)
    for a in range(3):
        for e in range(3):
            side_ref[a, :, e * CH : (e + 1) * CH] = mix_ref[a, e].astype(BF16)
    copies[0].wait()
    copies[1].wait()
    copies[2].start()
    copies[3].start()
    multiply(patch_ref, side_ref, w_ref, (out2, out1))
    copies[2].wait()
    copies[3].wait()


def near_body(patch_ref, side_ref, w_ref, *rest):
    multiply(patch_ref, side_ref, w_ref, rest[-2:])


def conv(flags, x, cache, stats, halo, cache_at, act_at, around, weight, ext, name, after=()):
    n = x.shape[0] * ROWS * COLS + ROWS * 8 * ext
    depth, width = weight.shape
    flops = n * depth * width
    piece = sds((n, CH))
    body = functools.partial(far_body, ext, cache_at, act_at, 0)
    out2, out1, patch, side, near = call(
        body,
        [piece] * 2
        + [
            sds((6, (ROWS + 2) * COLS, 3 * CH)),
            sds((3, (ROWS + 2) * 8 * ext, 3 * CH)),
            sds((depth, 2 * CH)),
        ],
        scratch=[
            pltpu.VMEM((depth, 2 * CH), BF16),
            pltpu.VMEM((3, 3, (ROWS + 2) * 8 * ext, CH), F32),
            pltpu.VMEM((16 * ROWS, CH), F32),
            pltpu.SemaphoreType.DMA((4,)),
        ],
        flops=flops,
        limit=20,
        name=name + "_far",
    )(flags, x, cache, stats, *halo, *around, Left(weight, HBM))
    got2 = to_peer(out2, 2)
    got1 = to_peer(out1, 1)
    out3, own = call(near_body, [piece] * 2, flops=flops, limit=16, name=name + "_near")(
        patch, side, near, *[Left(a) for a in after]
    )
    (far,) = call(add_body, [sds((n, CH), F32)], name=name + "_add")(got1, got2)
    return own, far, to_peer(out3, 3)


def add_body(a_ref, b_ref, o_ref):
    o_ref[...] = a_ref[...].astype(F32) + b_ref[...].astype(F32)


def gate_body(*refs):
    del refs


def gate(arrays, after):
    n = len(arrays)
    return pl.pallas_call(
        gate_body,
        out_shape=[sds(a.shape) for a in arrays],
        in_specs=[ANY] * (n + 1),
        out_specs=[ANY] * n,
        input_output_aliases={i: i for i in range(n)},
        compiler_params=pltpu.CompilerParams(vmem_limit_bytes=8 * MIB),
        name="gate",
    )(*arrays, after)


def to_peer(piece, k):
    n = lax.axis_size("col")
    return lax.ppermute(piece, "col", [(i, (i + k) % n) for i in range(n)])


def to_peers(pieces):
    got = {k: to_peer(pieces[k - 1], k) for k in (2, 1, 3)}
    return [got[k] for k in (1, 2, 3)]


def hidden_body(p0, far, p3, h_ref, side_ref, slot_ref, top_ref, bot_ref):
    h = (p0[...].astype(F32) + p3[...].astype(F32) + far[...]).astype(BF16).astype(F32)
    size = 4 * ROWS * COLS
    mean, m2 = local_stats(h[:size])
    store_stats(slot_ref, mean, m2)
    main = h[:size].reshape(h_ref.shape)
    h_ref[...] = main.astype(BF16)
    side_ref[...] = h[size:]
    for ref, r in ((top_ref, 0), (bot_ref, ROWS - 1)):
        ref[0 : 4 * COLS, :] = main[:, r].reshape(4 * COLS, CH).astype(BF16)
        ref[4 * COLS :, :] = h[size + 16 * r : size + 16 * (r + 1)].astype(BF16)


def resid_body(flag_ref, x_ref, lef_ref, rig_ref, p0, far, p3, o_ref, top_ref, bot_ref, side_ref):
    total = p0[...].astype(F32) + p3[...].astype(F32) + far[...]
    size = ROWS * COLS
    side_ref[...] = total[4 * size :]
    row = lax.broadcasted_iota(jnp.int32, (8, CH), 0)
    for t in range(4):
        main = x_ref[t].astype(F32).reshape(size, CH) + total[t * size : (t + 1) * size]
        o_ref[t, 0:size, :] = main.astype(BF16)
        beside = []
        for c, (ref, i) in enumerate(((lef_ref, WIDE - 1), (rig_ref, 0))):
            v = ref[2 + t, i].astype(F32)[0:ROWS] + side_ref[pl.ds(2 * t + c, ROWS, stride=8), :]
            beside.append(jnp.where(flag_ref[2 + c] > 0, v, 0.0))
            o_ref[t, size + 8 * c : size + 8 * (c + 1), :] = beside[c].astype(BF16)
        for ref, r in ((top_ref, 0), (bot_ref, ROWS - 1)):
            ref[t, 0:COLS, :] = main[r * COLS : (r + 1) * COLS].astype(BF16)
            px = [v[r : r + 1] for v in beside]
            ref[t, COLS:, :] = jnp.where(row == 0, px[0], jnp.where(row == 1, px[1], 0.0)).astype(BF16)


ROW_TAPS = {(0, 0): (-1, 0), (0, 1): (1,), (1, 0): (-1,), (1, 1): (0, 1)}
COL_TAPS = {(0, 0): (-1,), (0, 1): (0, 1), (1, 0): (-1, 0), (1, 1): (1,)}


def fold_body(w0, w1, w2, w3, *rest):
    o_ref = rest[-1]
    for k, ref in enumerate((w0, w1, w2, w3)):
        taps = [ref[i].astype(F32) for i in range(9)]
        for q in range(2):
            for r in range(2):
                for s in range(2):
                    for p in range(2):
                        total = None
                        for b in ROW_TAPS[p, r]:
                            for e in COL_TAPS[q, s]:
                                tap = taps[(b + 1) * 3 + (e + 1)]
                                total = tap if total is None else total + tap
                        at = (s * 4 + k) * CH
                        o_ref[q, r, at : at + CH, p * CH : (p + 1) * CH] = total.astype(BF16)


def inner_body(*refs):
    o_ref = refs[-1]
    size = ROWS * COLS
    for k, ref in enumerate(refs[:4]):
        for t in range(4):
            v = ref[t].astype(F32)
            rows = v[:size].reshape(ROWS, COLS, CH)
            place(o_ref, t, rows, 0, v[size : size + 8], v[size + 8 :], [(e * 4 + k) * CH for e in range(3)])


def up_body(*refs):
    borders = refs[:4]
    patch_ref, w_ref, o_ref, edge_ref, mix_ref = refs[4:]
    half = 2 * 4 * CH
    for k, border in enumerate(borders):
        edge = border[0].astype(F32)
        for i in range(2):
            v = edge[i * (COLS + 8) : (i + 1) * (COLS + 8)]
            lanes = [(e * 4 + k) * CH for e in range(3)]
            place(edge_ref, i, v[:COLS][None], 0, v[COLS : COLS + 1], v[COLS + 1 : COLS + 2], lanes)
    for q in range(2):
        lanes = pl.ds(q * 4 * CH, half)
        inner = patch_ref[0, :, lanes]
        acc = jnp.dot(jnp.concatenate([edge_ref[0, :, lanes], inner], axis=0), w_ref[q, 0], preferred_element_type=F32)
        acc += jnp.dot(jnp.concatenate([inner, edge_ref[1, :, lanes]], axis=0), w_ref[q, 1], preferred_element_type=F32)
        for n in range(ROWS + 1):
            for p in range(2):
                i = 2 * n - 1 + p
                if 0 <= i < 2 * ROWS:
                    mix_ref[i, pl.ds(q, COLS, stride=2), :] = acc[n * COLS : (n + 1) * COLS, p * CH : (p + 1) * CH]
    o_ref[0] = mix_ref[...].astype(BF16)


def up_conv(inner, borders, weight):
    def by_frame(a):
        return pl.BlockSpec((1,) + a.shape[1:], lambda t: (t, 0, 0))

    frames = inner.shape[0]
    out = (frames, 2 * ROWS, 2 * COLS, CH)
    return pl.pallas_call(
        up_body,
        out_shape=sds(out),
        grid=(frames,),
        in_specs=[by_frame(a) for a in borders]
        + [by_frame(inner), pl.BlockSpec(weight.shape, lambda t: (0, 0, 0, 0))],
        out_specs=pl.BlockSpec((1,) + out[1:], lambda t: (t, 0, 0, 0)),
        scratch_shapes=[
            pltpu.VMEM((2, COLS, 12 * CH), BF16),
            pltpu.VMEM((2 * ROWS, 2 * COLS, CH), F32),
        ],
        compiler_params=pltpu.CompilerParams(vmem_limit_bytes=24 * MIB),
        name="up_conv",
    )(*borders, inner, weight)


def on_device(features, cache_first, cache_second, weight_first, weight_second, weight_up):
    frames = features.shape[0]
    ha, wa, col = lax.axis_index(HA), lax.axis_index("wa"), lax.axis_index("col")
    nh, nw = lax.axis_size(HA), lax.axis_size("wa")
    flags = jnp.stack([ha > 0, ha < nh - 1, wa > 0, wa < nw - 1, col]).astype(jnp.int32)
    slots = sds((nh * nw, 2, CH), F32)

    x, c1, c2, stats, *edges = call(
        first_body,
        [sds(features.shape), sds(cache_first.shape), sds(cache_second.shape), slots]
        + [sds((8, COLS, CH))] * 2
        + [sds((8, WIDE, 16, CH))] * 2
        + [sds(weight_up.shape[:2] + (CH,))] * 4,
        scratch=[pltpu.SemaphoreType.DMA((7,))],
        limit=20,
        name="first",
    )(flags, *[Left(a, HBM) for a in (features, cache_first, cache_second, weight_up)])
    edges, w_pieces = edges[:4], edges[4:]
    stats = spread(stats)
    rows = swap_rows(*edges[:2])
    cornered = call(corner_body, [sds((8, WIDE, 16, CH))] * 2, name="corners")(*rows, *edges[2:])
    halo = rows + swap_columns(*cornered)
    pieces = conv(
        flags, x, c1, stats, halo, 0, 2, (), weight_first.reshape(-1, 4 * CH), 2, "conv_first"
    )
    hidden, side, stats, top, bot = call(
        hidden_body,
        [sds(features.shape), sds((16 * ROWS, CH), F32), slots] + [sds((4 * COLS + 16, CH))] * 2,
        limit=12,
        name="hidden",
    )(*pieces)
    w_got = to_peers(gate(w_pieces[1:], stats))
    stats = spread(stats)
    around = (side,) + swap_rows(top, bot)
    pieces = conv(
        flags, hidden, c2, stats, halo, 6, None, around, weight_second.reshape(-1, 4 * CH), 1, "conv_second", w_got
    )
    resid, top, bot = call(
        resid_body,
        [sds((frames, ROWS * COLS + 16, CH))] + [sds((frames, COLS + 8, CH))] * 2,
        scratch=[pltpu.VMEM((8 * ROWS, CH), F32)],
        name="resid",
    )(flags, features, *halo[2:], *pieces)
    others = to_peers([resid] * 3)
    (border,) = call(pack_body, [sds((frames, 2 * COLS + 16, CH))], name="pack")(
        *swap_rows(top, bot), Left(others[0])
    )
    borders = [border] + to_peers([border] * 3)
    (folded,) = call(fold_body, [sds((2, 2, 8 * CH, 2 * CH))], limit=12, name="fold")(
        w_pieces[0], *w_got, *[Left(a) for a in others[1:]]
    )
    (inner,) = call(inner_body, [sds((frames, ROWS * COLS, 12 * CH))], limit=16, name="inner")(resid, *others)
    return up_conv(inner, borders, folded)


def pack_body(top_ref, bot_ref, after_ref, o_ref):
    o_ref[:, : COLS + 8, :] = top_ref[...]
    o_ref[:, COLS + 8 :, :] = bot_ref[...]


def solution(mesh):
    shape = mesh.devices.shape
    mesh = jax.sharding.Mesh(
        mesh.devices.reshape((shape[0] // 2, 2) + shape[1:]), HA + tuple(mesh.axis_names[1:])
    )
    block = P(None, HA, "wa", "col")
    weight = P(None, "col", None)
    return jax.shard_map(
        on_device,
        mesh=mesh,
        in_specs=(block, block, block, weight, weight, weight),
        out_specs=block,
        check_vma=False,
    )
```

```python
import functools

import jax
import jax.numpy as jnp
from jax import lax
from jax.experimental import pallas as pl
from jax.experimental.pallas import tpu as pltpu
from jax.sharding import PartitionSpec as P

F32 = jnp.float32
BF16 = jnp.bfloat16
CH = 128
GROUP = 16
ROWS = 8
COLS = 32
WIDE = 3
BLOCK = 4 * ROWS * COLS * GROUP
MIB = 1 << 20

VMEM = pl.BlockSpec(memory_space=pltpu.VMEM)
SMEM = pl.BlockSpec(memory_space=pltpu.SMEM)
ANY = pl.BlockSpec(memory_space=pl.ANY)
HBM = pl.BlockSpec(memory_space=pltpu.HBM)
HA = ("z", "core")


class Left:
    def __init__(self, array, spec=ANY):
        self.array, self.spec = array, spec
        if spec is HBM:
            self.array = pltpu.with_memory_space_constraint(array, pltpu.HBM)


def call(body, outs, scratch=(), flops=0, limit=8, name=None):
    def run(*args):
        specs = [a.spec if isinstance(a, Left) else SMEM if a.dtype == jnp.int32 else VMEM for a in args]
        args = [a.array if isinstance(a, Left) else a for a in args]
        nbytes = sum(a.size * a.dtype.itemsize for a in args + list(outs))
        return pl.pallas_call(
            body,
            out_shape=list(outs),
            in_specs=specs,
            out_specs=[VMEM] * len(outs),
            scratch_shapes=list(scratch),
            compiler_params=pltpu.CompilerParams(vmem_limit_bytes=limit * MIB),
            cost_estimate=pl.CostEstimate(flops=flops, bytes_accessed=nbytes, transcendentals=0),
            name=name,
        )(*args)

    return run


def sds(shape, dtype=BF16):
    return jax.ShapeDtypeStruct(shape, dtype)


def group_sum(row):
    lane = lax.broadcasted_iota(jnp.int32, row.shape, 1)
    shift = 1
    while shift < GROUP:
        other = jnp.where((lane & shift) != 0, pltpu.roll(row, shift, 1), pltpu.roll(row, CH - shift, 1))
        row = row + other
        shift *= 2
    return row


def local_stats(flat):
    count = flat.shape[0] * GROUP
    mean = group_sum(jnp.sum(flat, axis=0, keepdims=True)) * (1.0 / count)
    dev = flat - mean
    m2 = group_sum(jnp.sum(dev * dev, axis=0, keepdims=True))
    return mean, m2


def merge(st_ref, count):
    means = st_ref[:, 0, :]
    mean = jnp.sum(means, axis=0, keepdims=True) * (1.0 / st_ref.shape[0])
    apart = means - mean
    m2 = jnp.sum(st_ref[:, 1, :] + count * (apart * apart), axis=0, keepdims=True)
    return mean, lax.rsqrt(m2 * (1.0 / (count * st_ref.shape[0])) + 1e-6)


def store_stats(ref, mean, m2):
    row = lax.broadcasted_iota(jnp.int32, (2, CH), 0)
    ref[...] = jnp.broadcast_to(jnp.where(row == 0, mean, m2)[None], ref.shape)


def spread(slots):
    return lax.all_to_all(slots, HA + ("wa",), 0, 0, tiled=True)


def store_edges(frames, refs):
    top_ref, bot_ref, lef_ref, rig_ref = refs
    at = 0
    for v in frames:
        n = v.shape[0]
        top_ref[at : at + n] = v[:, 0].astype(BF16)
        bot_ref[at : at + n] = v[:, ROWS - 1].astype(BF16)
        for i in range(WIDE):
            for ref, j in ((lef_ref, i), (rig_ref, COLS - WIDE + i)):
                column = jnp.concatenate([v[:, :, j, :], jnp.zeros((n, 8, CH), F32)], axis=1)
                ref[at : at + n, i] = column.astype(BF16)
        at += n


def first_body(flag_ref, x_hbm, c1_hbm, c2_hbm, w_hbm, x_ref, c1_ref, c2_ref, slot_ref, *rest):
    edges, pieces, sem = rest[:4], rest[4:8], rest[8]
    pairs = [(x_hbm, x_ref), (c1_hbm, c1_ref), (c2_hbm, c2_ref)]
    for k, piece in enumerate(pieces):
        block = pl.multiple_of(lax.rem(flag_ref[4] + k, 4) * CH, CH)
        pairs.append((w_hbm.at[:, :, pl.ds(block, CH)], piece))
    copies = [pltpu.make_async_copy(src, dst, sem.at[i]) for i, (src, dst) in enumerate(pairs)]
    for c in copies:
        c.start()
    for c in copies[:3]:
        c.wait()
    x, c1, c2 = x_ref[...].astype(F32), c1_ref[...].astype(F32), c2_ref[...].astype(F32)
    store_stats(slot_ref, *local_stats(x.reshape(-1, CH)))
    store_edges((c1, x, c2), edges)
    for c in copies[3:]:
        c.wait()


def corner_body(top_ref, bot_ref, lef_ref, rig_ref, lo_ref, ro_ref):
    top = top_ref[...].astype(F32)
    bot = bot_ref[...].astype(F32)
    shape = (lef_ref.shape[0],) + lef_ref.shape[2:]
    row = lax.broadcasted_iota(jnp.int32, shape, 1)
    for i in range(WIDE):
        for src, dst, at in ((lef_ref, lo_ref, i), (rig_ref, ro_ref, COLS - WIDE + i)):
            v = src[:, i].astype(F32)
            v = jnp.where(row == 8, top[:, at : at + 1, :], v)
            v = jnp.where(row == 9, bot[:, at : at + 1, :], v)
            dst[:, i] = v.astype(BF16)


def swap_rows(top, bot):
    n = lax.axis_size(HA)
    above = lax.ppermute(bot, HA, [(i, i + 1) for i in range(n - 1)])
    below = lax.ppermute(top, HA, [(i + 1, i) for i in range(n - 1)])
    return above, below


def swap_columns(lef, rig):
    n = lax.axis_size("wa")
    left = lax.ppermute(rig, "wa", [(i, i + 1) for i in range(n - 1)])
    right = lax.ppermute(lef, "wa", [(i + 1, i) for i in range(n - 1)])
    return left, right


def shifted(rows, left, right):
    n = rows.shape[0]
    flat = rows.reshape(n * COLS, CH)
    col = lax.broadcasted_iota(jnp.int32, rows.shape, 1)
    before = pltpu.roll(flat, 1, 0).reshape(rows.shape)
    after = pltpu.roll(flat, n * COLS - 1, 0).reshape(rows.shape)
    before = jnp.where(col == 0, left[:, None, :], before)
    after = jnp.where(col == COLS - 1, right[:, None, :], after)
    return before, after


def place(patch_ref, frame, rows, at, left, right, lanes):
    n = rows.shape[0]
    before, after = shifted(rows, left, right)
    for e, v in enumerate((before, rows, after)):
        patch_ref[frame, at * COLS : (at + n) * COLS, lanes[e] : lanes[e] + CH] = v.reshape(n * COLS, CH).astype(BF16)


def place_frame(patch_ref, frame, inner, top, bot, lef, rig, corners, lanes):
    place(patch_ref, frame, inner, 1, lef, rig, lanes)
    place(patch_ref, frame, top[None], 0, corners[0], corners[1], lanes)
    place(patch_ref, frame, bot[None], ROWS + 1, corners[2], corners[3], lanes)


def multiply(patch_ref, side_ref, w_ref, outs):
    depth = 9 * CH
    size = ROWS * COLS
    slot = side_ref.shape[1] // (ROWS + 2)
    jobs = [(t * size, size, [(patch_ref, t + a, COLS) for a in range(3)]) for t in range(4)]
    jobs.append((4 * size, ROWS * slot, [(side_ref, a, slot) for a in range(3)]))
    for at, rows, sources in jobs:
        acc = None
        for a, (ref, i, step) in enumerate(sources):
            lhs = jnp.concatenate([ref[i, b * step : b * step + rows, :] for b in range(3)], axis=1)
            part = jnp.dot(lhs, w_ref[a * depth : (a + 1) * depth, :], preferred_element_type=F32)
            acc = part if acc is None else acc + part
        for i, out in enumerate(outs):
            out[at : at + rows, :] = acc[:, i * CH : (i + 1) * CH].astype(BF16)


def halo_frame(refs, at, change, has, reach):
    top, bot, lef, rig = refs
    above = jnp.where(has[0], change(top[at].astype(F32)), 0.0)
    below = jnp.where(has[1], change(bot[at].astype(F32)), 0.0)
    columns = {}
    for i in range(reach):
        for ref, flag, j, x in ((lef, has[2], WIDE - 1 - i, -1 - i), (rig, has[3], i, COLS + i)):
            v = jnp.where(flag, change(ref[at, j].astype(F32)), 0.0)
            columns[x] = (v[0:8], jnp.where(has[0], v[8:9], 0.0), jnp.where(has[1], v[9:10], 0.0))
    return above, below, columns


def place_sides(mix_ref, frame, ext, inner, above, below, columns):
    columns = dict(columns)
    for x in (0, COLS - 1):
        columns[x] = (inner[:, x, :], above[x : x + 1], below[x : x + 1])
    step = 8 * ext
    for a in range(3):
        t = frame - a
        if not 0 <= t < 4:
            continue
        for c, x in enumerate(list(range(-ext, 0)) + list(range(COLS, COLS + ext))):
            w = t * 2 * ext + c
            for e in range(3):
                rows, up, down = columns[x + e - 1]
                mix_ref[a, e, pl.ds(w, 1), :] = up
                mix_ref[a, e, pl.ds(step + w, ROWS, stride=step), :] = rows
                mix_ref[a, e, pl.ds((ROWS + 1) * step + w, 1), :] = down


def far_body(ext, cache_at, act_at, extra, flag_ref, x_ref, c_ref, st_ref, *rest):
    halo, rest = rest[:4], rest[4:]
    if act_at is None:
        beside_ref, above_ref, below_ref = rest[:3]
        rest = rest[3:]
    w_hbm, rest = rest[0], rest[1 + extra :]
    out2, out1, patch_ref, side_ref, near_ref, w_ref, mix_ref, wide_ref, sem = rest
    col = flag_ref[4]
    copies = []
    for i, (k, dst, at) in enumerate(((2, w_ref, 0), (1, w_ref, CH), (3, near_ref, 0), (0, near_ref, CH))):
        block = pl.multiple_of(lax.rem(col + k, 4) * CH, CH)
        copies.append(
            pltpu.make_async_copy(w_hbm.at[:, pl.ds(block, CH)], dst.at[:, at : at + CH], sem.at[i])
        )
        copies[-1].start()
    has = [flag_ref[i] > 0 for i in range(4)]
    mean, scale = merge(st_ref, BLOCK)

    def act(v):
        u = (v - mean) * scale
        return u / (1.0 + jnp.exp(-u))

    if act_at is None:
        wide_ref[...] = act(beside_ref[...])
        outer = [
            jnp.where(flag, act(ref[...].astype(F32)), 0.0) for ref, flag in ((above_ref, has[0]), (below_ref, has[1]))
        ]
    for s in range(6):
        if s < 2:
            inner = c_ref[s].astype(F32)
            above, below, columns = halo_frame(halo, cache_at + s, lambda v: v, has, ext + 1)
        else:
            t = s - 2
            inner = act(x_ref[t].astype(F32))
            if act_at is not None:
                above, below, columns = halo_frame(halo, act_at + t, act, has, ext + 1)
            else:
                above, below = [v[t * COLS : (t + 1) * COLS] for v in outer]
                columns = {}
                for c, x in enumerate((-2, -1, COLS, COLS + 1)):
                    flag = has[2 + c // 2]
                    px = 4 * COLS + 4 * t + c
                    rows = wide_ref[pl.ds(4 * t + c, ROWS, stride=16), :]
                    columns[x] = tuple(
                        jnp.where(flag, v, 0.0) for v in (rows, outer[0][px : px + 1], outer[1][px : px + 1])
                    )
        corners = [columns[-1][1], columns[COLS][1], columns[-1][2], columns[COLS][2]]
        place_frame(
            patch_ref, s, inner, above, below, columns[-1][0], columns[COLS][0], corners, (0, CH, 2 * CH)
        )
        place_sides(mix_ref, s, ext, inner, above, below, columns)
    for a in range(3):
        for e in range(3):
            side_ref[a, :, e * CH : (e + 1) * CH] = mix_ref[a, e].astype(BF16)
    copies[0].wait()
    copies[1].wait()
    multiply(patch_ref, side_ref, w_ref, (out2, out1))
    copies[2].wait()
    copies[3].wait()


def near_body(patch_ref, side_ref, w_ref, *rest):
    multiply(patch_ref, side_ref, w_ref, rest[-2:])


def conv(flags, x, cache, stats, halo, cache_at, act_at, around, weight, ext, name, after=()):
    n = x.shape[0] * ROWS * COLS + ROWS * 8 * ext
    depth, width = weight.shape
    flops = n * depth * width
    piece = sds((n, CH))
    body = functools.partial(far_body, ext, cache_at, act_at, 0)
    out2, out1, patch, side, near = call(
        body,
        [piece] * 2
        + [
            sds((6, (ROWS + 2) * COLS, 3 * CH)),
            sds((3, (ROWS + 2) * 8 * ext, 3 * CH)),
            sds((depth, 2 * CH)),
        ],
        scratch=[
            pltpu.VMEM((depth, 2 * CH), BF16),
            pltpu.VMEM((3, 3, (ROWS + 2) * 8 * ext, CH), F32),
            pltpu.VMEM((16 * ROWS, CH), F32),
            pltpu.SemaphoreType.DMA((4,)),
        ],
        flops=flops,
        limit=20,
        name=name + "_far",
    )(flags, x, cache, stats, *halo, *around, Left(weight, HBM))
    got2 = to_peer(out2, 2)
    got1 = to_peer(out1, 1)
    out3, own = call(near_body, [piece] * 2, flops=flops, limit=16, name=name + "_near")(
        patch, side, near, *[Left(a) for a in after]
    )
    (far,) = call(add_body, [sds((n, CH), F32)], name=name + "_add")(got2, got1)
    return own, far, to_peer(out3, 3)


def add_body(a_ref, b_ref, o_ref):
    o_ref[...] = a_ref[...].astype(F32) + b_ref[...].astype(F32)


def gate_body(*refs):
    del refs


def gate(arrays, after):
    n = len(arrays)
    return pl.pallas_call(
        gate_body,
        out_shape=[sds(a.shape) for a in arrays],
        in_specs=[ANY] * (n + 1),
        out_specs=[ANY] * n,
        input_output_aliases={i: i for i in range(n)},
        compiler_params=pltpu.CompilerParams(vmem_limit_bytes=8 * MIB),
        name="gate",
    )(*arrays, after)


def to_peer(piece, k):
    n = lax.axis_size("col")
    return lax.ppermute(piece, "col", [(i, (i + k) % n) for i in range(n)])


def to_peers(pieces):
    got = {k: to_peer(pieces[k - 1], k) for k in (2, 1, 3)}
    return [got[k] for k in (1, 2, 3)]


def hidden_body(p0, far, p3, h_ref, side_ref, slot_ref, top_ref, bot_ref):
    h = (p0[...].astype(F32) + p3[...].astype(F32) + far[...]).astype(BF16).astype(F32)
    size = 4 * ROWS * COLS
    mean, m2 = local_stats(h[:size])
    store_stats(slot_ref, mean, m2)
    main = h[:size].reshape(h_ref.shape)
    h_ref[...] = main.astype(BF16)
    side_ref[...] = h[size:]
    for ref, r in ((top_ref, 0), (bot_ref, ROWS - 1)):
        ref[0 : 4 * COLS, :] = main[:, r].reshape(4 * COLS, CH).astype(BF16)
        ref[4 * COLS :, :] = h[size + 16 * r : size + 16 * (r + 1)].astype(BF16)


def resid_body(flag_ref, x_ref, lef_ref, rig_ref, p0, far, p3, o_ref, top_ref, bot_ref, side_ref):
    total = p0[...].astype(F32) + p3[...].astype(F32) + far[...]
    size = ROWS * COLS
    side_ref[...] = total[4 * size :]
    row = lax.broadcasted_iota(jnp.int32, (8, CH), 0)
    for t in range(4):
        main = x_ref[t].astype(F32).reshape(size, CH) + total[t * size : (t + 1) * size]
        o_ref[t, 0:size, :] = main.astype(BF16)
        beside = []
        for c, (ref, i) in enumerate(((lef_ref, WIDE - 1), (rig_ref, 0))):
            v = ref[2 + t, i].astype(F32)[0:ROWS] + side_ref[pl.ds(2 * t + c, ROWS, stride=8), :]
            beside.append(jnp.where(flag_ref[2 + c] > 0, v, 0.0))
            o_ref[t, size + 8 * c : size + 8 * (c + 1), :] = beside[c].astype(BF16)
        for ref, r in ((top_ref, 0), (bot_ref, ROWS - 1)):
            ref[t, 0:COLS, :] = main[r * COLS : (r + 1) * COLS].astype(BF16)
            px = [v[r : r + 1] for v in beside]
            ref[t, COLS:, :] = jnp.where(row == 0, px[0], jnp.where(row == 1, px[1], 0.0)).astype(BF16)


ROW_TAPS = {(0, 0): (-1, 0), (0, 1): (1,), (1, 0): (-1,), (1, 1): (0, 1)}
COL_TAPS = {(0, 0): (-1,), (0, 1): (0, 1), (1, 0): (-1, 0), (1, 1): (1,)}


def fold_body(w0, w1, w2, w3, *rest):
    o_ref = rest[-1]
    for k, ref in enumerate((w0, w1, w2, w3)):
        taps = [ref[i].astype(F32) for i in range(9)]
        for q in range(2):
            for r in range(2):
                for s in range(2):
                    for p in range(2):
                        total = None
                        for b in ROW_TAPS[p, r]:
                            for e in COL_TAPS[q, s]:
                                tap = taps[(b + 1) * 3 + (e + 1)]
                                total = tap if total is None else total + tap
                        at = (s * 4 + k) * CH
                        o_ref[q, r, at : at + CH, p * CH : (p + 1) * CH] = total.astype(BF16)


def inner_body(*refs):
    o_ref = refs[-1]
    size = ROWS * COLS
    for k, ref in enumerate(refs[:4]):
        for t in range(4):
            v = ref[t].astype(F32)
            rows = v[:size].reshape(ROWS, COLS, CH)
            place(o_ref, t, rows, 0, v[size : size + 8], v[size + 8 :], [(e * 4 + k) * CH for e in range(3)])


def up_body(*refs):
    borders = refs[:4]
    patch_ref, w_ref, o_ref, edge_ref, mix_ref = refs[4:]
    half = 2 * 4 * CH
    for k, border in enumerate(borders):
        edge = border[0].astype(F32)
        for i in range(2):
            v = edge[i * (COLS + 8) : (i + 1) * (COLS + 8)]
            lanes = [(e * 4 + k) * CH for e in range(3)]
            place(edge_ref, i, v[:COLS][None], 0, v[COLS : COLS + 1], v[COLS + 1 : COLS + 2], lanes)
    for q in range(2):
        lanes = pl.ds(q * 4 * CH, half)
        inner = patch_ref[0, :, lanes]
        acc = jnp.dot(jnp.concatenate([edge_ref[0, :, lanes], inner], axis=0), w_ref[q, 0], preferred_element_type=F32)
        acc += jnp.dot(jnp.concatenate([inner, edge_ref[1, :, lanes]], axis=0), w_ref[q, 1], preferred_element_type=F32)
        for n in range(ROWS + 1):
            for p in range(2):
                i = 2 * n - 1 + p
                if 0 <= i < 2 * ROWS:
                    mix_ref[i, pl.ds(q, COLS, stride=2), :] = acc[n * COLS : (n + 1) * COLS, p * CH : (p + 1) * CH]
    o_ref[0] = mix_ref[...].astype(BF16)


def up_conv(inner, borders, weight):
    def by_frame(a):
        return pl.BlockSpec((1,) + a.shape[1:], lambda t: (t, 0, 0))

    frames = inner.shape[0]
    out = (frames, 2 * ROWS, 2 * COLS, CH)
    return pl.pallas_call(
        up_body,
        out_shape=sds(out),
        grid=(frames,),
        in_specs=[by_frame(a) for a in borders]
        + [by_frame(inner), pl.BlockSpec(weight.shape, lambda t: (0, 0, 0, 0))],
        out_specs=pl.BlockSpec((1,) + out[1:], lambda t: (t, 0, 0, 0)),
        scratch_shapes=[
            pltpu.VMEM((2, COLS, 12 * CH), BF16),
            pltpu.VMEM((2 * ROWS, 2 * COLS, CH), F32),
        ],
        compiler_params=pltpu.CompilerParams(vmem_limit_bytes=24 * MIB),
        name="up_conv",
    )(*borders, inner, weight)


def on_device(features, cache_first, cache_second, weight_first, weight_second, weight_up):
    frames = features.shape[0]
    ha, wa, col = lax.axis_index(HA), lax.axis_index("wa"), lax.axis_index("col")
    nh, nw = lax.axis_size(HA), lax.axis_size("wa")
    flags = jnp.stack([ha > 0, ha < nh - 1, wa > 0, wa < nw - 1, col]).astype(jnp.int32)
    slots = sds((nh * nw, 2, CH), F32)

    x, c1, c2, stats, *edges = call(
        first_body,
        [sds(features.shape), sds(cache_first.shape), sds(cache_second.shape), slots]
        + [sds((8, COLS, CH))] * 2
        + [sds((8, WIDE, 16, CH))] * 2
        + [sds(weight_up.shape[:2] + (CH,))] * 4,
        scratch=[pltpu.SemaphoreType.DMA((7,))],
        limit=20,
        name="first",
    )(flags, *[Left(a, HBM) for a in (features, cache_first, cache_second, weight_up)])
    edges, w_pieces = edges[:4], edges[4:]
    stats = spread(stats)
    rows = swap_rows(*edges[:2])
    cornered = call(corner_body, [sds((8, WIDE, 16, CH))] * 2, name="corners")(*rows, *edges[2:])
    halo = rows + swap_columns(*cornered)
    pieces = conv(
        flags, x, c1, stats, halo, 0, 2, (), weight_first.reshape(-1, 4 * CH), 2, "conv_first"
    )
    hidden, side, stats, top, bot = call(
        hidden_body,
        [sds(features.shape), sds((16 * ROWS, CH), F32), slots] + [sds((4 * COLS + 16, CH))] * 2,
        limit=12,
        name="hidden",
    )(*pieces)
    w_got = to_peers(gate(w_pieces[1:], stats))
    stats = spread(stats)
    around = (side,) + swap_rows(top, bot)
    pieces = conv(
        flags, hidden, c2, stats, halo, 6, None, around, weight_second.reshape(-1, 4 * CH), 1, "conv_second", w_got
    )
    resid, top, bot = call(
        resid_body,
        [sds((frames, ROWS * COLS + 16, CH))] + [sds((frames, COLS + 8, CH))] * 2,
        scratch=[pltpu.VMEM((8 * ROWS, CH), F32)],
        name="resid",
    )(flags, features, *halo[2:], *pieces)
    others = to_peers([resid] * 3)
    (border,) = call(pack_body, [sds((frames, 2 * COLS + 16, CH))], name="pack")(
        *swap_rows(top, bot), Left(others[0])
    )
    borders = [border] + to_peers([border] * 3)
    (folded,) = call(fold_body, [sds((2, 2, 8 * CH, 2 * CH))], limit=12, name="fold")(
        w_pieces[0], *w_got, *[Left(a) for a in others[1:]]
    )
    (inner,) = call(inner_body, [sds((frames, ROWS * COLS, 12 * CH))], limit=16, name="inner")(resid, *others)
    return up_conv(inner, borders, folded)


def pack_body(top_ref, bot_ref, after_ref, o_ref):
    o_ref[:, : COLS + 8, :] = top_ref[...]
    o_ref[:, COLS + 8 :, :] = bot_ref[...]


def solution(mesh):
    shape = mesh.devices.shape
    mesh = jax.sharding.Mesh(
        mesh.devices.reshape((shape[0] // 2, 2) + shape[1:]), HA + tuple(mesh.axis_names[1:])
    )
    block = P(None, HA, "wa", "col")
    weight = P(None, "col", None)
    return jax.shard_map(
        on_device,
        mesh=mesh,
        in_specs=(block, block, block, weight, weight, weight),
        out_specs=block,
        check_vma=False,
    )
```

```python
import functools

import jax
import jax.numpy as jnp
from jax import lax
from jax.experimental import pallas as pl
from jax.experimental.pallas import tpu as pltpu
from jax.sharding import PartitionSpec as P

F32 = jnp.float32
BF16 = jnp.bfloat16
CH = 128
GROUP = 16
ROWS = 8
COLS = 32
WIDE = 3
BLOCK = 4 * ROWS * COLS * GROUP
MIB = 1 << 20

VMEM = pl.BlockSpec(memory_space=pltpu.VMEM)
SMEM = pl.BlockSpec(memory_space=pltpu.SMEM)
ANY = pl.BlockSpec(memory_space=pl.ANY)
HBM = pl.BlockSpec(memory_space=pltpu.HBM)
HA = ("z", "core")


class Left:
    def __init__(self, array, spec=ANY):
        self.array, self.spec = array, spec
        if spec is HBM:
            self.array = pltpu.with_memory_space_constraint(array, pltpu.HBM)


def call(body, outs, scratch=(), flops=0, limit=8, name=None):
    def run(*args):
        specs = [a.spec if isinstance(a, Left) else SMEM if a.dtype == jnp.int32 else VMEM for a in args]
        args = [a.array if isinstance(a, Left) else a for a in args]
        nbytes = sum(a.size * a.dtype.itemsize for a in args + list(outs))
        return pl.pallas_call(
            body,
            out_shape=list(outs),
            in_specs=specs,
            out_specs=[VMEM] * len(outs),
            scratch_shapes=list(scratch),
            compiler_params=pltpu.CompilerParams(vmem_limit_bytes=limit * MIB),
            cost_estimate=pl.CostEstimate(flops=flops, bytes_accessed=nbytes, transcendentals=0),
            name=name,
        )(*args)

    return run


def sds(shape, dtype=BF16):
    return jax.ShapeDtypeStruct(shape, dtype)


def group_sum(row):
    lane = lax.broadcasted_iota(jnp.int32, row.shape, 1)
    shift = 1
    while shift < GROUP:
        other = jnp.where((lane & shift) != 0, pltpu.roll(row, shift, 1), pltpu.roll(row, CH - shift, 1))
        row = row + other
        shift *= 2
    return row


def local_stats(flat):
    count = flat.shape[0] * GROUP
    mean = group_sum(jnp.sum(flat, axis=0, keepdims=True)) * (1.0 / count)
    dev = flat - mean
    m2 = group_sum(jnp.sum(dev * dev, axis=0, keepdims=True))
    return mean, m2


def merge(st_ref, count):
    means = st_ref[:, 0, :]
    mean = jnp.sum(means, axis=0, keepdims=True) * (1.0 / st_ref.shape[0])
    apart = means - mean
    m2 = jnp.sum(st_ref[:, 1, :] + count * (apart * apart), axis=0, keepdims=True)
    return mean, lax.rsqrt(m2 * (1.0 / (count * st_ref.shape[0])) + 1e-6)


def store_stats(ref, mean, m2):
    row = lax.broadcasted_iota(jnp.int32, (2, CH), 0)
    ref[...] = jnp.broadcast_to(jnp.where(row == 0, mean, m2)[None], ref.shape)


def spread(slots):
    return lax.all_to_all(slots, HA + ("wa",), 0, 0, tiled=True)


def store_edges(frames, refs):
    top_ref, bot_ref, lef_ref, rig_ref = refs
    at = 0
    for v in frames:
        n = v.shape[0]
        top_ref[at : at + n] = v[:, 0].astype(BF16)
        bot_ref[at : at + n] = v[:, ROWS - 1].astype(BF16)
        for i in range(WIDE):
            for ref, j in ((lef_ref, i), (rig_ref, COLS - WIDE + i)):
                column = jnp.concatenate([v[:, :, j, :], jnp.zeros((n, 8, CH), F32)], axis=1)
                ref[at : at + n, i] = column.astype(BF16)
        at += n


def first_body(flag_ref, x_hbm, c1_hbm, c2_hbm, w_hbm, x_ref, c1_ref, c2_ref, slot_ref, *rest):
    edges, pieces, sem = rest[:4], rest[4:8], rest[8]
    pairs = [(x_hbm, x_ref), (c1_hbm, c1_ref), (c2_hbm, c2_ref)]
    for k, piece in enumerate(pieces):
        block = pl.multiple_of(lax.rem(flag_ref[4] + k, 4) * CH, CH)
        pairs.append((w_hbm.at[:, :, pl.ds(block, CH)], piece))
    copies = [pltpu.make_async_copy(src, dst, sem.at[i]) for i, (src, dst) in enumerate(pairs)]
    for c in copies:
        c.start()
    for c in copies[:3]:
        c.wait()
    x, c1, c2 = x_ref[...].astype(F32), c1_ref[...].astype(F32), c2_ref[...].astype(F32)
    store_stats(slot_ref, *local_stats(x.reshape(-1, CH)))
    store_edges((c1, x, c2), edges)
    for c in copies[3:]:
        c.wait()


def corner_body(top_ref, bot_ref, lef_ref, rig_ref, lo_ref, ro_ref):
    top = top_ref[...].astype(F32)
    bot = bot_ref[...].astype(F32)
    shape = (lef_ref.shape[0],) + lef_ref.shape[2:]
    row = lax.broadcasted_iota(jnp.int32, shape, 1)
    for i in range(WIDE):
        for src, dst, at in ((lef_ref, lo_ref, i), (rig_ref, ro_ref, COLS - WIDE + i)):
            v = src[:, i].astype(F32)
            v = jnp.where(row == 8, top[:, at : at + 1, :], v)
            v = jnp.where(row == 9, bot[:, at : at + 1, :], v)
            dst[:, i] = v.astype(BF16)


def swap_rows(top, bot):
    n = lax.axis_size(HA)
    above = lax.ppermute(bot, HA, [(i, i + 1) for i in range(n - 1)])
    below = lax.ppermute(top, HA, [(i + 1, i) for i in range(n - 1)])
    return above, below


def swap_columns(lef, rig):
    n = lax.axis_size("wa")
    left = lax.ppermute(rig, "wa", [(i, i + 1) for i in range(n - 1)])
    right = lax.ppermute(lef, "wa", [(i + 1, i) for i in range(n - 1)])
    return left, right


def shifted(rows, left, right):
    n = rows.shape[0]
    flat = rows.reshape(n * COLS, CH)
    col = lax.broadcasted_iota(jnp.int32, rows.shape, 1)
    before = pltpu.roll(flat, 1, 0).reshape(rows.shape)
    after = pltpu.roll(flat, n * COLS - 1, 0).reshape(rows.shape)
    before = jnp.where(col == 0, left[:, None, :], before)
    after = jnp.where(col == COLS - 1, right[:, None, :], after)
    return before, after


def place(patch_ref, frame, rows, at, left, right, lanes):
    n = rows.shape[0]
    before, after = shifted(rows, left, right)
    for e, v in enumerate((before, rows, after)):
        patch_ref[frame, at * COLS : (at + n) * COLS, lanes[e] : lanes[e] + CH] = v.reshape(n * COLS, CH).astype(BF16)


def place_frame(patch_ref, frame, inner, top, bot, lef, rig, corners, lanes):
    place(patch_ref, frame, inner, 1, lef, rig, lanes)
    place(patch_ref, frame, top[None], 0, corners[0], corners[1], lanes)
    place(patch_ref, frame, bot[None], ROWS + 1, corners[2], corners[3], lanes)


def multiply(patch_ref, side_ref, w_ref, outs):
    depth = 9 * CH
    size = ROWS * COLS
    slot = side_ref.shape[1] // (ROWS + 2)
    jobs = [(t * size, size, [(patch_ref, t + a, COLS) for a in range(3)]) for t in range(4)]
    jobs.append((4 * size, ROWS * slot, [(side_ref, a, slot) for a in range(3)]))
    for at, rows, sources in jobs:
        acc = None
        for a, (ref, i, step) in enumerate(sources):
            lhs = jnp.concatenate([ref[i, b * step : b * step + rows, :] for b in range(3)], axis=1)
            part = jnp.dot(lhs, w_ref[a * depth : (a + 1) * depth, :], preferred_element_type=F32)
            acc = part if acc is None else acc + part
        for i, out in enumerate(outs):
            out[at : at + rows, :] = acc[:, i * CH : (i + 1) * CH].astype(BF16)


def halo_frame(refs, at, change, has, reach):
    top, bot, lef, rig = refs
    above = jnp.where(has[0], change(top[at].astype(F32)), 0.0)
    below = jnp.where(has[1], change(bot[at].astype(F32)), 0.0)
    columns = {}
    for i in range(reach):
        for ref, flag, j, x in ((lef, has[2], WIDE - 1 - i, -1 - i), (rig, has[3], i, COLS + i)):
            v = jnp.where(flag, change(ref[at, j].astype(F32)), 0.0)
            columns[x] = (v[0:8], jnp.where(has[0], v[8:9], 0.0), jnp.where(has[1], v[9:10], 0.0))
    return above, below, columns


def place_sides(mix_ref, frame, ext, inner, above, below, columns):
    columns = dict(columns)
    for x in (0, COLS - 1):
        columns[x] = (inner[:, x, :], above[x : x + 1], below[x : x + 1])
    step = 8 * ext
    for a in range(3):
        t = frame - a
        if not 0 <= t < 4:
            continue
        for c, x in enumerate(list(range(-ext, 0)) + list(range(COLS, COLS + ext))):
            w = t * 2 * ext + c
            for e in range(3):
                rows, up, down = columns[x + e - 1]
                mix_ref[a, e, pl.ds(w, 1), :] = up
                mix_ref[a, e, pl.ds(step + w, ROWS, stride=step), :] = rows
                mix_ref[a, e, pl.ds((ROWS + 1) * step + w, 1), :] = down


def far_body(ext, cache_at, act_at, extra, flag_ref, x_ref, c_ref, st_ref, *rest):
    halo, rest = rest[:4], rest[4:]
    if act_at is None:
        beside_ref, above_ref, below_ref = rest[:3]
        rest = rest[3:]
    w_hbm, rest = rest[0], rest[1 + extra :]
    out2, out1, patch_ref, side_ref, near_ref, w_ref, mix_ref, wide_ref, sem = rest
    col = flag_ref[4]
    copies = []
    for i, (k, dst, at) in enumerate(((2, w_ref, 0), (1, w_ref, CH), (3, near_ref, 0), (0, near_ref, CH))):
        block = pl.multiple_of(lax.rem(col + k, 4) * CH, CH)
        copies.append(
            pltpu.make_async_copy(w_hbm.at[:, pl.ds(block, CH)], dst.at[:, at : at + CH], sem.at[i])
        )
        copies[-1].start()
    has = [flag_ref[i] > 0 for i in range(4)]
    mean, scale = merge(st_ref, BLOCK)

    def act(v):
        u = (v - mean) * scale
        return u / (1.0 + jnp.exp(-u))

    if act_at is None:
        wide_ref[...] = act(beside_ref[...])
        outer = [
            jnp.where(flag, act(ref[...].astype(F32)), 0.0) for ref, flag in ((above_ref, has[0]), (below_ref, has[1]))
        ]
    for s in range(6):
        if s < 2:
            inner = c_ref[s].astype(F32)
            above, below, columns = halo_frame(halo, cache_at + s, lambda v: v, has, ext + 1)
        else:
            t = s - 2
            inner = act(x_ref[t].astype(F32))
            if act_at is not None:
                above, below, columns = halo_frame(halo, act_at + t, act, has, ext + 1)
            else:
                above, below = [v[t * COLS : (t + 1) * COLS] for v in outer]
                columns = {}
                for c, x in enumerate((-2, -1, COLS, COLS + 1)):
                    flag = has[2 + c // 2]
                    px = 4 * COLS + 4 * t + c
                    rows = wide_ref[pl.ds(4 * t + c, ROWS, stride=16), :]
                    columns[x] = tuple(
                        jnp.where(flag, v, 0.0) for v in (rows, outer[0][px : px + 1], outer[1][px : px + 1])
                    )
        corners = [columns[-1][1], columns[COLS][1], columns[-1][2], columns[COLS][2]]
        place_frame(
            patch_ref, s, inner, above, below, columns[-1][0], columns[COLS][0], corners, (0, CH, 2 * CH)
        )
        place_sides(mix_ref, s, ext, inner, above, below, columns)
    for a in range(3):
        for e in range(3):
            side_ref[a, :, e * CH : (e + 1) * CH] = mix_ref[a, e].astype(BF16)
    copies[0].wait()
    copies[1].wait()
    multiply(patch_ref, side_ref, w_ref, (out2, out1))
    copies[2].wait()
    copies[3].wait()


def near_body(patch_ref, side_ref, w_ref, *rest):
    multiply(patch_ref, side_ref, w_ref, rest[-2:])


def conv(flags, x, cache, stats, halo, cache_at, act_at, around, weight, ext, name, after=()):
    n = x.shape[0] * ROWS * COLS + ROWS * 8 * ext
    depth, width = weight.shape
    flops = n * depth * width
    piece = sds((n, CH))
    body = functools.partial(far_body, ext, cache_at, act_at, 0)
    out2, out1, patch, side, near = call(
        body,
        [piece] * 2
        + [
            sds((6, (ROWS + 2) * COLS, 3 * CH)),
            sds((3, (ROWS + 2) * 8 * ext, 3 * CH)),
            sds((depth, 2 * CH)),
        ],
        scratch=[
            pltpu.VMEM((depth, 2 * CH), BF16),
            pltpu.VMEM((3, 3, (ROWS + 2) * 8 * ext, CH), F32),
            pltpu.VMEM((16 * ROWS, CH), F32),
            pltpu.SemaphoreType.DMA((4,)),
        ],
        flops=flops,
        limit=20,
        name=name + "_far",
    )(flags, x, cache, stats, *halo, *around, Left(weight, HBM))
    got2 = to_peer(out2, 2)
    got1 = to_peer(out1, 1)
    out3, own = call(near_body, [piece] * 2, flops=flops, limit=16, name=name + "_near")(
        patch, side, near, *[Left(a) for a in after]
    )
    (far,) = call(add_body, [sds((n, CH), F32)], name=name + "_add")(got2, got1)
    return own, far, to_peer(out3, 3)


def add_body(a_ref, b_ref, o_ref):
    o_ref[...] = a_ref[...].astype(F32) + b_ref[...].astype(F32)


def gate_body(*refs):
    del refs


def gate(arrays, after):
    n = len(arrays)
    return pl.pallas_call(
        gate_body,
        out_shape=[sds(a.shape) for a in arrays],
        in_specs=[ANY] * (n + 1),
        out_specs=[ANY] * n,
        input_output_aliases={i: i for i in range(n)},
        compiler_params=pltpu.CompilerParams(vmem_limit_bytes=8 * MIB),
        name="gate",
    )(*arrays, after)


def to_peer(piece, k):
    n = lax.axis_size("col")
    return lax.ppermute(piece, "col", [(i, (i + k) % n) for i in range(n)])


def to_peers(pieces):
    got = {k: to_peer(pieces[k - 1], k) for k in (2, 1, 3)}
    return [got[k] for k in (1, 2, 3)]


def hidden_body(p0, far, p3, h_ref, side_ref, slot_ref, top_ref, bot_ref):
    h = (p0[...].astype(F32) + p3[...].astype(F32) + far[...]).astype(BF16).astype(F32)
    size = 4 * ROWS * COLS
    mean, m2 = local_stats(h[:size])
    store_stats(slot_ref, mean, m2)
    main = h[:size].reshape(h_ref.shape)
    h_ref[...] = main.astype(BF16)
    side_ref[...] = h[size:]
    for ref, r in ((top_ref, 0), (bot_ref, ROWS - 1)):
        ref[0 : 4 * COLS, :] = main[:, r].reshape(4 * COLS, CH).astype(BF16)
        ref[4 * COLS :, :] = h[size + 16 * r : size + 16 * (r + 1)].astype(BF16)


def resid_body(flag_ref, x_ref, lef_ref, rig_ref, p0, far, p3, o_ref, top_ref, bot_ref, side_ref):
    total = p0[...].astype(F32) + p3[...].astype(F32) + far[...]
    size = ROWS * COLS
    side_ref[...] = total[4 * size :]
    row = lax.broadcasted_iota(jnp.int32, (8, CH), 0)
    for t in range(4):
        main = x_ref[t].astype(F32).reshape(size, CH) + total[t * size : (t + 1) * size]
        o_ref[t, 0:size, :] = main.astype(BF16)
        beside = []
        for c, (ref, i) in enumerate(((lef_ref, WIDE - 1), (rig_ref, 0))):
            v = ref[2 + t, i].astype(F32)[0:ROWS] + side_ref[pl.ds(2 * t + c, ROWS, stride=8), :]
            beside.append(jnp.where(flag_ref[2 + c] > 0, v, 0.0))
            o_ref[t, size + 8 * c : size + 8 * (c + 1), :] = beside[c].astype(BF16)
        for ref, r in ((top_ref, 0), (bot_ref, ROWS - 1)):
            ref[t, 0:COLS, :] = main[r * COLS : (r + 1) * COLS].astype(BF16)
            px = [v[r : r + 1] for v in beside]
            ref[t, COLS:, :] = jnp.where(row == 0, px[0], jnp.where(row == 1, px[1], 0.0)).astype(BF16)


ROW_TAPS = {(0, 0): (-1, 0), (0, 1): (1,), (1, 0): (-1,), (1, 1): (0, 1)}
COL_TAPS = {(0, 0): (-1,), (0, 1): (0, 1), (1, 0): (-1, 0), (1, 1): (1,)}


def fold_body(w0, w1, w2, w3, *rest):
    o_ref = rest[-1]
    for k, ref in enumerate((w0, w1, w2, w3)):
        taps = [ref[i].astype(F32) for i in range(9)]
        for q in range(2):
            for r in range(2):
                for s in range(2):
                    for p in range(2):
                        total = None
                        for b in ROW_TAPS[p, r]:
                            for e in COL_TAPS[q, s]:
                                tap = taps[(b + 1) * 3 + (e + 1)]
                                total = tap if total is None else total + tap
                        at = (s * 4 + k) * CH
                        o_ref[q, r, at : at + CH, p * CH : (p + 1) * CH] = total.astype(BF16)


def inner_body(*refs):
    o_ref = refs[-1]
    size = ROWS * COLS
    for k, ref in enumerate(refs[:4]):
        for t in range(4):
            v = ref[t].astype(F32)
            rows = v[:size].reshape(ROWS, COLS, CH)
            place(o_ref, t, rows, 0, v[size : size + 8], v[size + 8 :], [(e * 4 + k) * CH for e in range(3)])


def up_body(*refs):
    borders = refs[:4]
    patch_ref, w_ref, o_ref, edge_ref, mix_ref = refs[4:]
    half = 2 * 4 * CH
    for k, border in enumerate(borders):
        edge = border[0].astype(F32)
        for i in range(2):
            v = edge[i * (COLS + 8) : (i + 1) * (COLS + 8)]
            lanes = [(e * 4 + k) * CH for e in range(3)]
            place(edge_ref, i, v[:COLS][None], 0, v[COLS : COLS + 1], v[COLS + 1 : COLS + 2], lanes)
    for q in range(2):
        lanes = pl.ds(q * 4 * CH, half)
        inner = patch_ref[0, :, lanes]
        acc = jnp.dot(jnp.concatenate([edge_ref[0, :, lanes], inner], axis=0), w_ref[q, 0], preferred_element_type=F32)
        acc += jnp.dot(jnp.concatenate([inner, edge_ref[1, :, lanes]], axis=0), w_ref[q, 1], preferred_element_type=F32)
        for n in range(ROWS + 1):
            for p in range(2):
                i = 2 * n - 1 + p
                if 0 <= i < 2 * ROWS:
                    mix_ref[i, pl.ds(q, COLS, stride=2), :] = acc[n * COLS : (n + 1) * COLS, p * CH : (p + 1) * CH]
    o_ref[0] = mix_ref[...].astype(BF16)


def up_conv(inner, borders, weight):
    def by_frame(a):
        return pl.BlockSpec((1,) + a.shape[1:], lambda t: (t, 0, 0))

    frames = inner.shape[0]
    out = (frames, 2 * ROWS, 2 * COLS, CH)
    return pl.pallas_call(
        up_body,
        out_shape=sds(out),
        grid=(frames,),
        in_specs=[by_frame(a) for a in borders]
        + [by_frame(inner), pl.BlockSpec(weight.shape, lambda t: (0, 0, 0, 0))],
        out_specs=pl.BlockSpec((1,) + out[1:], lambda t: (t, 0, 0, 0)),
        scratch_shapes=[
            pltpu.VMEM((2, COLS, 12 * CH), BF16),
            pltpu.VMEM((2 * ROWS, 2 * COLS, CH), F32),
        ],
        compiler_params=pltpu.CompilerParams(vmem_limit_bytes=24 * MIB),
        name="up_conv",
    )(*borders, inner, weight)


def on_device(features, cache_first, cache_second, weight_first, weight_second, weight_up):
    frames = features.shape[0]
    ha, wa, col = lax.axis_index(HA), lax.axis_index("wa"), lax.axis_index("col")
    nh, nw = lax.axis_size(HA), lax.axis_size("wa")
    flags = jnp.stack([ha > 0, ha < nh - 1, wa > 0, wa < nw - 1, col]).astype(jnp.int32)
    slots = sds((nh * nw, 2, CH), F32)

    x, c1, c2, stats, *edges = call(
        first_body,
        [sds(features.shape), sds(cache_first.shape), sds(cache_second.shape), slots]
        + [sds((8, COLS, CH))] * 2
        + [sds((8, WIDE, 16, CH))] * 2
        + [sds(weight_up.shape[:2] + (CH,))] * 4,
        scratch=[pltpu.SemaphoreType.DMA((7,))],
        limit=20,
        name="first",
    )(flags, *[Left(a, HBM) for a in (features, cache_first, cache_second, weight_up)])
    edges, w_pieces = edges[:4], edges[4:]
    stats = spread(stats)
    rows = swap_rows(*edges[:2])
    cornered = call(corner_body, [sds((8, WIDE, 16, CH))] * 2, name="corners")(*rows, *edges[2:])
    halo = rows + swap_columns(*cornered)
    pieces = conv(
        flags, x, c1, stats, halo, 0, 2, (), weight_first.reshape(-1, 4 * CH), 2, "conv_first"
    )
    hidden, side, stats, top, bot = call(
        hidden_body,
        [sds(features.shape), sds((16 * ROWS, CH), F32), slots] + [sds((4 * COLS + 16, CH))] * 2,
        limit=12,
        name="hidden",
    )(*pieces)
    w_got = to_peers(gate(w_pieces[1:], stats))
    stats = spread(stats)
    around = (side,) + swap_rows(top, bot)
    pieces = conv(
        flags, hidden, c2, stats, halo, 6, None, around, weight_second.reshape(-1, 4 * CH), 1, "conv_second", w_got
    )
    resid, top, bot = call(
        resid_body,
        [sds((frames, ROWS * COLS + 16, CH))] + [sds((frames, COLS + 8, CH))] * 2,
        scratch=[pltpu.VMEM((8 * ROWS, CH), F32)],
        name="resid",
    )(flags, features, *halo[2:], *pieces)
    others = to_peers([resid] * 3)
    (border,) = call(pack_body, [sds((frames, 2 * COLS + 16, CH))], name="pack")(
        *swap_rows(top, bot), Left(others[1])
    )
    borders = [border] + to_peers([border] * 3)
    (folded,) = call(fold_body, [sds((2, 2, 8 * CH, 2 * CH))], limit=12, name="fold")(
        w_pieces[0], *w_got, *[Left(a) for a in others[1:]]
    )
    (inner,) = call(inner_body, [sds((frames, ROWS * COLS, 12 * CH))], limit=16, name="inner")(resid, *others)
    return up_conv(inner, borders, folded)


def pack_body(top_ref, bot_ref, after_ref, o_ref):
    o_ref[:, : COLS + 8, :] = top_ref[...]
    o_ref[:, COLS + 8 :, :] = bot_ref[...]


def solution(mesh):
    shape = mesh.devices.shape
    mesh = jax.sharding.Mesh(
        mesh.devices.reshape((shape[0] // 2, 2) + shape[1:]), HA + tuple(mesh.axis_names[1:])
    )
    block = P(None, HA, "wa", "col")
    weight = P(None, "col", None)
    return jax.shard_map(
        on_device,
        mesh=mesh,
        in_specs=(block, block, block, weight, weight, weight),
        out_specs=block,
        check_vma=False,
    )
```
